32 devices in a mesh: blk: 4 (over z), grp: 8 (over y, x, core).
Axes of the slice: x: 2, y: 2, z: 4, core: 2. Of those that a mesh axis runs over, the one named last changes fastest.
Arguments:
- basis: bfloat16 [8, 512, 1152], P('grp', 'blk'), may hold values from -6 to 6
- coeffs: bfloat16 [2, 1152, 768], replicated, may hold values from -0.1875 to 0.1875
- stiff_blocks: bfloat16 [8, 4, 4, 128, 128], P('grp', 'blk'), as said below
- mass_blocks: bfloat16 [8, 4, 4, 128, 128], P('grp', 'blk'), as said below
- block_cols: int32 [8, 4, 4], P('grp', 'blk'), may hold values from 0 to 3
Outputs:
- basis_out: bfloat16 [8, 512, 1152], P('grp', 'blk')
- ritz_value: float32 [384], replicated
- gram: float32 [1152, 2, 1152], P('grp', None, 'blk')
The draws below stay inside these ranges and needn't reach their ends.
Inputs may be any that keep to these rules, and one draw needn't show every extreme that they name: block_cols names row blocks of the same substructure. `mass_blocks`: real-valued blocks of order 1 / sqrt(512). `stiff_blocks`: real-valued blocks, of larger size than the mass blocks.
All inputs are finite; a program needn't handle non-finite values.
Results may differ from the reference program's by a relative error of at most 0.02.
Values may be sent and summed in bfloat16 or wider, within the bound.
No kernel may reach another device: no remote copies, remote signals or barrier semaphores. Data moves between devices by JAX's collectives and lax.ppermute only.
A program may use at most 64 MiB of HBM per device.

```python
import math
import jax
import jax.numpy as jnp
from jax import lax

MODES = 384
BLOCK = 128
NB = 4
ITERS = 2
BASIS = 1152
SUBS = 8
SUBBLOCKS = 4
SUBROWS = 512
ROWS = 4096


def shared_parts(key):
    shape = (SUBS, SUBBLOCKS, NB, BLOCK, BLOCK)
    spread = (3.0 / (NB * BLOCK)) ** 0.5
    mass = jax.random.uniform(jax.random.fold_in(key, 101), shape, jnp.float32, -spread, spread)
    noise = jax.random.uniform(jax.random.fold_in(key, 102), shape, jnp.float32, -spread, spread)
    total = SUBS * SUBBLOCKS
    place = jnp.arange(total, dtype=jnp.float32).reshape(SUBS, SUBBLOCKS) / max(total - 1, 1)
    reach = math.log(5.0)
    rough = jnp.exp(jax.random.uniform(jax.random.fold_in(key, 103), (SUBS, SUBBLOCKS), jnp.float32) * reach)
    scale = (1.0 + 2.0 * place) * rough
    return (mass, noise, scale)


def draw_stiff_blocks(key, part):
    mass, noise, scale = shared_parts(key)
    stiff = scale[:, :, None, None, None] * mass + noise
    return stiff.astype(jnp.bfloat16)


def draw_mass_blocks(key, part):
    mass, noise, scale = shared_parts(key)
    return mass.astype(jnp.bfloat16)


def place_ends(result, own_key, low, top_value):
    spot = [jax.random.randint(jax.random.fold_in(own_key, axis), (), 0, length) for axis, length in enumerate(result.shape)]
    widest = result.shape.index(max(result.shape))
    neighbour = spot[:widest] + [(spot[widest] + 1) % result.shape[widest]] + spot[widest + 1:]
    return result.at[tuple(spot)].set(low).at[tuple(neighbour)].set(top_value)


def levels(own_key, shape, pieces, low, top_value):
    def one(dim, shards_of):
        heights = jax.random.uniform(jax.random.fold_in(jax.random.fold_in(own_key, 6), dim), (shards_of,), jnp.float32, low / len(pieces), top_value / len(pieces))
        return jnp.repeat(jnp.exp(heights), shape[dim] // shards_of).reshape((-1,) + (1,) * (len(shape) - dim - 1))

    gain = one(*pieces[0])
    for cut in pieces[1:]:
        gain = gain * one(*cut)
    return gain


def scatter_about(stream_key, extent, width, bound, cuts=(), held_as=jnp.bfloat16):
    gain = levels(stream_key, extent, cuts, -0.22, 0.18) if cuts else 1.0
    array = jax.random.normal(stream_key, extent, jnp.float32) * width * gain
    return jnp.minimum(jnp.maximum(array, -bound), bound).astype(held_as)


def setup_inputs(seed: int = 0) -> dict:
    key_of = jax.random.split(jax.random.key(seed), 6)
    basis = scatter_about(key_of[0], (SUBS, SUBROWS, BASIS), 1.0, 6.0, ((0, 8), (1, 4)))
    coeffs = scatter_about(key_of[1], (ITERS, BASIS, 2 * MODES), BASIS ** -0.5, 0.1875)
    stiff_blocks = draw_stiff_blocks(jax.random.fold_in(key_of[5], 71), 0)
    mass_blocks = draw_mass_blocks(jax.random.fold_in(key_of[5], 71), 0)
    block_cols = place_ends(jax.random.randint(key_of[4], (SUBS, SUBBLOCKS, NB), 0, SUBBLOCKS), jax.random.fold_in(key_of[4], 1), 0, SUBBLOCKS - 1).astype(jnp.int32)
    return {"basis": basis, "coeffs": coeffs, "stiff_blocks": stiff_blocks, "mass_blocks": mass_blocks, "block_cols": block_cols}


epsilon = 1e-06

def apply_operators(stiff_blocks, mass_blocks, block_cols, field):
    columns = field.shape[-1]

    def one_structure(inputs):
        stiff_sub, mass_sub, cols_sub, field_sub = inputs
        tile_rows = field_sub.reshape(SUBBLOCKS, BLOCK, columns)
        picked = tile_rows[cols_sub].astype(jnp.float32)
        stiff_out = jnp.einsum('snij,snjw->siw', stiff_sub.astype(jnp.float32), picked, precision=lax.Precision.HIGHEST)
        mass_out = jnp.einsum('snij,snjw->siw', mass_sub.astype(jnp.float32), picked, precision=lax.Precision.HIGHEST)
        return (stiff_out.reshape(SUBROWS, columns), mass_out.reshape(SUBROWS, columns))
    return lax.map(one_structure, (stiff_blocks, mass_blocks, block_cols, field))

def reference(basis, coeffs, stiff_blocks, mass_blocks, block_cols):
    current = basis.reshape(ROWS, BASIS)
    ritz_value = jnp.zeros((MODES,), jnp.float32)
    for sweep in range(ITERS):
        turned = jnp.dot(current, coeffs[sweep], preferred_element_type=jnp.float32).astype(jnp.bfloat16)
        next_modes = turned[:, :MODES]
        next_history = turned[:, MODES:]
        stiff_x, mass_x = apply_operators(stiff_blocks, mass_blocks, block_cols, next_modes.reshape(SUBS, SUBROWS, MODES))
        stiff_x = stiff_x.reshape(ROWS, MODES)
        mass_x = mass_x.reshape(ROWS, MODES)
        numerator = lax.optimization_barrier(jnp.sum(stiff_x * mass_x, axis=0))
        denominator = lax.optimization_barrier(jnp.sum(mass_x * mass_x, axis=0))
        ritz_value = numerator / (denominator + epsilon)
        residual = stiff_x - ritz_value * mass_x
        resid_norm = lax.optimization_barrier(jnp.sum(residual * residual, axis=0)) / ROWS
        next_search = (residual * lax.rsqrt(resid_norm + epsilon)).astype(jnp.bfloat16)
        current = jnp.concatenate([next_modes, next_search, next_history], axis=1)
    stiff_all, mass_all = apply_operators(stiff_blocks, mass_blocks, block_cols, current.reshape(SUBS, SUBROWS, BASIS))
    stiff_all = stiff_all.reshape(ROWS, BASIS).astype(jnp.bfloat16)
    mass_all = mass_all.reshape(ROWS, BASIS).astype(jnp.bfloat16)
    gram_stiff = jnp.dot(current.T, stiff_all, preferred_element_type=jnp.float32)
    gram_mass = jnp.dot(current.T, mass_all, preferred_element_type=jnp.float32)
    gram = jnp.stack([gram_stiff, gram_mass], axis=1)
    return (current.reshape(SUBS, SUBROWS, BASIS), ritz_value, gram)
```

```python
import functools

import jax
import jax.numpy as jnp
from jax import lax
from jax.experimental import pallas as pl
from jax.experimental.pallas import tpu as pltpu
from jax.sharding import PartitionSpec as P

epsilon = 1e-06
tiny = 1e-30
f32 = jnp.float32
bf16 = jnp.bfloat16
VMEM_BYTES = 56 * 1024 * 1024


def vmem():
    return pl.BlockSpec(memory_space=pltpu.VMEM)


def smem():
    return pl.BlockSpec(memory_space=pltpu.SMEM)


def block_dot(pieces_k, slots, edge, cols, k, field, lanes):
    half = slots * edge
    top = jnp.concatenate([pieces_k[s * edge : (s + 1) * edge, :] for s in range(slots)], axis=1)
    low = jnp.concatenate(
        [pieces_k[half + s * edge : half + (s + 1) * edge, :] for s in range(slots)], axis=1
    )
    rows = [
        field[pl.ds(pl.multiple_of(cols[k, s] * edge, edge), edge), lanes] for s in range(slots)
    ]
    return jnp.dot(
        jnp.concatenate([top, low], axis=0),
        jnp.concatenate(rows, axis=0),
        preferred_element_type=f32,
    )


def column_stats(stiff_x, mass_x):
    num = jnp.sum(stiff_x * mass_x, axis=0, keepdims=True)
    den = jnp.sum(mass_x * mass_x, axis=0, keepdims=True)
    rest = stiff_x - (num / jnp.maximum(den, tiny)) * mass_x
    return num, den, jnp.sum(rest * rest, axis=0, keepdims=True)


def shift_and_scale(stats, total_rows):
    num, den, about = stats[0:1, :], stats[1:2, :], stats[2:3, :]
    shift = num / (den + epsilon)
    off = shift - num / jnp.maximum(den, tiny)
    scale = lax.rsqrt((about + off * off * den) / total_rows + epsilon)
    return shift, scale


def stats_kernel(nz, slots, edge, modes, rows_of, meta, cols, *refs):
    x_refs, km_refs = refs[:nz], refs[nz : nz + rows_of]
    stats_ref, field, stiff, mass = refs[nz + rows_of :]
    z = meta[0]
    for k in range(nz):
        field[pl.ds(pl.multiple_of((z ^ k) * edge, edge), edge), :] = x_refs[k][...]
    for k in range(rows_of):
        both = block_dot(km_refs[k], slots, edge, cols, k, field, slice(None))
        at = pl.ds(pl.multiple_of((z ^ k) * edge, edge), edge) if rows_of > 1 else slice(None)
        stiff[at, :] = both[:edge]
        mass[at, :] = both[edge:]
    num, den, about = column_stats(stiff[...], mass[...])
    stats_ref[0:1, :] = num
    stats_ref[1:2, :] = den
    stats_ref[2:3, :] = about


def sweep_kernel(nz, slots, edge, modes, total_rows, meta, cols, *refs):
    x_refs, h_refs, km_refs = refs[:nz], refs[nz : 2 * nz], refs[2 * nz : 3 * nz]
    stats, coeffs, turned_ref, stiff_ref, mass_ref, stats_ref, full = refs[3 * nz :]
    z = meta[0]
    at = [pl.ds(pl.multiple_of((z ^ k) * edge, edge), edge) for k in range(nz)]
    for k in range(nz):
        full[at[k], 0:modes] = x_refs[k][...]
        full[at[k], 2 * modes : 3 * modes] = h_refs[k][...]
    shift, scale = shift_and_scale(stats, total_rows)
    for k in range(nz):
        both = block_dot(km_refs[k], slots, edge, cols, k, full, slice(0, modes))
        full[at[k], modes : 2 * modes] = ((both[:edge] - shift * both[edge:]) * scale).astype(bf16)
    turned_ref[...] = jnp.dot(full[...], coeffs[...], preferred_element_type=f32).astype(bf16)
    for k in range(nz):
        both = block_dot(km_refs[k], slots, edge, cols, k, turned_ref, slice(0, modes))
        stiff_ref[at[k], :] = both[:edge]
        mass_ref[at[k], :] = both[edge:]
    num, den, about = column_stats(stiff_ref[...], mass_ref[...])
    stats_ref[0:1, :] = num
    stats_ref[1:2, :] = den
    stats_ref[2:3, :] = about


def gram_kernel(nz, ng, slots, edge, modes, total_rows, split, meta, cols, *refs):
    km_refs = refs[:nz]
    turned, stiff, mass, stats, basis_ref, ritz_ref, gram_ref, full, chosen, applied = refs[nz:]
    z, core, chip = meta[0], meta[1], meta[2]
    at = [pl.ds(pl.multiple_of((z ^ k) * edge, edge), edge) for k in range(nz)]
    width = 3 * modes // nz
    shift, scale = shift_and_scale(stats, total_rows)
    ritz_ref[...] = shift
    full[:, 0:modes] = turned[:, 0:modes]
    full[:, modes : 2 * modes] = ((stiff[...] - shift * mass[...]) * scale).astype(bf16)
    full[:, 2 * modes : 3 * modes] = turned[:, modes : 2 * modes]
    basis_ref[...] = full[at[0], :]
    window = chosen.shape[1]
    start = z * width // 128 * 128
    picked = full[:, pl.ds(pl.multiple_of(start, 128), window)].astype(f32)
    chosen[...] = pltpu.roll(picked, window - (z * width - start), 1).astype(bf16)
    for k in range(nz):
        both = block_dot(km_refs[k], slots, edge, cols, k, chosen, slice(0, width)).astype(bf16)
        applied[at[k], 0:width] = both[:edge]
        applied[at[k], width : 2 * width] = both[edge:]
    gram = lax.dot_general(
        full[...], applied[...], (((0,), (0,)), ((), ())), preferred_element_type=f32
    ).astype(bf16)
    if split:
        rows = 3 * modes // ng
        for q in range(ng):
            gram_ref[(q % 2) ^ core, (q // 2) ^ chip] = gram[q * rows : (q + 1) * rows]
    else:
        gram_ref[...] = gram


def call(kernel, inputs, n_smem, out_shape, scratch, flops):
    return pl.pallas_call(
        kernel,
        out_shape=out_shape,
        in_specs=[smem()] * n_smem + [vmem()] * (len(inputs) - n_smem),
        out_specs=jax.tree.map(lambda _: vmem(), out_shape),
        scratch_shapes=scratch,
        compiler_params=pltpu.CompilerParams(vmem_limit_bytes=VMEM_BYTES),
        cost_estimate=pl.CostEstimate(flops=flops, bytes_accessed=4_000_000, transcendentals=0),
    )(*inputs)


def by_xor(size, k):
    return [(i, i ^ k) for i in range(size)]


def merge(one, two):
    num, den = one[0] + two[0], one[1] + two[1]
    apart = one[0] / jnp.maximum(one[1], tiny) - two[0] / jnp.maximum(two[1], tiny)
    weight = jnp.sqrt(one[1]) * jnp.sqrt(two[1]) * lax.rsqrt(jnp.maximum(den, tiny))
    gap = apart * weight
    return jnp.stack([num, den, (one[2] + two[2]) + gap * gap])


def merge_over(axis, size, stats):
    step = 1
    if axis == "grp" and size >= 8:
        stats = merge(stats, lax.ppermute(stats, axis, by_xor(size, 1)))
        step = 2
        if size == 8:
            got = [lax.ppermute(stats, axis, by_xor(size, 2 * k)) for k in (1, 2, 3)]
            return merge(merge(stats, got[0]), merge(got[1], got[2]))
    while step < size:
        stats = merge(stats, lax.ppermute(stats, axis, by_xor(size, step)))
        step *= 2
    return stats


def gather(x, nz):
    return [x] + [lax.ppermute(x, "blk", by_xor(nz, k)) for k in range(1, nz)]


def body(basis, coeffs, stiff_blocks, mass_blocks, block_cols):
    nz, ng = lax.axis_size("blk"), lax.axis_size("grp")
    z, g = lax.axis_index("blk"), lax.axis_index("grp")
    current = basis[0]
    edge, columns = current.shape
    slots = block_cols.shape[-1]
    modes = columns // 3
    rows = edge * nz
    total_rows = rows * ng
    width = columns // nz

    tag = jnp.pad(block_cols[0, 0].astype(bf16)[None, :], ((0, 15), (0, edge - slots)))
    payload = jnp.concatenate(
        [
            stiff_blocks[0, 0].reshape(slots * edge, edge),
            mass_blocks[0, 0].reshape(slots * edge, edge),
            tag,
        ],
        axis=0,
    )
    first = jnp.dot(current, coeffs[0][:, :modes], preferred_element_type=f32).astype(bf16)
    x_parts = gather(first, nz)
    km_parts = gather(payload, nz)
    later = jnp.dot(current, coeffs[0][:, modes:], preferred_element_type=f32).astype(bf16)
    h_parts = gather(later, nz)

    meta = jnp.stack([z, g % 2, g // 2]).astype(jnp.int32)
    own_cols = block_cols[0]
    stats = call(
        functools.partial(stats_kernel, nz, slots, edge, modes, 1),
        [meta, own_cols, *x_parts, payload],
        2,
        jax.ShapeDtypeStruct((3, modes), f32),
        [
            pltpu.VMEM((rows, modes), bf16),
            pltpu.VMEM((edge, modes), f32),
            pltpu.VMEM((edge, modes), f32),
        ],
        4 * edge * slots * edge * modes,
    )
    stats = merge_over("blk", nz, stats)
    stats = merge_over("grp", ng, stats)

    cols = jnp.stack([p[2 * slots * edge, :slots] for p in km_parts]).astype(jnp.int32)
    turned, stiff_x, mass_x, stats = call(
        functools.partial(sweep_kernel, nz, slots, edge, modes, total_rows),
        [meta, cols, *x_parts, *h_parts, *km_parts, stats, coeffs[1]],
        2,
        (
            jax.ShapeDtypeStruct((rows, 2 * modes), bf16),
            jax.ShapeDtypeStruct((rows, modes), f32),
            jax.ShapeDtypeStruct((rows, modes), f32),
            jax.ShapeDtypeStruct((3, modes), f32),
        ),
        [pltpu.VMEM((rows, columns), bf16)],
        2 * rows * columns * 2 * modes,
    )
    stats = merge_over("grp", ng, stats)

    split = (columns // ng) % 16 == 0
    chips = ng // 2
    block = columns // ng
    gram_shape = (2, chips, block, 2 * width) if split else (columns, 2 * width)
    window = -(-(width + max(i * width % 128 for i in range(nz))) // 128) * 128
    basis_out, ritz, gram = call(
        functools.partial(gram_kernel, nz, ng, slots, edge, modes, total_rows, split),
        [meta, cols, *km_parts, turned, stiff_x, mass_x, stats],
        2,
        (
            jax.ShapeDtypeStruct((edge, columns), bf16),
            jax.ShapeDtypeStruct((1, modes), f32),
            jax.ShapeDtypeStruct(gram_shape, bf16),
        ),
        [
            pltpu.VMEM((rows, columns), bf16),
            pltpu.VMEM((rows, window), bf16),
            pltpu.VMEM((rows, 2 * width), bf16),
        ],
        2 * rows * columns * 2 * width,
    )
    if split:
        keep, send = gram[0], gram[1]
        got = lax.ppermute(send, "grp", by_xor(ng, 1))
        mine = (keep.astype(f32) + got.astype(f32)).astype(bf16)
        total = mine[0].astype(f32)
        for k in range(1, chips):
            total = total + lax.ppermute(mine[k], "grp", by_xor(ng, 2 * k)).astype(f32)
    else:
        total = lax.psum_scatter(gram, "grp", scatter_dimension=0, tiled=True).astype(f32)
    return (basis_out[None], ritz[0], total.reshape(block, 2, width))


def solution(mesh):
    in_specs = (
        P("grp", "blk", None),
        P(),
        P("grp", "blk", None, None, None),
        P("grp", "blk", None, None, None),
        P("grp", "blk", None),
    )
    out_specs = (P("grp", "blk", None), P(), P("grp", None, "blk"))
    return jax.shard_map(body, mesh=mesh, in_specs=in_specs, out_specs=out_specs, check_vma=False)
```

```python
import functools

import jax
import jax.numpy as jnp
from jax import lax
from jax.experimental import pallas as pl
from jax.experimental.pallas import tpu as pltpu
from jax.sharding import PartitionSpec as P

epsilon = 1e-06
tiny = 1e-30
f32 = jnp.float32
bf16 = jnp.bfloat16
VMEM_BYTES = 24 * 1024 * 1024


def vmem():
    return pl.BlockSpec(memory_space=pltpu.VMEM)


def smem():
    return pl.BlockSpec(memory_space=pltpu.SMEM)


def block_dot(pieces_k, slots, edge, cols, k, field, lanes):
    half = slots * edge
    top = jnp.concatenate([pieces_k[s * edge : (s + 1) * edge, :] for s in range(slots)], axis=1)
    low = jnp.concatenate(
        [pieces_k[half + s * edge : half + (s + 1) * edge, :] for s in range(slots)], axis=1
    )
    rows = [
        field[pl.ds(pl.multiple_of(cols[k, s] * edge, edge), edge), lanes] for s in range(slots)
    ]
    return jnp.dot(
        jnp.concatenate([top, low], axis=0),
        jnp.concatenate(rows, axis=0),
        preferred_element_type=f32,
    )


def column_stats(stiff_x, mass_x):
    num = jnp.sum(stiff_x * mass_x, axis=0, keepdims=True)
    den = jnp.sum(mass_x * mass_x, axis=0, keepdims=True)
    rest = stiff_x - (num / jnp.maximum(den, tiny)) * mass_x
    return num, den, jnp.sum(rest * rest, axis=0, keepdims=True)


def shift_and_scale(stats, total_rows):
    num, den, about = stats[0:1, :], stats[1:2, :], stats[2:3, :]
    shift = num / (den + epsilon)
    off = shift - num / jnp.maximum(den, tiny)
    scale = lax.rsqrt((about + off * off * den) / total_rows + epsilon)
    return shift, scale


def turn_kernel(current, coeffs, out_ref):
    out_ref[...] = jnp.dot(current[...], coeffs[0], preferred_element_type=f32).astype(bf16)


def turn_part(current, coeffs, sweep, part, modes):
    rows, columns = current.shape
    return pl.pallas_call(
        turn_kernel,
        grid=(1,),
        out_shape=jax.ShapeDtypeStruct((rows, modes), bf16),
        in_specs=[
            pl.BlockSpec((rows, columns), lambda i: (0, 0)),
            pl.BlockSpec((1, columns, modes), lambda i: (sweep, 0, part)),
        ],
        out_specs=pl.BlockSpec((rows, modes), lambda i: (0, 0)),
        compiler_params=pltpu.CompilerParams(vmem_limit_bytes=VMEM_BYTES),
        cost_estimate=pl.CostEstimate(
            flops=2 * rows * columns * modes, bytes_accessed=2 * columns * modes, transcendentals=0
        ),
    )(current, coeffs)


def stats_kernel(nz, slots, edge, modes, rows_of, cols, *refs):
    x_refs, km_refs = refs[:nz], refs[nz : nz + rows_of]
    stats_ref, field, stiff, mass = refs[nz + rows_of :]
    z = lax.axis_index("blk")
    for k in range(nz):
        field[pl.ds(pl.multiple_of((z ^ k) * edge, edge), edge), :] = x_refs[k][...]
    for k in range(rows_of):
        both = block_dot(km_refs[k], slots, edge, cols, k, field, slice(None))
        at = pl.ds(pl.multiple_of((z ^ k) * edge, edge), edge) if rows_of > 1 else slice(None)
        stiff[at, :] = both[:edge]
        mass[at, :] = both[edge:]
    num, den, about = column_stats(stiff[...], mass[...])
    stats_ref[0:1, :] = num
    stats_ref[1:2, :] = den
    stats_ref[2:3, :] = about


def sweep_kernel(nz, slots, edge, modes, total_rows, cols, *refs):
    x_refs, h_refs, km_refs = refs[:nz], refs[nz : 2 * nz], refs[2 * nz : 3 * nz]
    stats, coeffs, turned_ref, stiff_ref, mass_ref, stats_ref, full = refs[3 * nz :]
    z = lax.axis_index("blk")
    at = [pl.ds(pl.multiple_of((z ^ k) * edge, edge), edge) for k in range(nz)]
    for k in range(nz):
        full[at[k], 0:modes] = x_refs[k][...]
        full[at[k], 2 * modes : 3 * modes] = h_refs[k][...]
    shift, scale = shift_and_scale(stats, total_rows)
    for k in range(nz):
        both = block_dot(km_refs[k], slots, edge, cols, k, full, slice(0, modes))
        full[at[k], modes : 2 * modes] = ((both[:edge] - shift * both[edge:]) * scale).astype(bf16)
    turned_ref[...] = jnp.dot(full[...], coeffs[...], preferred_element_type=f32).astype(bf16)
    for k in range(nz):
        both = block_dot(km_refs[k], slots, edge, cols, k, turned_ref, slice(0, modes))
        stiff_ref[at[k], :] = both[:edge]
        mass_ref[at[k], :] = both[edge:]
    num, den, about = column_stats(stiff_ref[...], mass_ref[...])
    stats_ref[0:1, :] = num
    stats_ref[1:2, :] = den
    stats_ref[2:3, :] = about


def gram_kernel(nz, ng, slots, edge, modes, total_rows, split, cols, *refs):
    km_refs = refs[:nz]
    turned, stiff, mass, stats, basis_ref, ritz_ref, gram_ref, send_ref, full, chosen, applied = refs[nz:]
    z, g = lax.axis_index("blk"), lax.axis_index("grp")
    core, chip = lax.rem(g, 2), lax.div(g, 2)
    at = [pl.ds(pl.multiple_of((z ^ k) * edge, edge), edge) for k in range(nz)]
    width = 3 * modes // nz
    shift, scale = shift_and_scale(stats, total_rows)
    ritz_ref[...] = shift
    full[:, 0:modes] = turned[:, 0:modes]
    full[:, modes : 2 * modes] = ((stiff[...] - shift * mass[...]) * scale).astype(bf16)
    full[:, 2 * modes : 3 * modes] = turned[:, modes : 2 * modes]
    basis_ref[...] = full[at[0], :]
    window = chosen.shape[1]
    start = z * width // 128 * 128
    picked = full[:, pl.ds(pl.multiple_of(start, 128), window)].astype(f32)
    chosen[...] = pltpu.roll(picked, window - (z * width - start), 1).astype(bf16)
    for k in range(nz):
        both = block_dot(km_refs[k], slots, edge, cols, k, chosen, slice(0, width)).astype(bf16)
        applied[at[k], 0:width] = both[:edge]
        applied[at[k], width : 2 * width] = both[edge:]
    gram = lax.dot_general(
        full[...], applied[...], (((0,), (0,)), ((), ())), preferred_element_type=f32
    ).astype(bf16)
    if split:
        rows = 3 * modes // ng
        for q in range(ng):
            piece = gram[q * rows : (q + 1) * rows]

            @pl.when(core == q % 2)
            def _():
                gram_ref[(q // 2) ^ chip] = piece

            @pl.when(core != q % 2)
            def _():
                send_ref[(q // 2) ^ chip] = piece
    else:
        gram_ref[...] = gram


def call(kernel, inputs, n_smem, out_shape, scratch, flops):
    return pl.pallas_call(
        kernel,
        out_shape=out_shape,
        in_specs=[smem()] * n_smem + [vmem()] * (len(inputs) - n_smem),
        out_specs=jax.tree.map(lambda _: vmem(), out_shape),
        scratch_shapes=scratch,
        compiler_params=pltpu.CompilerParams(vmem_limit_bytes=VMEM_BYTES),
        cost_estimate=pl.CostEstimate(flops=flops, bytes_accessed=4_000_000, transcendentals=0),
    )(*inputs)


def by_xor(size, k):
    return [(i, i ^ k) for i in range(size)]


def merge(one, two):
    num, den = one[0] + two[0], one[1] + two[1]
    apart = one[0] / jnp.maximum(one[1], tiny) - two[0] / jnp.maximum(two[1], tiny)
    weight = jnp.sqrt(one[1]) * jnp.sqrt(two[1]) * lax.rsqrt(jnp.maximum(den, tiny))
    gap = apart * weight
    return jnp.stack([num, den, (one[2] + two[2]) + gap * gap])


def merge_over(axis, size, stats):
    step = 1
    if axis == "grp" and size >= 8:
        stats = merge(stats, lax.ppermute(stats, axis, by_xor(size, 1)))
        step = 2
        if size == 8:
            got = [lax.ppermute(stats, axis, by_xor(size, 2 * k)) for k in (1, 2, 3)]
            return merge(merge(stats, got[0]), merge(got[1], got[2]))
    while step < size:
        stats = merge(stats, lax.ppermute(stats, axis, by_xor(size, step)))
        step *= 2
    return stats


def gather(x, nz):
    return [x] + [lax.ppermute(x, "blk", by_xor(nz, k)) for k in range(1, nz)]


def body(basis, coeffs, stiff_blocks, mass_blocks, block_cols):
    nz, ng = lax.axis_size("blk"), lax.axis_size("grp")
    current = basis[0]
    edge, columns = current.shape
    slots = block_cols.shape[-1]
    modes = columns // 3
    rows = edge * nz
    total_rows = rows * ng
    width = columns // nz

    payload = jnp.concatenate(
        [
            stiff_blocks[0, 0].reshape(slots * edge, edge),
            mass_blocks[0, 0].reshape(slots * edge, edge),
        ],
        axis=0,
    )
    first = turn_part(current, coeffs, 0, 0, modes)
    x_parts = gather(first, nz)
    km_parts = gather(payload, nz)
    later = turn_part(current, coeffs, 0, 1, modes)
    h_parts = gather(later, nz)

    cols = jnp.concatenate(gather(block_cols[0], nz))
    stats = call(
        functools.partial(stats_kernel, nz, slots, edge, modes, nz),
        [cols, *x_parts, *km_parts],
        1,
        jax.ShapeDtypeStruct((3, modes), f32),
        [
            pltpu.VMEM((rows, modes), bf16),
            pltpu.VMEM((rows, modes), f32),
            pltpu.VMEM((rows, modes), f32),
        ],
        4 * edge * slots * edge * modes,
    )
    stats = merge_over("grp", ng, stats)

    turned, stiff_x, mass_x, stats = call(
        functools.partial(sweep_kernel, nz, slots, edge, modes, total_rows),
        [cols, *x_parts, *h_parts, *km_parts, stats, coeffs[1]],
        1,
        (
            jax.ShapeDtypeStruct((rows, 2 * modes), bf16),
            jax.ShapeDtypeStruct((rows, modes), f32),
            jax.ShapeDtypeStruct((rows, modes), f32),
            jax.ShapeDtypeStruct((3, modes), f32),
        ),
        [pltpu.VMEM((rows, columns), bf16)],
        2 * rows * columns * 2 * modes,
    )
    stats = merge_over("grp", ng, stats)

    split = (columns // ng) % 16 == 0
    chips = ng // 2
    block = columns // ng
    gram_shape = (chips, block, 2 * width) if split else (columns, 2 * width)
    window = -(-(width + max(i * width % 128 for i in range(nz))) // 128) * 128
    basis_out, ritz, gram, send = call(
        functools.partial(gram_kernel, nz, ng, slots, edge, modes, total_rows, split),
        [cols, *km_parts, turned, stiff_x, mass_x, stats],
        1,
        (
            jax.ShapeDtypeStruct((edge, columns), bf16),
            jax.ShapeDtypeStruct((1, modes), f32),
            jax.ShapeDtypeStruct(gram_shape, bf16),
            jax.ShapeDtypeStruct(gram_shape, bf16),
        ),
        [
            pltpu.VMEM((rows, columns), bf16),
            pltpu.VMEM((rows, window), bf16),
            pltpu.VMEM((rows, 2 * width), bf16),
        ],
        2 * rows * columns * 2 * width,
    )
    if split:
        got = lax.ppermute(send, "grp", by_xor(ng, 1))
        mine = (gram.astype(f32) + got.astype(f32)).astype(bf16)
        total = mine[0].astype(f32)
        for k in range(1, chips):
            total = total + lax.ppermute(mine[k], "grp", by_xor(ng, 2 * k)).astype(f32)
    else:
        total = lax.psum_scatter(gram, "grp", scatter_dimension=0, tiled=True).astype(f32)
    return (basis_out[None], ritz[0], total.reshape(block, 2, width))


def solution(mesh):
    in_specs = (
        P("grp", "blk", None),
        P(),
        P("grp", "blk", None, None, None),
        P("grp", "blk", None, None, None),
        P("grp", "blk", None),
    )
    out_specs = (P("grp", "blk", None), P(), P("grp", None, "blk"))
    return jax.shard_map(body, mesh=mesh, in_specs=in_specs, out_specs=out_specs, check_vma=False)
```

```python
import functools

import jax
import jax.numpy as jnp
from jax import lax
from jax.experimental import pallas as pl
from jax.experimental.pallas import tpu as pltpu
from jax.sharding import PartitionSpec as P

epsilon = 1e-06
tiny = 1e-30
f32 = jnp.float32
bf16 = jnp.bfloat16
VMEM_BYTES = 24 * 1024 * 1024


def vmem():
    return pl.BlockSpec(memory_space=pltpu.VMEM)


def smem():
    return pl.BlockSpec(memory_space=pltpu.SMEM)


def block_dot(pieces_k, slots, edge, cols, k, field, lanes):
    half = slots * edge
    top = jnp.concatenate([pieces_k[s * edge : (s + 1) * edge, :] for s in range(slots)], axis=1)
    low = jnp.concatenate(
        [pieces_k[half + s * edge : half + (s + 1) * edge, :] for s in range(slots)], axis=1
    )
    rows = [
        field[pl.ds(pl.multiple_of(cols[k, s] * edge, edge), edge), lanes] for s in range(slots)
    ]
    return jnp.dot(
        jnp.concatenate([top, low], axis=0),
        jnp.concatenate(rows, axis=0),
        preferred_element_type=f32,
    )


def column_stats(stiff_x, mass_x):
    num = jnp.sum(stiff_x * mass_x, axis=0, keepdims=True)
    den = jnp.sum(mass_x * mass_x, axis=0, keepdims=True)
    rest = stiff_x - (num / jnp.maximum(den, tiny)) * mass_x
    return num, den, jnp.sum(rest * rest, axis=0, keepdims=True)


def shift_and_scale(stats, total_rows):
    num, den, about = stats[0:1, :], stats[1:2, :], stats[2:3, :]
    shift = num / (den + epsilon)
    off = shift - num / jnp.maximum(den, tiny)
    scale = lax.rsqrt((about + off * off * den) / total_rows + epsilon)
    return shift, scale


def turn_kernel(modes, current, coeffs, first_ref, later_ref):
    turned = jnp.dot(current[...], coeffs[0], preferred_element_type=f32).astype(bf16)
    first_ref[...] = turned[:, :modes]
    later_ref[...] = turned[:, modes:]


def turn_first(current, coeffs, modes):
    rows, columns = current.shape
    half = jax.ShapeDtypeStruct((rows, modes), bf16)
    return pl.pallas_call(
        functools.partial(turn_kernel, modes),
        grid=(1,),
        out_shape=(half, half),
        in_specs=[
            pl.BlockSpec((rows, columns), lambda i: (0, 0)),
            pl.BlockSpec((1, columns, 2 * modes), lambda i: (0, 0, 0)),
        ],
        out_specs=(pl.BlockSpec((rows, modes), lambda i: (0, 0)),) * 2,
        compiler_params=pltpu.CompilerParams(vmem_limit_bytes=VMEM_BYTES),
        cost_estimate=pl.CostEstimate(
            flops=4 * rows * columns * modes, bytes_accessed=4 * columns * modes, transcendentals=0
        ),
    )(current, coeffs)


def stats_kernel(nz, slots, edge, cols, *refs):
    x_refs, km_refs = refs[:nz], refs[nz : 2 * nz]
    _, stats_ref, field, stiff, mass = refs[2 * nz :]
    z = lax.axis_index("blk")
    for k in range(nz):
        field[pl.ds(pl.multiple_of((z ^ k) * edge, edge), edge), :] = x_refs[k][...]
    for k in range(nz):
        both = block_dot(km_refs[k], slots, edge, cols, k, field, slice(None))
        at = pl.ds(pl.multiple_of((z ^ k) * edge, edge), edge)
        stiff[at, :] = both[:edge]
        mass[at, :] = both[edge:]
    num, den, about = column_stats(stiff[...], mass[...])
    stats_ref[0:1, :] = num
    stats_ref[1:2, :] = den
    stats_ref[2:3, :] = about


def sweep_kernel(nz, slots, edge, modes, total_rows, cols, *refs):
    x_refs, h_refs, km_refs = refs[:nz], refs[nz : 2 * nz], refs[2 * nz : 3 * nz]
    stats, coeffs, turned_ref, stiff_ref, mass_ref, stats_ref, full = refs[3 * nz :]
    z = lax.axis_index("blk")
    at = [pl.ds(pl.multiple_of((z ^ k) * edge, edge), edge) for k in range(nz)]
    for k in range(nz):
        full[at[k], 0:modes] = x_refs[k][...]
        full[at[k], 2 * modes : 3 * modes] = h_refs[k][...]
    shift, scale = shift_and_scale(stats, total_rows)
    for k in range(nz):
        both = block_dot(km_refs[k], slots, edge, cols, k, full, slice(0, modes))
        full[at[k], modes : 2 * modes] = ((both[:edge] - shift * both[edge:]) * scale).astype(bf16)
    turned_ref[...] = jnp.dot(full[...], coeffs[...], preferred_element_type=f32).astype(bf16)
    for k in range(nz):
        both = block_dot(km_refs[k], slots, edge, cols, k, turned_ref, slice(0, modes))
        stiff_ref[at[k], :] = both[:edge]
        mass_ref[at[k], :] = both[edge:]
    num, den, about = column_stats(stiff_ref[...], mass_ref[...])
    stats_ref[0:1, :] = num
    stats_ref[1:2, :] = den
    stats_ref[2:3, :] = about


def gram_kernel(nz, ng, slots, edge, modes, total_rows, split, cols, *refs):
    km_refs = refs[:nz]
    turned, stiff, mass, stats, basis_ref, ritz_ref, gram_ref, send_ref, full, chosen, applied = refs[nz:]
    z, g = lax.axis_index("blk"), lax.axis_index("grp")
    core, chip = lax.rem(g, 2), lax.div(g, 2)
    at = [pl.ds(pl.multiple_of((z ^ k) * edge, edge), edge) for k in range(nz)]
    width = 3 * modes // nz
    shift, scale = shift_and_scale(stats, total_rows)
    ritz_ref[...] = shift
    full[:, 0:modes] = turned[:, 0:modes]
    full[:, modes : 2 * modes] = ((stiff[...] - shift * mass[...]) * scale).astype(bf16)
    full[:, 2 * modes : 3 * modes] = turned[:, modes : 2 * modes]
    basis_ref[...] = full[at[0], :]
    window = chosen.shape[1]
    start = z * width // 128 * 128
    picked = full[:, pl.ds(pl.multiple_of(start, 128), window)].astype(f32)
    chosen[...] = pltpu.roll(picked, window - (z * width - start), 1).astype(bf16)
    for k in range(nz):
        both = block_dot(km_refs[k], slots, edge, cols, k, chosen, slice(0, width)).astype(bf16)
        applied[at[k], 0:width] = both[:edge]
        applied[at[k], width : 2 * width] = both[edge:]
    gram = lax.dot_general(
        full[...], applied[...], (((0,), (0,)), ((), ())), preferred_element_type=f32
    ).astype(bf16)
    if split:
        rows = 3 * modes // ng
        for q in range(ng):
            piece = gram[q * rows : (q + 1) * rows]

            @pl.when(core == q % 2)
            def _():
                gram_ref[(q // 2) ^ chip] = piece

            @pl.when(core != q % 2)
            def _():
                send_ref[(q // 2) ^ chip] = piece
    else:
        gram_ref[...] = gram


def call(kernel, inputs, n_smem, out_shape, scratch, flops):
    return pl.pallas_call(
        kernel,
        out_shape=out_shape,
        in_specs=[smem()] * n_smem + [vmem()] * (len(inputs) - n_smem),
        out_specs=jax.tree.map(lambda _: vmem(), out_shape),
        scratch_shapes=scratch,
        compiler_params=pltpu.CompilerParams(vmem_limit_bytes=VMEM_BYTES),
        cost_estimate=pl.CostEstimate(flops=flops, bytes_accessed=4_000_000, transcendentals=0),
    )(*inputs)


def by_xor(size, k):
    return [(i, i ^ k) for i in range(size)]


def merge(one, two):
    num, den = one[0] + two[0], one[1] + two[1]
    apart = one[0] / jnp.maximum(one[1], tiny) - two[0] / jnp.maximum(two[1], tiny)
    weight = jnp.sqrt(one[1]) * jnp.sqrt(two[1]) * lax.rsqrt(jnp.maximum(den, tiny))
    gap = apart * weight
    return jnp.stack([num, den, (one[2] + two[2]) + gap * gap])


def merge_over(axis, size, stats):
    step = 1
    if axis == "grp" and size >= 8:
        stats = merge(stats, lax.ppermute(stats, axis, by_xor(size, 1)))
        step = 2
        if size == 8:
            got = [lax.ppermute(stats, axis, by_xor(size, 2 * k)) for k in (1, 2, 3)]
            return merge(merge(stats, got[0]), merge(got[1], got[2]))
    while step < size:
        stats = merge(stats, lax.ppermute(stats, axis, by_xor(size, step)))
        step *= 2
    return stats


def gather(x, nz):
    return [x] + [lax.ppermute(x, "blk", by_xor(nz, k)) for k in range(1, nz)]


def body(basis, coeffs, stiff_blocks, mass_blocks, block_cols):
    nz, ng = lax.axis_size("blk"), lax.axis_size("grp")
    current = basis[0]
    edge, columns = current.shape
    slots = block_cols.shape[-1]
    modes = columns // 3
    rows = edge * nz
    total_rows = rows * ng
    width = columns // nz

    tag = jnp.pad(block_cols[0, 0].astype(bf16)[None, :], ((0, 15), (0, edge - slots)))
    payload = jnp.concatenate(
        [
            stiff_blocks[0, 0].reshape(slots * edge, edge),
            mass_blocks[0, 0].reshape(slots * edge, edge),
            tag,
        ],
        axis=0,
    )
    first, later = turn_first(current, coeffs, modes)
    x_parts = gather(first, nz)
    km_parts = gather(payload, nz)
    h_parts = gather(later, nz)

    cols = jnp.stack([p[2 * slots * edge, :slots] for p in km_parts]).astype(jnp.int32)
    stats = call(
        functools.partial(stats_kernel, nz, slots, edge),
        [cols, *x_parts, *km_parts, h_parts[1]],
        1,
        jax.ShapeDtypeStruct((3, modes), f32),
        [
            pltpu.VMEM((rows, modes), bf16),
            pltpu.VMEM((rows, modes), f32),
            pltpu.VMEM((rows, modes), f32),
        ],
        4 * edge * slots * edge * modes,
    )
    stats = merge_over("grp", ng, stats)

    turned, stiff_x, mass_x, stats = call(
        functools.partial(sweep_kernel, nz, slots, edge, modes, total_rows),
        [cols, *x_parts, *h_parts, *km_parts, stats, coeffs[1]],
        1,
        (
            jax.ShapeDtypeStruct((rows, 2 * modes), bf16),
            jax.ShapeDtypeStruct((rows, modes), f32),
            jax.ShapeDtypeStruct((rows, modes), f32),
            jax.ShapeDtypeStruct((3, modes), f32),
        ),
        [pltpu.VMEM((rows, columns), bf16)],
        2 * rows * columns * 2 * modes,
    )
    stats = merge_over("grp", ng, stats)

    split = (columns // ng) % 16 == 0
    chips = ng // 2
    block = columns // ng
    gram_shape = (chips, block, 2 * width) if split else (columns, 2 * width)
    window = -(-(width + max(i * width % 128 for i in range(nz))) // 128) * 128
    basis_out, ritz, gram, send = call(
        functools.partial(gram_kernel, nz, ng, slots, edge, modes, total_rows, split),
        [cols, *km_parts, turned, stiff_x, mass_x, stats],
        1,
        (
            jax.ShapeDtypeStruct((edge, columns), bf16),
            jax.ShapeDtypeStruct((1, modes), f32),
            jax.ShapeDtypeStruct(gram_shape, bf16),
            jax.ShapeDtypeStruct(gram_shape, bf16),
        ),
        [
            pltpu.VMEM((rows, columns), bf16),
            pltpu.VMEM((rows, window), bf16),
            pltpu.VMEM((rows, 2 * width), bf16),
        ],
        2 * rows * columns * 2 * width,
    )
    if split:
        got = lax.ppermute(send, "grp", by_xor(ng, 1))
        mine = (gram.astype(f32) + got.astype(f32)).astype(bf16)
        total = mine[0].astype(f32)
        for k in range(1, chips):
            total = total + lax.ppermute(mine[k], "grp", by_xor(ng, 2 * k)).astype(f32)
    else:
        total = lax.psum_scatter(gram, "grp", scatter_dimension=0, tiled=True).astype(f32)
    return (basis_out[None], ritz[0], total.reshape(block, 2, width))


def solution(mesh):
    in_specs = (
        P("grp", "blk", None),
        P(),
        P("grp", "blk", None, None, None),
        P("grp", "blk", None, None, None),
        P("grp", "blk", None),
    )
    out_specs = (P("grp", "blk", None), P(), P("grp", None, "blk"))
    return jax.shard_map(body, mesh=mesh, in_specs=in_specs, out_specs=out_specs, check_vma=False)
```

```python
import functools

import jax
import jax.numpy as jnp
from jax import lax
from jax.experimental import pallas as pl
from jax.experimental.pallas import tpu as pltpu
from jax.sharding import PartitionSpec as P

epsilon = 1e-06
tiny = 1e-30
f32 = jnp.float32
bf16 = jnp.bfloat16
VMEM_BYTES = 24 * 1024 * 1024
FIRST_VMEM_BYTES = 61 * 1024 * 1024


def vmem():
    return pl.BlockSpec(memory_space=pltpu.VMEM)


def smem():
    return pl.BlockSpec(memory_space=pltpu.SMEM)


def block_dot(pieces_k, slots, edge, cols, k, field, lanes):
    half = slots * edge
    top = jnp.concatenate([pieces_k[s * edge : (s + 1) * edge, :] for s in range(slots)], axis=1)
    low = jnp.concatenate(
        [pieces_k[half + s * edge : half + (s + 1) * edge, :] for s in range(slots)], axis=1
    )
    rows = [
        field[pl.ds(pl.multiple_of(cols[k, s] * edge, edge), edge), lanes] for s in range(slots)
    ]
    return jnp.dot(
        jnp.concatenate([top, low], axis=0),
        jnp.concatenate(rows, axis=0),
        preferred_element_type=f32,
    )


def column_stats(stiff_x, mass_x):
    num = jnp.sum(stiff_x * mass_x, axis=0, keepdims=True)
    den = jnp.sum(mass_x * mass_x, axis=0, keepdims=True)
    rest = stiff_x - (num / jnp.maximum(den, tiny)) * mass_x
    return num, den, jnp.sum(rest * rest, axis=0, keepdims=True)


def shift_and_scale(stats, total_rows):
    num, den, about = stats[0:1, :], stats[1:2, :], stats[2:3, :]
    shift = num / (den + epsilon)
    off = shift - num / jnp.maximum(den, tiny)
    scale = lax.rsqrt((about + off * off * den) / total_rows + epsilon)
    return shift, scale


def hbm():
    return pl.BlockSpec(memory_space=pltpu.HBM)


def first_kernel(
    chunks, modes, cols, stiff_hbm, mass_hbm, current_hbm, coeffs_hbm,
    packed_ref, later_ref, current, coeffs, sems,
):
    kept, edge = stiff_hbm.shape
    rows = current.shape[1] // chunks
    copies = [pltpu.make_async_copy(current_hbm, current, sems.at[0])]
    for c in range(chunks):
        part = pl.ds(c * rows, rows)
        copies.append(pltpu.make_async_copy(coeffs_hbm.at[0, part], coeffs.at[part], sems.at[c + 1]))
    for i, operator in enumerate((stiff_hbm, mass_hbm)):
        target = packed_ref.at[pl.ds(i * kept, kept)]
        copies.append(pltpu.make_async_copy(operator, target, sems.at[chunks + 1 + i]))
    for copy in copies:
        copy.start()
    lane = lax.broadcasted_iota(jnp.int32, (16, edge), 1)
    tag = jnp.zeros((16, edge), jnp.int32)
    for s in range(kept // edge):
        tag = jnp.where(lane == s, cols[0, s], tag)
    packed_ref[2 * kept : 2 * kept + 16, :] = tag.astype(f32).astype(bf16)
    copies[0].wait()
    turned = None
    for c in range(chunks):
        copies[c + 1].wait()
        part = slice(c * rows, (c + 1) * rows)
        more = jnp.dot(current[:, part], coeffs[part, :], preferred_element_type=f32)
        turned = more if turned is None else turned + more
    turned = turned.astype(bf16)
    for b in range(modes // edge):
        packed_ref[pl.ds(2 * kept + 16 + b * current.shape[0], current.shape[0]), :] = turned[
            :, b * edge : (b + 1) * edge
        ]
    later_ref[...] = turned[:, modes:]
    copies[chunks + 1].wait()
    copies[chunks + 2].wait()


def first_step(cols, stiff, mass, current, coeffs, modes):
    rows, columns = current.shape
    kept, edge = stiff.shape
    half = jax.ShapeDtypeStruct((rows, modes), bf16)
    chunks = 3
    return pl.pallas_call(
        functools.partial(first_kernel, chunks, modes),
        out_shape=(jax.ShapeDtypeStruct((2 * kept + 16 + modes, edge), bf16), half),
        in_specs=[smem(), hbm(), hbm(), hbm(), hbm()],
        out_specs=(vmem(),) * 2,
        scratch_shapes=[
            pltpu.VMEM((rows, columns), bf16),
            pltpu.VMEM((columns, 2 * modes), bf16),
            pltpu.SemaphoreType.DMA((chunks + 3,)),
        ],
        compiler_params=pltpu.CompilerParams(vmem_limit_bytes=FIRST_VMEM_BYTES),
        cost_estimate=pl.CostEstimate(
            flops=4 * rows * columns * modes, bytes_accessed=4 * columns * modes, transcendentals=0
        ),
    )(cols, stiff, mass, current, coeffs)


def unpack_modes(z, slots, edge, km_refs, field):
    base = 2 * slots * edge + 16
    for k, packed in enumerate(km_refs):
        at = pl.ds(pl.multiple_of((z ^ k) * edge, edge), edge)
        for b in range((packed.shape[0] - base) // edge):
            part = packed[base + b * edge : base + (b + 1) * edge, :]
            field[at, b * edge : (b + 1) * edge] = part


def stats_kernel(nz, slots, edge, cols, *refs):
    km_refs = refs[:nz]
    stats_ref, field, stiff, mass = refs[nz:]
    z = lax.axis_index("blk")
    unpack_modes(z, slots, edge, km_refs, field)
    for k in range(nz):
        both = block_dot(km_refs[k], slots, edge, cols, k, field, slice(None))
        at = pl.ds(pl.multiple_of((z ^ k) * edge, edge), edge)
        stiff[at, :] = both[:edge]
        mass[at, :] = both[edge:]
    num, den, about = column_stats(stiff[...], mass[...])
    stats_ref[0:1, :] = num
    stats_ref[1:2, :] = den
    stats_ref[2:3, :] = about


def sweep_kernel(nz, slots, edge, modes, total_rows, cols, *refs):
    h_refs, km_refs = refs[:nz], refs[nz : 2 * nz]
    stats, coeffs, turned_ref, stiff_ref, mass_ref, stats_ref, full = refs[2 * nz :]
    z = lax.axis_index("blk")
    at = [pl.ds(pl.multiple_of((z ^ k) * edge, edge), edge) for k in range(nz)]
    unpack_modes(z, slots, edge, km_refs, full)
    for k in range(nz):
        full[at[k], 2 * modes : 3 * modes] = h_refs[k][...]
    shift, scale = shift_and_scale(stats, total_rows)
    for k in range(nz):
        both = block_dot(km_refs[k], slots, edge, cols, k, full, slice(0, modes))
        full[at[k], modes : 2 * modes] = ((both[:edge] - shift * both[edge:]) * scale).astype(bf16)
    turned_ref[...] = jnp.dot(full[...], coeffs[...], preferred_element_type=f32).astype(bf16)
    for k in range(nz):
        both = block_dot(km_refs[k], slots, edge, cols, k, turned_ref, slice(0, modes))
        stiff_ref[at[k], :] = both[:edge]
        mass_ref[at[k], :] = both[edge:]
    num, den, about = column_stats(stiff_ref[...], mass_ref[...])
    stats_ref[0:1, :] = num
    stats_ref[1:2, :] = den
    stats_ref[2:3, :] = about


def gram_kernel(nz, ng, slots, edge, modes, total_rows, split, cols, *refs):
    km_refs = refs[:nz]
    turned, stiff, mass, stats, basis_ref, ritz_ref, gram_ref, send_ref, full, chosen, applied = refs[nz:]
    z, g = lax.axis_index("blk"), lax.axis_index("grp")
    core, chip = lax.rem(g, 2), lax.div(g, 2)
    at = [pl.ds(pl.multiple_of((z ^ k) * edge, edge), edge) for k in range(nz)]
    width = 3 * modes // nz
    shift, scale = shift_and_scale(stats, total_rows)
    ritz_ref[...] = shift
    full[:, 0:modes] = turned[:, 0:modes]
    full[:, modes : 2 * modes] = ((stiff[...] - shift * mass[...]) * scale).astype(bf16)
    full[:, 2 * modes : 3 * modes] = turned[:, modes : 2 * modes]
    basis_ref[...] = full[at[0], :]
    window = chosen.shape[1]
    start = z * width // 128 * 128
    picked = full[:, pl.ds(pl.multiple_of(start, 128), window)].astype(f32)
    chosen[...] = pltpu.roll(picked, window - (z * width - start), 1).astype(bf16)
    for k in range(nz):
        both = block_dot(km_refs[k], slots, edge, cols, k, chosen, slice(0, width)).astype(bf16)
        applied[at[k], 0:width] = both[:edge]
        applied[at[k], width : 2 * width] = both[edge:]
    gram = lax.dot_general(
        full[...], applied[...], (((0,), (0,)), ((), ())), preferred_element_type=f32
    ).astype(bf16)
    if split:
        rows = 3 * modes // ng
        for q in range(ng):
            piece = gram[q * rows : (q + 1) * rows]

            @pl.when(core == q % 2)
            def _():
                gram_ref[(q // 2) ^ chip] = piece

            @pl.when(core != q % 2)
            def _():
                send_ref[(q // 2) ^ chip] = piece
    else:
        gram_ref[...] = gram


def call(kernel, inputs, n_smem, out_shape, scratch, flops):
    return pl.pallas_call(
        kernel,
        out_shape=out_shape,
        in_specs=[smem()] * n_smem + [vmem()] * (len(inputs) - n_smem),
        out_specs=jax.tree.map(lambda _: vmem(), out_shape),
        scratch_shapes=scratch,
        compiler_params=pltpu.CompilerParams(vmem_limit_bytes=VMEM_BYTES),
        cost_estimate=pl.CostEstimate(flops=flops, bytes_accessed=4_000_000, transcendentals=0),
    )(*inputs)


def by_xor(size, k):
    return [(i, i ^ k) for i in range(size)]


def merge(one, two):
    num, den = one[0] + two[0], one[1] + two[1]
    apart = one[0] / jnp.maximum(one[1], tiny) - two[0] / jnp.maximum(two[1], tiny)
    weight = jnp.sqrt(one[1]) * jnp.sqrt(two[1]) * lax.rsqrt(jnp.maximum(den, tiny))
    gap = apart * weight
    return jnp.stack([num, den, (one[2] + two[2]) + gap * gap])


def merge_over(axis, size, stats):
    step = 1
    if axis == "grp" and size >= 8:
        stats = merge(stats, lax.ppermute(stats, axis, by_xor(size, 1)))
        step = 2
        if size == 8:
            got = [lax.ppermute(stats, axis, by_xor(size, 2 * k)) for k in (1, 2, 3)]
            return merge(merge(stats, got[0]), merge(got[1], got[2]))
    while step < size:
        stats = merge(stats, lax.ppermute(stats, axis, by_xor(size, step)))
        step *= 2
    return stats


def gather(x, nz):
    parts = {0: x}
    step = nz // 2
    while step:
        parts |= {k ^ step: lax.ppermute(p, "blk", by_xor(nz, step)) for k, p in parts.items()}
        step //= 2
    return [parts[k] for k in range(nz)]


def body(basis, coeffs, stiff_blocks, mass_blocks, block_cols):
    nz, ng = lax.axis_size("blk"), lax.axis_size("grp")
    current = basis[0]
    edge, columns = current.shape
    slots = block_cols.shape[-1]
    modes = columns // 3
    rows = edge * nz
    total_rows = rows * ng
    width = columns // nz

    payload, later = first_step(
        block_cols[0],
        stiff_blocks[0, 0].reshape(slots * edge, edge),
        mass_blocks[0, 0].reshape(slots * edge, edge),
        current,
        coeffs,
        modes,
    )
    km_parts = gather(payload, nz)
    h_parts = gather(later, nz)

    cols = jnp.stack([p[2 * slots * edge, :slots] for p in km_parts]).astype(jnp.int32)
    stats = call(
        functools.partial(stats_kernel, nz, slots, edge),
        [cols, *km_parts],
        1,
        jax.ShapeDtypeStruct((3, modes), f32),
        [
            pltpu.VMEM((rows, modes), bf16),
            pltpu.VMEM((rows, modes), f32),
            pltpu.VMEM((rows, modes), f32),
        ],
        4 * edge * slots * edge * modes,
    )
    stats = merge_over("grp", ng, stats)

    turned, stiff_x, mass_x, stats = call(
        functools.partial(sweep_kernel, nz, slots, edge, modes, total_rows),
        [cols, *h_parts, *km_parts, stats, coeffs[1]],
        1,
        (
            jax.ShapeDtypeStruct((rows, 2 * modes), bf16),
            jax.ShapeDtypeStruct((rows, modes), f32),
            jax.ShapeDtypeStruct((rows, modes), f32),
            jax.ShapeDtypeStruct((3, modes), f32),
        ),
        [pltpu.VMEM((rows, columns), bf16)],
        2 * rows * columns * 2 * modes,
    )
    stats = merge_over("grp", ng, stats)

    split = (columns // ng) % 16 == 0
    chips = ng // 2
    block = columns // ng
    gram_shape = (chips, block, 2 * width) if split else (columns, 2 * width)
    window = -(-(width + max(i * width % 128 for i in range(nz))) // 128) * 128
    basis_out, ritz, gram, send = call(
        functools.partial(gram_kernel, nz, ng, slots, edge, modes, total_rows, split),
        [cols, *km_parts, turned, stiff_x, mass_x, stats],
        1,
        (
            jax.ShapeDtypeStruct((edge, columns), bf16),
            jax.ShapeDtypeStruct((1, modes), f32),
            jax.ShapeDtypeStruct(gram_shape, bf16),
            jax.ShapeDtypeStruct(gram_shape, bf16),
        ),
        [
            pltpu.VMEM((rows, columns), bf16),
            pltpu.VMEM((rows, window), bf16),
            pltpu.VMEM((rows, 2 * width), bf16),
        ],
        2 * rows * columns * 2 * width,
    )
    if split:
        got = lax.ppermute(send, "grp", by_xor(ng, 1))
        mine = (gram.astype(f32) + got.astype(f32)).astype(bf16)
        total = mine[0].astype(f32)
        for k in range(1, chips):
            total = total + lax.ppermute(mine[k], "grp", by_xor(ng, 2 * k)).astype(f32)
    else:
        total = lax.psum_scatter(gram, "grp", scatter_dimension=0, tiled=True).astype(f32)
    return (basis_out[None], ritz[0], total.reshape(block, 2, width))


def solution(mesh):
    in_specs = (
        P("grp", "blk", None),
        P(),
        P("grp", "blk", None, None, None),
        P("grp", "blk", None, None, None),
        P("grp", "blk", None),
    )
    out_specs = (P("grp", "blk", None), P(), P("grp", None, "blk"))
    return jax.shard_map(body, mesh=mesh, in_specs=in_specs, out_specs=out_specs, check_vma=False)
```

```python
import functools

import jax
import jax.numpy as jnp
from jax import lax
from jax.experimental import pallas as pl
from jax.experimental.pallas import tpu as pltpu
from jax.sharding import PartitionSpec as P

epsilon = 1e-06
tiny = 1e-30
f32 = jnp.float32
bf16 = jnp.bfloat16
VMEM_BYTES = 24 * 1024 * 1024


def vmem():
    return pl.BlockSpec(memory_space=pltpu.VMEM)


def smem():
    return pl.BlockSpec(memory_space=pltpu.SMEM)


def block_dot(pieces_k, slots, edge, cols, k, field, lanes):
    half = slots * edge
    top = jnp.concatenate([pieces_k[s * edge : (s + 1) * edge, :] for s in range(slots)], axis=1)
    low = jnp.concatenate(
        [pieces_k[half + s * edge : half + (s + 1) * edge, :] for s in range(slots)], axis=1
    )
    rows = [
        field[pl.ds(pl.multiple_of(cols[k, s] * edge, edge), edge), lanes] for s in range(slots)
    ]
    return jnp.dot(
        jnp.concatenate([top, low], axis=0),
        jnp.concatenate(rows, axis=0),
        preferred_element_type=f32,
    )


def column_stats(stiff_x, mass_x):
    num = jnp.sum(stiff_x * mass_x, axis=0, keepdims=True)
    den = jnp.sum(mass_x * mass_x, axis=0, keepdims=True)
    rest = stiff_x - (num / jnp.maximum(den, tiny)) * mass_x
    return num, den, jnp.sum(rest * rest, axis=0, keepdims=True)


def shift_and_scale(stats, total_rows):
    num, den, about = stats[0:1, :], stats[1:2, :], stats[2:3, :]
    shift = num / (den + epsilon)
    off = shift - num / jnp.maximum(den, tiny)
    scale = lax.rsqrt((about + off * off * den) / total_rows + epsilon)
    return shift, scale


def block_dot(pieces_k, slots, edge, cols, k, field, lanes):
    half = slots * edge
    top = jnp.concatenate([pieces_k[s * edge : (s + 1) * edge, :] for s in range(slots)], axis=1)
    low = jnp.concatenate(
        [pieces_k[half + s * edge : half + (s + 1) * edge, :] for s in range(slots)], axis=1
    )
    rows = [
        field[pl.ds(pl.multiple_of(cols[k, s] * edge, edge), edge), lanes] for s in range(slots)
    ]
    return jnp.dot(
        jnp.concatenate([top, low], axis=0),
        jnp.concatenate(rows, axis=0),
        preferred_element_type=f32,
    )


def column_stats(stiff_x, mass_x):
    num = jnp.sum(stiff_x * mass_x, axis=0, keepdims=True)
    den = jnp.sum(mass_x * mass_x, axis=0, keepdims=True)
    rest = stiff_x - (num / jnp.maximum(den, tiny)) * mass_x
    return num, den, jnp.sum(rest * rest, axis=0, keepdims=True)


def shift_and_scale(stats, total_rows):
    num, den, about = stats[0:1, :], stats[1:2, :], stats[2:3, :]
    shift = num / (den + epsilon)
    off = shift - num / jnp.maximum(den, tiny)
    scale = lax.rsqrt((about + off * off * den) / total_rows + epsilon)
    return shift, scale


def hbm():
    return pl.BlockSpec(memory_space=pltpu.HBM)


def pack_kernel(cols, stiff, mass, out_ref):
    rows, edge = stiff.shape
    out_ref[0:rows, :] = stiff[...]
    out_ref[rows : 2 * rows, :] = mass[...]
    lane = lax.broadcasted_iota(jnp.int32, (16, edge), 1)
    tag = jnp.zeros((16, edge), jnp.int32)
    for s in range(rows // edge):
        tag = jnp.where(lane == s, cols[0, s], tag)
    out_ref[2 * rows : 2 * rows + 16, :] = tag.astype(f32).astype(bf16)


def turn_kernel(current, coeffs, out_ref):
    out_ref[...] = jnp.dot(current[...], coeffs[0], preferred_element_type=f32).astype(bf16)


def stats_kernel(nz, slots, edge, cols, *refs):
    t_refs, km_refs = refs[:nz], refs[nz : 2 * nz]
    stats_ref, field, stiff, mass = refs[2 * nz :]
    z = lax.axis_index("blk")
    for k in range(nz):
        at = pl.ds(pl.multiple_of((z ^ k) * edge, edge), edge)
        field[at, :] = t_refs[k][:, : field.shape[1]]
    for k in range(nz):
        both = block_dot(km_refs[k], slots, edge, cols, k, field, slice(None))
        at = pl.ds(pl.multiple_of((z ^ k) * edge, edge), edge)
        stiff[at, :] = both[:edge]
        mass[at, :] = both[edge:]
    num, den, about = column_stats(stiff[...], mass[...])
    stats_ref[0:1, :] = num
    stats_ref[1:2, :] = den
    stats_ref[2:3, :] = about


def sweep_kernel(nz, slots, edge, modes, total_rows, cols, *refs):
    t_refs, km_refs = refs[:nz], refs[nz : 2 * nz]
    stats, coeffs, turned_ref, stiff_ref, mass_ref, stats_ref, full = refs[2 * nz :]
    z = lax.axis_index("blk")
    at = [pl.ds(pl.multiple_of((z ^ k) * edge, edge), edge) for k in range(nz)]
    for k in range(nz):
        full[at[k], 0:modes] = t_refs[k][:, :modes]
        full[at[k], 2 * modes : 3 * modes] = t_refs[k][:, modes:]
    shift, scale = shift_and_scale(stats, total_rows)
    for k in range(nz):
        both = block_dot(km_refs[k], slots, edge, cols, k, full, slice(0, modes))
        full[at[k], modes : 2 * modes] = ((both[:edge] - shift * both[edge:]) * scale).astype(bf16)
    turned_ref[...] = jnp.dot(full[...], coeffs[1], preferred_element_type=f32).astype(bf16)
    for k in range(nz):
        both = block_dot(km_refs[k], slots, edge, cols, k, turned_ref, slice(0, modes))
        stiff_ref[at[k], :] = both[:edge]
        mass_ref[at[k], :] = both[edge:]
    num, den, about = column_stats(stiff_ref[...], mass_ref[...])
    stats_ref[0:1, :] = num
    stats_ref[1:2, :] = den
    stats_ref[2:3, :] = about


def gram_kernel(nz, ng, slots, edge, modes, total_rows, split, cols, *refs):
    km_refs = refs[:nz]
    turned, stiff, mass, stats, basis_ref, ritz_ref, gram_ref, send_ref, full, chosen, applied = refs[nz:]
    z, g = lax.axis_index("blk"), lax.axis_index("grp")
    core, chip = lax.rem(g, 2), lax.div(g, 2)
    at = [pl.ds(pl.multiple_of((z ^ k) * edge, edge), edge) for k in range(nz)]
    width = 3 * modes // nz
    shift, scale = shift_and_scale(stats, total_rows)
    ritz_ref[...] = shift
    full[:, 0:modes] = turned[:, 0:modes]
    full[:, modes : 2 * modes] = ((stiff[...] - shift * mass[...]) * scale).astype(bf16)
    full[:, 2 * modes : 3 * modes] = turned[:, modes : 2 * modes]
    basis_ref[...] = full[at[0], :]
    window = chosen.shape[1]
    start = z * width // 128 * 128
    picked = full[:, pl.ds(pl.multiple_of(start, 128), window)].astype(f32)
    chosen[...] = pltpu.roll(picked, window - (z * width - start), 1).astype(bf16)
    for k in range(nz):
        both = block_dot(km_refs[k], slots, edge, cols, k, chosen, slice(0, width)).astype(bf16)
        applied[at[k], 0:width] = both[:edge]
        applied[at[k], width : 2 * width] = both[edge:]
    gram = lax.dot_general(
        full[...], applied[...], (((0,), (0,)), ((), ())), preferred_element_type=f32
    ).astype(bf16)
    if split:
        rows = 3 * modes // ng
        for q in range(ng):
            piece = gram[q * rows : (q + 1) * rows]

            @pl.when(core == q % 2)
            def _():
                gram_ref[(q // 2) ^ chip] = piece

            @pl.when(core != q % 2)
            def _():
                send_ref[(q // 2) ^ chip] = piece
    else:
        gram_ref[...] = gram


def call(kernel, inputs, n_smem, out_shape, scratch, flops):
    return pl.pallas_call(
        kernel,
        out_shape=out_shape,
        in_specs=[smem()] * n_smem + [vmem()] * (len(inputs) - n_smem),
        out_specs=jax.tree.map(lambda _: vmem(), out_shape),
        scratch_shapes=scratch,
        compiler_params=pltpu.CompilerParams(vmem_limit_bytes=VMEM_BYTES),
        cost_estimate=pl.CostEstimate(flops=flops, bytes_accessed=4_000_000, transcendentals=0),
    )(*inputs)


def by_xor(size, k):
    return [(i, i ^ k) for i in range(size)]


def merge(one, two):
    num, den = one[0] + two[0], one[1] + two[1]
    apart = one[0] / jnp.maximum(one[1], tiny) - two[0] / jnp.maximum(two[1], tiny)
    weight = jnp.sqrt(one[1]) * jnp.sqrt(two[1]) * lax.rsqrt(jnp.maximum(den, tiny))
    gap = apart * weight
    return jnp.stack([num, den, (one[2] + two[2]) + gap * gap])


def merge_over(axis, size, stats):
    step = 1
    if axis == "grp" and size >= 8:
        stats = merge(stats, lax.ppermute(stats, axis, by_xor(size, 1)))
        step = 2
        if size == 8:
            got = [lax.ppermute(stats, axis, by_xor(size, 2 * k)) for k in (1, 2, 3)]
            return merge(merge(stats, got[0]), merge(got[1], got[2]))
    while step < size:
        stats = merge(stats, lax.ppermute(stats, axis, by_xor(size, step)))
        step *= 2
    return stats


def hold_kernel(*refs):
    pass


def hold(arrays, until):
    anywhere = pl.BlockSpec(memory_space=pl.ANY)
    return pl.pallas_call(
        hold_kernel,
        out_shape=tuple(jax.ShapeDtypeStruct(a.shape, a.dtype) for a in arrays),
        in_specs=[anywhere] * (len(arrays) + len(until)),
        out_specs=(anywhere,) * len(arrays),
        input_output_aliases={i: i for i in range(len(arrays))},
        compiler_params=pltpu.CompilerParams(vmem_limit_bytes=1024 * 1024),
        cost_estimate=pl.CostEstimate(flops=0, bytes_accessed=0, transcendentals=0),
    )(*arrays, *until)


def gather(arrays, nz):
    far = nz // 2

    def send(held, step):
        return tuple(lax.ppermute(a, "blk", by_xor(nz, step)) for a in held)

    parts = {0: tuple(arrays)}
    if nz == 4:
        parts[2], parts[1] = send(arrays, 2), send(arrays, 1)
        parts[2] = hold(parts[2], parts[1])
        parts[3] = send(parts[2], 1)
    else:
        while far:
            parts |= {k ^ far: send(held, far) for k, held in parts.items()}
            far //= 2
    return [[parts[k][i] for k in range(nz)] for i in range(len(arrays))]


def body(basis, coeffs, stiff_blocks, mass_blocks, block_cols):
    nz, ng = lax.axis_size("blk"), lax.axis_size("grp")
    current = basis[0]
    edge, columns = current.shape
    slots = block_cols.shape[-1]
    modes = columns // 3
    rows = edge * nz
    total_rows = rows * ng
    width = columns // nz

    payload = call(
        pack_kernel,
        [
            block_cols[0],
            stiff_blocks[0, 0].reshape(slots * edge, edge),
            mass_blocks[0, 0].reshape(slots * edge, edge),
        ],
        1,
        jax.ShapeDtypeStruct((2 * slots * edge + 16, edge), bf16),
        [],
        0,
    )
    turned = call(
        turn_kernel,
        [current, coeffs],
        0,
        jax.ShapeDtypeStruct((edge, 2 * modes), bf16),
        [],
        2 * edge * columns * 2 * modes,
    )
    km_parts, t_parts = gather((payload, turned), nz)

    cols = jnp.stack([p[2 * slots * edge, :slots] for p in km_parts]).astype(jnp.int32)
    stats = call(
        functools.partial(stats_kernel, nz, slots, edge),
        [cols, *t_parts, *km_parts],
        1,
        jax.ShapeDtypeStruct((3, modes), f32),
        [
            pltpu.VMEM((rows, modes), bf16),
            pltpu.VMEM((rows, modes), f32),
            pltpu.VMEM((rows, modes), f32),
        ],
        4 * edge * slots * edge * modes,
    )
    stats = merge_over("grp", ng, stats)

    turned, stiff_x, mass_x, stats = call(
        functools.partial(sweep_kernel, nz, slots, edge, modes, total_rows),
        [cols, *t_parts, *km_parts, stats, coeffs],
        1,
        (
            jax.ShapeDtypeStruct((rows, 2 * modes), bf16),
            jax.ShapeDtypeStruct((rows, modes), f32),
            jax.ShapeDtypeStruct((rows, modes), f32),
            jax.ShapeDtypeStruct((3, modes), f32),
        ),
        [pltpu.VMEM((rows, columns), bf16)],
        2 * rows * columns * 2 * modes,
    )
    stats = merge_over("grp", ng, stats)

    split = (columns // ng) % 16 == 0
    chips = ng // 2
    block = columns // ng
    gram_shape = (chips, block, 2 * width) if split else (columns, 2 * width)
    window = -(-(width + max(i * width % 128 for i in range(nz))) // 128) * 128
    basis_out, ritz, gram, send = call(
        functools.partial(gram_kernel, nz, ng, slots, edge, modes, total_rows, split),
        [cols, *km_parts, turned, stiff_x, mass_x, stats],
        1,
        (
            jax.ShapeDtypeStruct((edge, columns), bf16),
            jax.ShapeDtypeStruct((1, modes), f32),
            jax.ShapeDtypeStruct(gram_shape, bf16),
            jax.ShapeDtypeStruct(gram_shape, bf16),
        ),
        [
            pltpu.VMEM((rows, columns), bf16),
            pltpu.VMEM((rows, window), bf16),
            pltpu.VMEM((rows, 2 * width), bf16),
        ],
        2 * rows * columns * 2 * width,
    )
    if split:
        got = lax.ppermute(send, "grp", by_xor(ng, 1))
        mine = (gram.astype(f32) + got.astype(f32)).astype(bf16)
        total = mine[0].astype(f32)
        for k in range(1, chips):
            total = total + lax.ppermute(mine[k], "grp", by_xor(ng, 2 * k)).astype(f32)
    else:
        total = lax.psum_scatter(gram, "grp", scatter_dimension=0, tiled=True).astype(f32)
    return (basis_out[None], ritz[0], total.reshape(block, 2, width))


def solution(mesh):
    in_specs = (
        P("grp", "blk", None),
        P(),
        P("grp", "blk", None, None, None),
        P("grp", "blk", None, None, None),
        P("grp", "blk", None),
    )
    out_specs = (P("grp", "blk", None), P(), P("grp", None, "blk"))
    return jax.shard_map(body, mesh=mesh, in_specs=in_specs, out_specs=out_specs, check_vma=False)
```

```python
import functools

import jax
import jax.numpy as jnp
from jax import lax
from jax.experimental import pallas as pl
from jax.experimental.pallas import tpu as pltpu
from jax.sharding import PartitionSpec as P

epsilon = 1e-06
tiny = 1e-30
f32 = jnp.float32
bf16 = jnp.bfloat16
VMEM_BYTES = 24 * 1024 * 1024


def vmem():
    return pl.BlockSpec(memory_space=pltpu.VMEM)


def smem():
    return pl.BlockSpec(memory_space=pltpu.SMEM)


def block_dot(pieces_k, slots, edge, cols, k, field, lanes):
    half = slots * edge
    top = jnp.concatenate([pieces_k[s * edge : (s + 1) * edge, :] for s in range(slots)], axis=1)
    low = jnp.concatenate(
        [pieces_k[half + s * edge : half + (s + 1) * edge, :] for s in range(slots)], axis=1
    )
    rows = [
        field[pl.ds(pl.multiple_of(cols[k, s] * edge, edge), edge), lanes] for s in range(slots)
    ]
    return jnp.dot(
        jnp.concatenate([top, low], axis=0),
        jnp.concatenate(rows, axis=0),
        preferred_element_type=f32,
    )


def column_stats(stiff_x, mass_x):
    num = jnp.sum(stiff_x * mass_x, axis=0, keepdims=True)
    den = jnp.sum(mass_x * mass_x, axis=0, keepdims=True)
    rest = stiff_x - (num / jnp.maximum(den, tiny)) * mass_x
    return num, den, jnp.sum(rest * rest, axis=0, keepdims=True)


def shift_and_scale(stats, total_rows):
    num, den, about = stats[0:1, :], stats[1:2, :], stats[2:3, :]
    shift = num / (den + epsilon)
    off = shift - num / jnp.maximum(den, tiny)
    scale = lax.rsqrt((about + off * off * den) / total_rows + epsilon)
    return shift, scale


def block_dot(pieces_k, slots, edge, cols, k, field, lanes):
    half = slots * edge
    top = jnp.concatenate([pieces_k[s * edge : (s + 1) * edge, :] for s in range(slots)], axis=1)
    low = jnp.concatenate(
        [pieces_k[half + s * edge : half + (s + 1) * edge, :] for s in range(slots)], axis=1
    )
    rows = [
        field[pl.ds(pl.multiple_of(cols[k, s] * edge, edge), edge), lanes] for s in range(slots)
    ]
    return jnp.dot(
        jnp.concatenate([top, low], axis=0),
        jnp.concatenate(rows, axis=0),
        preferred_element_type=f32,
    )


def column_stats(stiff_x, mass_x):
    num = jnp.sum(stiff_x * mass_x, axis=0, keepdims=True)
    den = jnp.sum(mass_x * mass_x, axis=0, keepdims=True)
    rest = stiff_x - (num / jnp.maximum(den, tiny)) * mass_x
    return num, den, jnp.sum(rest * rest, axis=0, keepdims=True)


def shift_and_scale(stats, total_rows):
    num, den, about = stats[0:1, :], stats[1:2, :], stats[2:3, :]
    shift = num / (den + epsilon)
    off = shift - num / jnp.maximum(den, tiny)
    scale = lax.rsqrt((about + off * off * den) / total_rows + epsilon)
    return shift, scale


def hbm():
    return pl.BlockSpec(memory_space=pltpu.HBM)


def turn_kernel(modes, cols, current, coeffs, out_ref):
    rows, columns = out_ref.shape[0] - 16, out_ref.shape[1]
    lane = lax.broadcasted_iota(jnp.int32, (16, columns), 1)
    tag = jnp.zeros((16, columns), jnp.int32)
    for s in range(cols.shape[1]):
        tag = jnp.where(lane == s, cols[0, s], tag)
    out_ref[rows : rows + 16, :] = tag.astype(f32).astype(bf16)
    out_ref[0:rows, :] = jnp.dot(current[...], coeffs[0], preferred_element_type=f32).astype(bf16)


def stats_kernel(nz, slots, edge, cols, *refs):
    t_refs, km_refs = refs[:nz], refs[nz : 2 * nz]
    stats_ref, field, stiff, mass = refs[2 * nz :]
    z = lax.axis_index("blk")
    for k in range(nz):
        at = pl.ds(pl.multiple_of((z ^ k) * edge, edge), edge)
        field[at, :] = t_refs[k][:edge, : field.shape[1]]
    for k in range(nz):
        both = block_dot(km_refs[k], slots, edge, cols, k, field, slice(None))
        at = pl.ds(pl.multiple_of((z ^ k) * edge, edge), edge)
        stiff[at, :] = both[:edge]
        mass[at, :] = both[edge:]
    num, den, about = column_stats(stiff[...], mass[...])
    stats_ref[0:1, :] = num
    stats_ref[1:2, :] = den
    stats_ref[2:3, :] = about


def sweep_kernel(nz, slots, edge, modes, total_rows, cols, *refs):
    t_refs, km_refs = refs[:nz], refs[nz : 2 * nz]
    stats, coeffs, turned_ref, stiff_ref, mass_ref, stats_ref, full = refs[2 * nz :]
    z = lax.axis_index("blk")
    at = [pl.ds(pl.multiple_of((z ^ k) * edge, edge), edge) for k in range(nz)]
    for k in range(nz):
        full[at[k], 0:modes] = t_refs[k][:edge, :modes]
        full[at[k], 2 * modes : 3 * modes] = t_refs[k][:edge, modes:]
    shift, scale = shift_and_scale(stats, total_rows)
    for k in range(nz):
        both = block_dot(km_refs[k], slots, edge, cols, k, full, slice(0, modes))
        full[at[k], modes : 2 * modes] = ((both[:edge] - shift * both[edge:]) * scale).astype(bf16)
    turned_ref[...] = jnp.dot(full[...], coeffs[1], preferred_element_type=f32).astype(bf16)
    for k in range(nz):
        both = block_dot(km_refs[k], slots, edge, cols, k, turned_ref, slice(0, modes))
        stiff_ref[at[k], :] = both[:edge]
        mass_ref[at[k], :] = both[edge:]
    num, den, about = column_stats(stiff_ref[...], mass_ref[...])
    stats_ref[0:1, :] = num
    stats_ref[1:2, :] = den
    stats_ref[2:3, :] = about


def gram_kernel(nz, ng, slots, edge, modes, total_rows, split, cols, *refs):
    km_refs = refs[:nz]
    turned, stiff, mass, stats, basis_ref, ritz_ref, gram_ref, send_ref, full, chosen, applied = refs[nz:]
    z, g = lax.axis_index("blk"), lax.axis_index("grp")
    core, chip = lax.rem(g, 2), lax.div(g, 2)
    at = [pl.ds(pl.multiple_of((z ^ k) * edge, edge), edge) for k in range(nz)]
    width = 3 * modes // nz
    shift, scale = shift_and_scale(stats, total_rows)
    ritz_ref[...] = shift
    full[:, 0:modes] = turned[:, 0:modes]
    full[:, modes : 2 * modes] = ((stiff[...] - shift * mass[...]) * scale).astype(bf16)
    full[:, 2 * modes : 3 * modes] = turned[:, modes : 2 * modes]
    basis_ref[...] = full[at[0], :]
    window = chosen.shape[1]
    start = z * width // 128 * 128
    picked = full[:, pl.ds(pl.multiple_of(start, 128), window)].astype(f32)
    chosen[...] = pltpu.roll(picked, window - (z * width - start), 1).astype(bf16)
    for k in range(nz):
        both = block_dot(km_refs[k], slots, edge, cols, k, chosen, slice(0, width)).astype(bf16)
        applied[at[k], 0:width] = both[:edge]
        applied[at[k], width : 2 * width] = both[edge:]
    gram = lax.dot_general(
        full[...], applied[...], (((0,), (0,)), ((), ())), preferred_element_type=f32
    ).astype(bf16)
    if split:
        rows = 3 * modes // ng
        for q in range(ng):
            piece = gram[q * rows : (q + 1) * rows]

            @pl.when(core == q % 2)
            def _():
                gram_ref[(q // 2) ^ chip] = piece

            @pl.when(core != q % 2)
            def _():
                send_ref[(q // 2) ^ chip] = piece
    else:
        gram_ref[...] = gram


def call(kernel, inputs, n_smem, out_shape, scratch, flops):
    return pl.pallas_call(
        kernel,
        out_shape=out_shape,
        in_specs=[smem()] * n_smem + [vmem()] * (len(inputs) - n_smem),
        out_specs=jax.tree.map(lambda _: vmem(), out_shape),
        scratch_shapes=scratch,
        compiler_params=pltpu.CompilerParams(vmem_limit_bytes=VMEM_BYTES),
        cost_estimate=pl.CostEstimate(flops=flops, bytes_accessed=4_000_000, transcendentals=0),
    )(*inputs)


def by_xor(size, k):
    return [(i, i ^ k) for i in range(size)]


def merge(one, two):
    num, den = one[0] + two[0], one[1] + two[1]
    apart = one[0] / jnp.maximum(one[1], tiny) - two[0] / jnp.maximum(two[1], tiny)
    weight = jnp.sqrt(one[1]) * jnp.sqrt(two[1]) * lax.rsqrt(jnp.maximum(den, tiny))
    gap = apart * weight
    return jnp.stack([num, den, (one[2] + two[2]) + gap * gap])


def merge_over(axis, size, stats):
    step = 1
    if axis == "grp" and size >= 8:
        stats = merge(stats, lax.ppermute(stats, axis, by_xor(size, 1)))
        step = 2
        if size == 8:
            got = [lax.ppermute(stats, axis, by_xor(size, 2 * k)) for k in (1, 2, 3)]
            return merge(merge(stats, got[0]), merge(got[1], got[2]))
    while step < size:
        stats = merge(stats, lax.ppermute(stats, axis, by_xor(size, step)))
        step *= 2
    return stats


def hold_kernel(*refs):
    pass


def hold(arrays, until):
    anywhere = pl.BlockSpec(memory_space=pl.ANY)
    return pl.pallas_call(
        hold_kernel,
        out_shape=tuple(jax.ShapeDtypeStruct(a.shape, a.dtype) for a in arrays),
        in_specs=[anywhere] * (len(arrays) + len(until)),
        out_specs=(anywhere,) * len(arrays),
        input_output_aliases={i: i for i in range(len(arrays))},
        compiler_params=pltpu.CompilerParams(vmem_limit_bytes=1024 * 1024),
        cost_estimate=pl.CostEstimate(flops=0, bytes_accessed=0, transcendentals=0),
    )(*arrays, *until)


def gather(arrays, nz):
    far = nz // 2

    def send(held, step):
        return tuple(lax.ppermute(a, "blk", by_xor(nz, step)) for a in held)

    parts = {0: tuple(arrays)}
    if nz == 4:
        parts[2], parts[1] = send(arrays, 2), send(arrays, 1)
        parts[2] = hold(parts[2], parts[1])
        parts[3] = send(parts[2], 1)
    else:
        while far:
            parts |= {k ^ far: send(held, far) for k, held in parts.items()}
            far //= 2
    return [[parts[k][i] for k in range(nz)] for i in range(len(arrays))]


def body(basis, coeffs, stiff_blocks, mass_blocks, block_cols):
    nz, ng = lax.axis_size("blk"), lax.axis_size("grp")
    current = basis[0]
    edge, columns = current.shape
    slots = block_cols.shape[-1]
    modes = columns // 3
    rows = edge * nz
    total_rows = rows * ng
    width = columns // nz

    payload = jnp.concatenate(
        [
            stiff_blocks[0, 0].reshape(slots * edge, edge),
            mass_blocks[0, 0].reshape(slots * edge, edge),
        ],
        axis=0,
    )
    turned = call(
        functools.partial(turn_kernel, modes),
        [block_cols[0], current, coeffs],
        1,
        jax.ShapeDtypeStruct((edge + 16, 2 * modes), bf16),
        [],
        2 * edge * columns * 2 * modes,
    )
    km_parts, t_parts = gather((payload, turned), nz)

    cols = jnp.stack([p[edge, :slots] for p in t_parts]).astype(jnp.int32)
    stats = call(
        functools.partial(stats_kernel, nz, slots, edge),
        [cols, *t_parts, *km_parts],
        1,
        jax.ShapeDtypeStruct((3, modes), f32),
        [
            pltpu.VMEM((rows, modes), bf16),
            pltpu.VMEM((rows, modes), f32),
            pltpu.VMEM((rows, modes), f32),
        ],
        4 * edge * slots * edge * modes,
    )
    stats = merge_over("grp", ng, stats)

    turned, stiff_x, mass_x, stats = call(
        functools.partial(sweep_kernel, nz, slots, edge, modes, total_rows),
        [cols, *t_parts, *km_parts, stats, coeffs],
        1,
        (
            jax.ShapeDtypeStruct((rows, 2 * modes), bf16),
            jax.ShapeDtypeStruct((rows, modes), f32),
            jax.ShapeDtypeStruct((rows, modes), f32),
            jax.ShapeDtypeStruct((3, modes), f32),
        ),
        [pltpu.VMEM((rows, columns), bf16)],
        2 * rows * columns * 2 * modes,
    )
    stats = merge_over("grp", ng, stats)

    split = (columns // ng) % 16 == 0
    chips = ng // 2
    block = columns // ng
    gram_shape = (chips, block, 2 * width) if split else (columns, 2 * width)
    window = -(-(width + max(i * width % 128 for i in range(nz))) // 128) * 128
    basis_out, ritz, gram, send = call(
        functools.partial(gram_kernel, nz, ng, slots, edge, modes, total_rows, split),
        [cols, *km_parts, turned, stiff_x, mass_x, stats],
        1,
        (
            jax.ShapeDtypeStruct((edge, columns), bf16),
            jax.ShapeDtypeStruct((1, modes), f32),
            jax.ShapeDtypeStruct(gram_shape, bf16),
            jax.ShapeDtypeStruct(gram_shape, bf16),
        ),
        [
            pltpu.VMEM((rows, columns), bf16),
            pltpu.VMEM((rows, window), bf16),
            pltpu.VMEM((rows, 2 * width), bf16),
        ],
        2 * rows * columns * 2 * width,
    )
    if split:
        got = lax.ppermute(send, "grp", by_xor(ng, 1))
        mine = (gram.astype(f32) + got.astype(f32)).astype(bf16)
        total = mine[0].astype(f32)
        for k in range(1, chips):
            total = total + lax.ppermute(mine[k], "grp", by_xor(ng, 2 * k)).astype(f32)
    else:
        total = lax.psum_scatter(gram, "grp", scatter_dimension=0, tiled=True).astype(f32)
    return (basis_out[None], ritz[0], total.reshape(block, 2, width))


def solution(mesh):
    in_specs = (
        P("grp", "blk", None),
        P(),
        P("grp", "blk", None, None, None),
        P("grp", "blk", None, None, None),
        P("grp", "blk", None),
    )
    out_specs = (P("grp", "blk", None), P(), P("grp", None, "blk"))
    return jax.shard_map(body, mesh=mesh, in_specs=in_specs, out_specs=out_specs, check_vma=False)
```

```python
import functools

import jax
import jax.numpy as jnp
from jax import lax
from jax.experimental import pallas as pl
from jax.experimental.pallas import tpu as pltpu
from jax.sharding import PartitionSpec as P

epsilon = 1e-06
tiny = 1e-30
f32 = jnp.float32
bf16 = jnp.bfloat16
VMEM_BYTES = 24 * 1024 * 1024


def vmem():
    return pl.BlockSpec(memory_space=pltpu.VMEM)


def smem():
    return pl.BlockSpec(memory_space=pltpu.SMEM)


def block_dot(pieces_k, slots, edge, cols, k, field, lanes):
    half = slots * edge
    top = jnp.concatenate([pieces_k[s * edge : (s + 1) * edge, :] for s in range(slots)], axis=1)
    low = jnp.concatenate(
        [pieces_k[half + s * edge : half + (s + 1) * edge, :] for s in range(slots)], axis=1
    )
    rows = [
        field[pl.ds(pl.multiple_of(cols[k, s] * edge, edge), edge), lanes] for s in range(slots)
    ]
    return jnp.dot(
        jnp.concatenate([top, low], axis=0),
        jnp.concatenate(rows, axis=0),
        preferred_element_type=f32,
    )


def shift_and_scale(stats, total_rows):
    num, den, about = stats[0:1, :], stats[1:2, :], stats[2:3, :]
    shift = num / (den + epsilon)
    off = shift - num / jnp.maximum(den, tiny)
    scale = lax.rsqrt((about + off * off * den) / total_rows + epsilon)
    return shift, scale


def block_dot(pieces_k, slots, edge, cols, k, field, lanes):
    half = slots * edge
    top = jnp.concatenate([pieces_k[s * edge : (s + 1) * edge, :] for s in range(slots)], axis=1)
    low = jnp.concatenate(
        [pieces_k[half + s * edge : half + (s + 1) * edge, :] for s in range(slots)], axis=1
    )
    rows = [
        field[pl.ds(pl.multiple_of(cols[k, s] * edge, edge), edge), lanes] for s in range(slots)
    ]
    return jnp.dot(
        jnp.concatenate([top, low], axis=0),
        jnp.concatenate(rows, axis=0),
        preferred_element_type=f32,
    )


def column_stats(stiff_x, mass_x):
    num = jnp.sum(stiff_x * mass_x, axis=0, keepdims=True)
    den = jnp.sum(mass_x * mass_x, axis=0, keepdims=True)
    rest = stiff_x - (num / jnp.maximum(den, tiny)) * mass_x
    return num, den, jnp.sum(rest * rest, axis=0, keepdims=True)


def shift_and_scale(stats, total_rows):
    num, den, about = stats[0:1, :], stats[1:2, :], stats[2:3, :]
    shift = num / (den + epsilon)
    off = shift - num / jnp.maximum(den, tiny)
    scale = lax.rsqrt((about + off * off * den) / total_rows + epsilon)
    return shift, scale


def hbm():
    return pl.BlockSpec(memory_space=pltpu.HBM)


def turn_kernel(modes, cols, current, coeffs, out_ref):
    rows, columns = out_ref.shape[0] - 16, out_ref.shape[1]
    lane = lax.broadcasted_iota(jnp.int32, (16, columns), 1)
    tag = jnp.zeros((16, columns), jnp.int32)
    for s in range(cols.shape[1]):
        tag = jnp.where(lane == s, cols[0, s], tag)
    out_ref[rows : rows + 16, :] = tag.astype(f32).astype(bf16)
    out_ref[0:rows, :] = jnp.dot(current[...], coeffs[0], preferred_element_type=f32).astype(bf16)


def rows_kernel(nz, slots, edge, modes, cols, *refs):
    t_refs, km_refs = refs[:nz], refs[nz : 2 * nz - 1]
    placed, stiff_ref, mass_ref = refs[2 * nz - 1 :]
    z = lax.axis_index("blk")
    for k in range(nz):
        placed[pl.ds(pl.multiple_of((z ^ k) * edge, edge), edge), :] = t_refs[k][:edge, :]
    for k in range(nz - 1):
        both = block_dot(km_refs[k], slots, edge, cols, k, placed, slice(0, modes))
        stiff_ref[k] = both[:edge]
        mass_ref[k] = both[edge:]


def block_stats(z, pairs, sums, stats_ref):
    for k, (stiff_x, mass_x) in enumerate(pairs):
        sums[z ^ k, 0:1, :] = jnp.sum(stiff_x * mass_x, axis=0, keepdims=True)
        sums[z ^ k, 1:2, :] = jnp.sum(mass_x * mass_x, axis=0, keepdims=True)
    total = sums[0]
    for r in range(1, len(pairs)):
        total = total + sums[r]
    own_shift = total[0:1, :] / jnp.maximum(total[1:2, :], tiny)
    for k, (stiff_x, mass_x) in enumerate(pairs):
        rest = stiff_x - own_shift * mass_x
        sums[z ^ k, 2:3, :] = jnp.sum(rest * rest, axis=0, keepdims=True)
    about = sums[0, 2:3, :]
    for r in range(1, len(pairs)):
        about = about + sums[r, 2:3, :]
    stats_ref[0:2, :] = total[0:2, :]
    stats_ref[2:3, :] = about


def stats_kernel(nz, slots, edge, modes, cols, km_last, placed, stiff, mass, stiff_ref, mass_ref, stats_ref, sums):
    z = lax.axis_index("blk")
    both = block_dot(km_last, slots, edge, cols, nz - 1, placed, slice(0, modes))
    stiff_ref[...] = both[:edge]
    mass_ref[...] = both[edge:]
    pairs = [(stiff[k], mass[k]) for k in range(nz - 1)] + [(both[:edge], both[edge:])]
    sums[...] = jnp.zeros_like(sums)
    block_stats(z, pairs, sums, stats_ref)


def early_turn_kernel(modes, placed, coeffs, out_ref):
    out_ref[...] = jnp.dot(
        placed[:, :modes], coeffs[1, :modes, :], preferred_element_type=f32
    ) + jnp.dot(placed[:, modes:], coeffs[1, 2 * modes :, :], preferred_element_type=f32)


def sweep_kernel(nz, slots, edge, modes, total_rows, cols, *refs):
    km_refs = refs[:nz]
    early, stiff, mass, stiff_last, mass_last, stats, coeffs = refs[nz : nz + 7]
    turned_ref, stiff_ref, mass_ref, stats_ref, search, sums = refs[nz + 7 :]
    z = lax.axis_index("blk")
    at = [pl.ds(pl.multiple_of((z ^ k) * edge, edge), edge) for k in range(nz)]
    shift, scale = shift_and_scale(stats, total_rows)
    for k in range(nz):
        stiff_x = stiff[k] if k < nz - 1 else stiff_last[...]
        mass_x = mass[k] if k < nz - 1 else mass_last[...]
        search[at[k], :] = ((stiff_x - shift * mass_x) * scale).astype(bf16)
    late = jnp.dot(search[...], coeffs[1, modes : 2 * modes, :], preferred_element_type=f32)
    turned_ref[...] = (early[...] + late).astype(bf16)
    pairs = []
    for k in range(nz):
        both = block_dot(km_refs[k], slots, edge, cols, k, turned_ref, slice(0, modes))
        stiff_ref[at[k], :] = both[:edge]
        mass_ref[at[k], :] = both[edge:]
        pairs.append((both[:edge], both[edge:]))
    sums[...] = jnp.zeros_like(sums)
    block_stats(z, pairs, sums, stats_ref)


def gram_rows(full_t, applied, chips, core, out_ref):
    chip = lax.div(lax.axis_index("grp"), 2)
    block = full_t.shape[0] // (2 * chips)
    rows = [
        full_t[pl.ds(pl.multiple_of((2 * j + core) * block, 16), block), :] for j in range(chips)
    ]
    gram = jnp.dot(jnp.concatenate(rows, axis=0), applied[...], preferred_element_type=f32)
    gram = gram.astype(bf16)
    for j in range(chips):
        out_ref[j ^ chip] = gram[j * block : (j + 1) * block]


def gram_kernel(nz, chips, slots, edge, modes, total_rows, split, cols, *refs):
    km_refs = refs[:nz]
    turned, stiff, mass, stats = refs[nz : nz + 4]
    basis_ref, ritz_ref, gram_ref, full_t, applied, full, chosen = refs[nz + 4 :]
    z = lax.axis_index("blk")
    at = [pl.ds(pl.multiple_of((z ^ k) * edge, edge), edge) for k in range(nz)]
    width = 3 * modes // nz
    shift, scale = shift_and_scale(stats, total_rows)
    ritz_ref[...] = shift
    full[:, 0:modes] = turned[:, 0:modes]
    full[:, modes : 2 * modes] = ((stiff[...] - shift * mass[...]) * scale).astype(bf16)
    full[:, 2 * modes : 3 * modes] = turned[:, modes : 2 * modes]
    basis_ref[...] = full[at[0], :]
    window = chosen.shape[1]
    start = z * width // 128 * 128
    picked = full[:, pl.ds(pl.multiple_of(start, 128), window)].astype(f32)
    chosen[...] = pltpu.roll(picked, window - (z * width - start), 1).astype(bf16)
    for k in range(nz):
        both = block_dot(km_refs[k], slots, edge, cols, k, chosen, slice(0, width)).astype(bf16)
        applied[at[k], 0:width] = both[:edge]
        applied[at[k], width : 2 * width] = both[edge:]
    full_t[...] = full[...].T
    if split:
        gram_rows(full_t, applied, chips, 1 - lax.rem(lax.axis_index("grp"), 2), gram_ref)
    else:
        gram_ref[...] = jnp.dot(full_t[...], applied[...], preferred_element_type=f32).astype(bf16)


def gram_rest_kernel(chips, full_t, applied, gram_ref):
    gram_rows(full_t, applied, chips, lax.rem(lax.axis_index("grp"), 2), gram_ref)


def call(kernel, inputs, n_smem, out_shape, scratch, flops):
    return pl.pallas_call(
        kernel,
        out_shape=out_shape,
        in_specs=[smem()] * n_smem + [vmem()] * (len(inputs) - n_smem),
        out_specs=jax.tree.map(lambda _: vmem(), out_shape),
        scratch_shapes=scratch,
        compiler_params=pltpu.CompilerParams(vmem_limit_bytes=VMEM_BYTES),
        cost_estimate=pl.CostEstimate(flops=flops, bytes_accessed=4_000_000, transcendentals=0),
    )(*inputs)


def by_xor(size, k):
    return [(i, i ^ k) for i in range(size)]


def merge(one, two):
    num, den = one[0] + two[0], one[1] + two[1]
    apart = one[0] / jnp.maximum(one[1], tiny) - two[0] / jnp.maximum(two[1], tiny)
    weight = jnp.sqrt(one[1]) * jnp.sqrt(two[1]) * lax.rsqrt(jnp.maximum(den, tiny))
    gap = apart * weight
    return jnp.stack([num, den, (one[2] + two[2]) + gap * gap])


def merge_over(axis, size, stats):
    step = 1
    if axis == "grp" and size >= 8:
        stats = merge(stats, lax.ppermute(stats, axis, by_xor(size, 1)))
        step = 2
        if size == 8:
            got = [lax.ppermute(stats, axis, by_xor(size, 2 * k)) for k in (1, 2, 3)]
            return merge(merge(stats, got[0]), merge(got[1], got[2]))
    while step < size:
        stats = merge(stats, lax.ppermute(stats, axis, by_xor(size, step)))
        step *= 2
    return stats


def hold_kernel(*refs):
    pass


def hold(arrays, until):
    anywhere = pl.BlockSpec(memory_space=pl.ANY)
    return pl.pallas_call(
        hold_kernel,
        out_shape=tuple(jax.ShapeDtypeStruct(a.shape, a.dtype) for a in arrays),
        in_specs=[anywhere] * (len(arrays) + len(until)),
        out_specs=(anywhere,) * len(arrays),
        input_output_aliases={i: i for i in range(len(arrays))},
        compiler_params=pltpu.CompilerParams(vmem_limit_bytes=1024 * 1024),
        cost_estimate=pl.CostEstimate(flops=0, bytes_accessed=0, transcendentals=0),
    )(*arrays, *until)


def gather(arrays, nz):
    far = nz // 2

    def send(held, step):
        return tuple(lax.ppermute(a, "blk", by_xor(nz, step)) for a in held)

    parts = {0: tuple(arrays)}
    if nz == 4:
        parts[2], parts[1] = send(arrays, 2), send(arrays, 1)
        parts[2] = hold(parts[2], parts[1])
        parts[3] = send(parts[2], 1)
    else:
        while far:
            parts |= {k ^ far: send(held, far) for k, held in parts.items()}
            far //= 2
    return [[parts[k][i] for k in range(nz)] for i in range(len(arrays))]


def body(basis, coeffs, stiff_blocks, mass_blocks, block_cols):
    nz, ng = lax.axis_size("blk"), lax.axis_size("grp")
    current = basis[0]
    edge, columns = current.shape
    slots = block_cols.shape[-1]
    modes = columns // 3
    rows = edge * nz
    total_rows = rows * ng
    width = columns // nz

    payload = jnp.concatenate(
        [
            stiff_blocks[0, 0].reshape(slots * edge, edge),
            mass_blocks[0, 0].reshape(slots * edge, edge),
        ],
        axis=0,
    )
    turned = call(
        functools.partial(turn_kernel, modes),
        [block_cols[0], current, coeffs],
        1,
        jax.ShapeDtypeStruct((edge + 16, 2 * modes), bf16),
        [],
        2 * edge * columns * 2 * modes,
    )
    km_parts, t_parts = gather((payload, turned), nz)

    cols = jnp.stack([p[edge, :slots] for p in t_parts]).astype(jnp.int32)
    some = jax.ShapeDtypeStruct((nz - 1, edge, modes), f32)
    last = jax.ShapeDtypeStruct((edge, modes), f32)
    stats_shape = jax.ShapeDtypeStruct((3, modes), f32)
    work = 4 * edge * slots * edge * modes
    placed, stiff_some, mass_some = call(
        functools.partial(rows_kernel, nz, slots, edge, modes),
        [cols, *t_parts, *km_parts[:-1]],
        1,
        (jax.ShapeDtypeStruct((rows, 2 * modes), bf16), some, some),
        [],
        (nz - 1) * work,
    )
    stiff_last, mass_last, stats = call(
        functools.partial(stats_kernel, nz, slots, edge, modes),
        [cols, km_parts[-1], placed, stiff_some, mass_some],
        1,
        (last, last, stats_shape),
        [pltpu.VMEM((nz, 8, modes), f32)],
        work,
    )
    stats = merge_over("grp", ng, stats)
    early = call(
        functools.partial(early_turn_kernel, modes),
        [placed, coeffs],
        0,
        jax.ShapeDtypeStruct((rows, 2 * modes), f32),
        [],
        8 * rows * modes * modes,
    )
    turned, stiff_x, mass_x, stats = call(
        functools.partial(sweep_kernel, nz, slots, edge, modes, total_rows),
        [cols, *km_parts, early, stiff_some, mass_some, stiff_last, mass_last, stats, coeffs],
        1,
        (
            jax.ShapeDtypeStruct((rows, 2 * modes), bf16),
            jax.ShapeDtypeStruct((rows, modes), f32),
            jax.ShapeDtypeStruct((rows, modes), f32),
            stats_shape,
        ),
        [pltpu.VMEM((rows, modes), bf16), pltpu.VMEM((nz, 8, modes), f32)],
        4 * rows * modes * modes + nz * work,
    )
    stats = merge_over("grp", ng, stats)

    chips = ng // 2
    block = columns // ng
    split = block % 16 == 0
    gram_shape = jax.ShapeDtypeStruct(
        (chips, block, 2 * width) if split else (columns, 2 * width), bf16
    )
    window = -(-(width + max(i * width % 128 for i in range(nz))) // 128) * 128
    basis_out, ritz, gram, full_t, applied = call(
        functools.partial(gram_kernel, nz, chips, slots, edge, modes, total_rows, split),
        [cols, *km_parts, turned, stiff_x, mass_x, stats],
        1,
        (
            jax.ShapeDtypeStruct((edge, columns), bf16),
            jax.ShapeDtypeStruct((1, modes), f32),
            gram_shape,
            jax.ShapeDtypeStruct((columns, rows), bf16),
            jax.ShapeDtypeStruct((rows, 2 * width), bf16),
        ),
        [pltpu.VMEM((rows, columns), bf16), pltpu.VMEM((rows, window), bf16)],
        2 * rows * columns * width,
    )
    if split:
        got = lax.ppermute(gram, "grp", by_xor(ng, 1))
        keep = call(
            functools.partial(gram_rest_kernel, chips),
            [full_t, applied],
            0,
            gram_shape,
            [],
            2 * rows * columns * width,
        )
        mine = (keep.astype(f32) + got.astype(f32)).astype(bf16)
        total = mine[0].astype(f32)
        for k in range(1, chips):
            total = total + lax.ppermute(mine[k], "grp", by_xor(ng, 2 * k)).astype(f32)
    else:
        total = lax.psum_scatter(gram, "grp", scatter_dimension=0, tiled=True).astype(f32)
    return (basis_out[None], ritz[0], total.reshape(block, 2, width))


def solution(mesh):
    in_specs = (
        P("grp", "blk", None),
        P(),
        P("grp", "blk", None, None, None),
        P("grp", "blk", None, None, None),
        P("grp", "blk", None),
    )
    out_specs = (P("grp", "blk", None), P(), P("grp", None, "blk"))
    return jax.shard_map(body, mesh=mesh, in_specs=in_specs, out_specs=out_specs, check_vma=False)
```

```python
import functools

import jax
import jax.numpy as jnp
from jax import lax
from jax.experimental import pallas as pl
from jax.experimental.pallas import tpu as pltpu
from jax.sharding import PartitionSpec as P

epsilon = 1e-06
tiny = 1e-30
f32 = jnp.float32
bf16 = jnp.bfloat16
VMEM_BYTES = 24 * 1024 * 1024


def vmem():
    return pl.BlockSpec(memory_space=pltpu.VMEM)


def smem():
    return pl.BlockSpec(memory_space=pltpu.SMEM)


def block_dot(pieces_k, slots, edge, cols, k, field, lanes):
    half = slots * edge
    top = jnp.concatenate([pieces_k[s * edge : (s + 1) * edge, :] for s in range(slots)], axis=1)
    low = jnp.concatenate(
        [pieces_k[half + s * edge : half + (s + 1) * edge, :] for s in range(slots)], axis=1
    )
    rows = [
        field[pl.ds(pl.multiple_of(cols[k, s] * edge, edge), edge), lanes] for s in range(slots)
    ]
    return jnp.dot(
        jnp.concatenate([top, low], axis=0),
        jnp.concatenate(rows, axis=0),
        preferred_element_type=f32,
    )


def shift_and_scale(stats, total_rows):
    num, den, about = stats[0:1, :], stats[1:2, :], stats[2:3, :]
    shift = num / (den + epsilon)
    off = shift - num / jnp.maximum(den, tiny)
    scale = lax.rsqrt((about + off * off * den) / total_rows + epsilon)
    return shift, scale


def block_dot(pieces_k, slots, edge, cols, k, field, lanes):
    half = slots * edge
    top = jnp.concatenate([pieces_k[s * edge : (s + 1) * edge, :] for s in range(slots)], axis=1)
    low = jnp.concatenate(
        [pieces_k[half + s * edge : half + (s + 1) * edge, :] for s in range(slots)], axis=1
    )
    rows = [
        field[pl.ds(pl.multiple_of(cols[k, s] * edge, edge), edge), lanes] for s in range(slots)
    ]
    return jnp.dot(
        jnp.concatenate([top, low], axis=0),
        jnp.concatenate(rows, axis=0),
        preferred_element_type=f32,
    )


def column_stats(stiff_x, mass_x):
    num = jnp.sum(stiff_x * mass_x, axis=0, keepdims=True)
    den = jnp.sum(mass_x * mass_x, axis=0, keepdims=True)
    rest = stiff_x - (num / jnp.maximum(den, tiny)) * mass_x
    return num, den, jnp.sum(rest * rest, axis=0, keepdims=True)


def shift_and_scale(stats, total_rows):
    num, den, about = stats[0:1, :], stats[1:2, :], stats[2:3, :]
    shift = num / (den + epsilon)
    off = shift - num / jnp.maximum(den, tiny)
    scale = lax.rsqrt((about + off * off * den) / total_rows + epsilon)
    return shift, scale


def hbm():
    return pl.BlockSpec(memory_space=pltpu.HBM)


def turn_kernel(modes, cols, current, coeffs, out_ref):
    rows, columns = out_ref.shape[0] - 16, out_ref.shape[1]
    lane = lax.broadcasted_iota(jnp.int32, (16, columns), 1)
    tag = jnp.zeros((16, columns), jnp.int32)
    for s in range(cols.shape[1]):
        tag = jnp.where(lane == s, cols[0, s], tag)
    out_ref[rows : rows + 16, :] = tag.astype(f32).astype(bf16)
    out_ref[0:rows, :] = jnp.dot(current[...], coeffs[0], preferred_element_type=f32).astype(bf16)


def rows_kernel(nz, slots, edge, modes, cols, *refs):
    t_refs, km_refs = refs[:nz], refs[nz : 2 * nz - 1]
    placed, stiff_ref, mass_ref = refs[2 * nz - 1 :]
    z = lax.axis_index("blk")
    for k in range(nz):
        placed[pl.ds(pl.multiple_of((z ^ k) * edge, edge), edge), :] = t_refs[k][:edge, :]
    for k in range(nz - 1):
        both = block_dot(km_refs[k], slots, edge, cols, k, placed, slice(0, modes))
        stiff_ref[k] = both[:edge]
        mass_ref[k] = both[edge:]


def block_stats(z, pairs, sums, stats_ref):
    for k, (stiff_x, mass_x) in enumerate(pairs):
        sums[z ^ k, 0:1, :] = jnp.sum(stiff_x * mass_x, axis=0, keepdims=True)
        sums[z ^ k, 1:2, :] = jnp.sum(mass_x * mass_x, axis=0, keepdims=True)
    total = sums[0]
    for r in range(1, len(pairs)):
        total = total + sums[r]
    own_shift = total[0:1, :] / jnp.maximum(total[1:2, :], tiny)
    for k, (stiff_x, mass_x) in enumerate(pairs):
        rest = stiff_x - own_shift * mass_x
        sums[z ^ k, 2:3, :] = jnp.sum(rest * rest, axis=0, keepdims=True)
    about = sums[0, 2:3, :]
    for r in range(1, len(pairs)):
        about = about + sums[r, 2:3, :]
    stats_ref[0:2, :] = total[0:2, :]
    stats_ref[2:3, :] = about


def stats_kernel(nz, slots, edge, modes, cols, km_last, placed, stiff, mass, stiff_ref, mass_ref, stats_ref, sums):
    z = lax.axis_index("blk")
    both = block_dot(km_last, slots, edge, cols, nz - 1, placed, slice(0, modes))
    stiff_ref[...] = both[:edge]
    mass_ref[...] = both[edge:]
    pairs = [(stiff[k], mass[k]) for k in range(nz - 1)] + [(both[:edge], both[edge:])]
    sums[...] = jnp.zeros_like(sums)
    block_stats(z, pairs, sums, stats_ref)


def early_turn_kernel(modes, placed, coeffs, out_ref):
    out_ref[...] = jnp.dot(
        placed[:, :modes], coeffs[1, :modes, :], preferred_element_type=f32
    ) + jnp.dot(placed[:, modes:], coeffs[1, 2 * modes :, :], preferred_element_type=f32)


def sweep_kernel(nz, slots, edge, modes, total_rows, cols, *refs):
    km_refs = refs[:nz]
    early, stiff, mass, stiff_last, mass_last, stats, coeffs = refs[nz : nz + 7]
    turned_ref, stiff_ref, mass_ref, stats_ref, search, sums = refs[nz + 7 :]
    z = lax.axis_index("blk")
    at = [pl.ds(pl.multiple_of((z ^ k) * edge, edge), edge) for k in range(nz)]
    shift, scale = shift_and_scale(stats, total_rows)
    for k in range(nz):
        stiff_x = stiff[k] if k < nz - 1 else stiff_last[...]
        mass_x = mass[k] if k < nz - 1 else mass_last[...]
        search[at[k], :] = ((stiff_x - shift * mass_x) * scale).astype(bf16)
    late = jnp.dot(search[...], coeffs[1, modes : 2 * modes, :], preferred_element_type=f32)
    turned_ref[...] = (early[...] + late).astype(bf16)
    pairs = []
    for k in range(nz):
        both = block_dot(km_refs[k], slots, edge, cols, k, turned_ref, slice(0, modes))
        stiff_ref[at[k], :] = both[:edge]
        mass_ref[at[k], :] = both[edge:]
        pairs.append((both[:edge], both[edge:]))
    sums[...] = jnp.zeros_like(sums)
    block_stats(z, pairs, sums, stats_ref)


def gram_rows(full_t, applied, chips, core, out_ref):
    chip = lax.div(lax.axis_index("grp"), 2)
    block = full_t.shape[0] // (2 * chips)
    rows = [
        full_t[pl.ds(pl.multiple_of((2 * j + core) * block, 16), block), :] for j in range(chips)
    ]
    gram = jnp.dot(jnp.concatenate(rows, axis=0), applied[...], preferred_element_type=f32)
    gram = gram.astype(bf16)
    for j in range(chips):
        out_ref[j ^ chip] = gram[j * block : (j + 1) * block]


def gram_kernel(nz, chips, slots, edge, modes, total_rows, split, cols, *refs):
    km_refs = refs[:nz]
    turned, stiff, mass, stats = refs[nz : nz + 4]
    gram_ref, full, full_t, applied, chosen = refs[nz + 4 :]
    z = lax.axis_index("blk")
    at = [pl.ds(pl.multiple_of((z ^ k) * edge, edge), edge) for k in range(nz)]
    width = 3 * modes // nz
    shift, scale = shift_and_scale(stats, total_rows)
    full[:, 0:modes] = turned[:, 0:modes]
    full[:, modes : 2 * modes] = ((stiff[...] - shift * mass[...]) * scale).astype(bf16)
    full[:, 2 * modes : 3 * modes] = turned[:, modes : 2 * modes]
    window = chosen.shape[1]
    start = z * width // 128 * 128
    picked = full[:, pl.ds(pl.multiple_of(start, 128), window)].astype(f32)
    chosen[...] = pltpu.roll(picked, window - (z * width - start), 1).astype(bf16)
    for k in range(nz):
        both = block_dot(km_refs[k], slots, edge, cols, k, chosen, slice(0, width)).astype(bf16)
        applied[at[k], 0:width] = both[:edge]
        applied[at[k], width : 2 * width] = both[edge:]
    full_t[...] = full[...].T
    if split:
        gram_rows(full_t, applied, chips, 1 - lax.rem(lax.axis_index("grp"), 2), gram_ref)
    else:
        gram_ref[...] = jnp.dot(full_t[...], applied[...], preferred_element_type=f32).astype(bf16)


def results_kernel(edge, total_rows, stats, full, basis_ref, ritz_ref):
    z = lax.axis_index("blk")
    basis_ref[...] = full[pl.ds(pl.multiple_of(z * edge, edge), edge), :]
    ritz_ref[...] = shift_and_scale(stats, total_rows)[0]


def gram_rest_kernel(chips, full_t, applied, gram_ref):
    gram_rows(full_t, applied, chips, lax.rem(lax.axis_index("grp"), 2), gram_ref)


def call(kernel, inputs, n_smem, out_shape, scratch, flops):
    return pl.pallas_call(
        kernel,
        out_shape=out_shape,
        in_specs=[smem()] * n_smem + [vmem()] * (len(inputs) - n_smem),
        out_specs=jax.tree.map(lambda _: vmem(), out_shape),
        scratch_shapes=scratch,
        compiler_params=pltpu.CompilerParams(vmem_limit_bytes=VMEM_BYTES),
        cost_estimate=pl.CostEstimate(flops=flops, bytes_accessed=4_000_000, transcendentals=0),
    )(*inputs)


def by_xor(size, k):
    return [(i, i ^ k) for i in range(size)]


def merge(one, two):
    num, den = one[0] + two[0], one[1] + two[1]
    apart = one[0] / jnp.maximum(one[1], tiny) - two[0] / jnp.maximum(two[1], tiny)
    weight = jnp.sqrt(one[1]) * jnp.sqrt(two[1]) * lax.rsqrt(jnp.maximum(den, tiny))
    gap = apart * weight
    return jnp.stack([num, den, (one[2] + two[2]) + gap * gap])


def merge_over(axis, size, stats):
    step = 1
    if axis == "grp" and size >= 8:
        stats = merge(stats, lax.ppermute(stats, axis, by_xor(size, 1)))
        step = 2
        if size == 8:
            got = [lax.ppermute(stats, axis, by_xor(size, 2 * k)) for k in (1, 2, 3)]
            return merge(merge(stats, got[0]), merge(got[1], got[2]))
    while step < size:
        stats = merge(stats, lax.ppermute(stats, axis, by_xor(size, step)))
        step *= 2
    return stats


def gather(operators, turned, nz):
    def send(x, step):
        return lax.ppermute(x, "blk", by_xor(nz, step))

    if nz == 4:
        km_2, km_1 = send(operators, 2), send(operators, 1)
        t_3, t_2, t_1 = send(turned, 3), send(turned, 2), send(turned, 1)
        return [operators, km_1, km_2, send(km_2, 1)], [turned, t_1, t_2, t_3]
    parts, far = {0: (operators, turned)}, nz // 2
    while far:
        parts |= {k ^ far: tuple(send(x, far) for x in held) for k, held in parts.items()}
        far //= 2
    return [[parts[k][i] for k in range(nz)] for i in range(2)]


def body(basis, coeffs, stiff_blocks, mass_blocks, block_cols):
    nz, ng = lax.axis_size("blk"), lax.axis_size("grp")
    current = basis[0]
    edge, columns = current.shape
    slots = block_cols.shape[-1]
    modes = columns // 3
    rows = edge * nz
    total_rows = rows * ng
    width = columns // nz

    payload = jnp.concatenate(
        [
            stiff_blocks[0, 0].reshape(slots * edge, edge),
            mass_blocks[0, 0].reshape(slots * edge, edge),
        ],
        axis=0,
    )
    turned = call(
        functools.partial(turn_kernel, modes),
        [block_cols[0], current, coeffs],
        1,
        jax.ShapeDtypeStruct((edge + 16, 2 * modes), bf16),
        [],
        2 * edge * columns * 2 * modes,
    )
    km_parts, t_parts = gather(payload, turned, nz)

    cols = jnp.stack([p[edge, :slots] for p in t_parts]).astype(jnp.int32)
    some = jax.ShapeDtypeStruct((nz - 1, edge, modes), f32)
    last = jax.ShapeDtypeStruct((edge, modes), f32)
    stats_shape = jax.ShapeDtypeStruct((3, modes), f32)
    work = 4 * edge * slots * edge * modes
    placed, stiff_some, mass_some = call(
        functools.partial(rows_kernel, nz, slots, edge, modes),
        [cols, *t_parts, *km_parts[:-1]],
        1,
        (jax.ShapeDtypeStruct((rows, 2 * modes), bf16), some, some),
        [],
        (nz - 1) * work,
    )
    stiff_last, mass_last, stats = call(
        functools.partial(stats_kernel, nz, slots, edge, modes),
        [cols, km_parts[-1], placed, stiff_some, mass_some],
        1,
        (last, last, stats_shape),
        [pltpu.VMEM((nz, 8, modes), f32)],
        work,
    )
    stats = merge_over("grp", ng, stats)
    early = call(
        functools.partial(early_turn_kernel, modes),
        [placed, coeffs],
        0,
        jax.ShapeDtypeStruct((rows, 2 * modes), f32),
        [],
        8 * rows * modes * modes,
    )
    turned, stiff_x, mass_x, stats = call(
        functools.partial(sweep_kernel, nz, slots, edge, modes, total_rows),
        [cols, *km_parts, early, stiff_some, mass_some, stiff_last, mass_last, stats, coeffs],
        1,
        (
            jax.ShapeDtypeStruct((rows, 2 * modes), bf16),
            jax.ShapeDtypeStruct((rows, modes), f32),
            jax.ShapeDtypeStruct((rows, modes), f32),
            stats_shape,
        ),
        [pltpu.VMEM((rows, modes), bf16), pltpu.VMEM((nz, 8, modes), f32)],
        4 * rows * modes * modes + nz * work,
    )
    stats = merge_over("grp", ng, stats)

    chips = ng // 2
    block = columns // ng
    split = block % 16 == 0
    gram_shape = jax.ShapeDtypeStruct(
        (chips, block, 2 * width) if split else (columns, 2 * width), bf16
    )
    window = -(-(width + max(i * width % 128 for i in range(nz))) // 128) * 128
    gram, full, full_t, applied = call(
        functools.partial(gram_kernel, nz, chips, slots, edge, modes, total_rows, split),
        [cols, *km_parts, turned, stiff_x, mass_x, stats],
        1,
        (
            gram_shape,
            jax.ShapeDtypeStruct((rows, columns), bf16),
            jax.ShapeDtypeStruct((columns, rows), bf16),
            jax.ShapeDtypeStruct((rows, 2 * width), bf16),
        ),
        [pltpu.VMEM((rows, window), bf16)],
        2 * rows * columns * width,
    )
    basis_out, ritz = call(
        functools.partial(results_kernel, edge, total_rows),
        [stats, full],
        0,
        (jax.ShapeDtypeStruct((edge, columns), bf16), jax.ShapeDtypeStruct((1, modes), f32)),
        [],
        0,
    )
    if split:
        got = lax.ppermute(gram, "grp", by_xor(ng, 1))
        keep = call(
            functools.partial(gram_rest_kernel, chips),
            [full_t, applied],
            0,
            gram_shape,
            [],
            2 * rows * columns * width,
        )
        mine = (keep.astype(f32) + got.astype(f32)).astype(bf16)
        total = mine[0].astype(f32)
        for k in range(1, chips):
            total = total + lax.ppermute(mine[k], "grp", by_xor(ng, 2 * k)).astype(f32)
    else:
        total = lax.psum_scatter(gram, "grp", scatter_dimension=0, tiled=True).astype(f32)
    return (basis_out[None], ritz[0], total.reshape(block, 2, width))


def solution(mesh):
    in_specs = (
        P("grp", "blk", None),
        P(),
        P("grp", "blk", None, None, None),
        P("grp", "blk", None, None, None),
        P("grp", "blk", None),
    )
    out_specs = (P("grp", "blk", None), P(), P("grp", None, "blk"))
    return jax.shard_map(body, mesh=mesh, in_specs=in_specs, out_specs=out_specs, check_vma=False)
```

```python
import functools

import jax
import jax.numpy as jnp
from jax import lax
from jax.experimental import pallas as pl
from jax.experimental.pallas import tpu as pltpu
from jax.sharding import PartitionSpec as P

epsilon = 1e-06
tiny = 1e-30
f32 = jnp.float32
bf16 = jnp.bfloat16
VMEM_BYTES = 24 * 1024 * 1024


def vmem():
    return pl.BlockSpec(memory_space=pltpu.VMEM)


def smem():
    return pl.BlockSpec(memory_space=pltpu.SMEM)


def block_dot(pieces_k, slots, edge, cols, k, field, lanes):
    half = slots * edge
    top = jnp.concatenate([pieces_k[s * edge : (s + 1) * edge, :] for s in range(slots)], axis=1)
    low = jnp.concatenate(
        [pieces_k[half + s * edge : half + (s + 1) * edge, :] for s in range(slots)], axis=1
    )
    rows = [
        field[pl.ds(pl.multiple_of(cols[k, s] * edge, edge), edge), lanes] for s in range(slots)
    ]
    return jnp.dot(
        jnp.concatenate([top, low], axis=0),
        jnp.concatenate(rows, axis=0),
        preferred_element_type=f32,
    )


def shift_and_scale(stats, total_rows):
    num, den, about = stats[0:1, :], stats[1:2, :], stats[2:3, :]
    shift = num / (den + epsilon)
    off = shift - num / jnp.maximum(den, tiny)
    scale = lax.rsqrt((about + off * off * den) / total_rows + epsilon)
    return shift, scale


def block_dot(pieces_k, slots, edge, cols, k, field, lanes):
    half = slots * edge
    top = jnp.concatenate([pieces_k[s * edge : (s + 1) * edge, :] for s in range(slots)], axis=1)
    low = jnp.concatenate(
        [pieces_k[half + s * edge : half + (s + 1) * edge, :] for s in range(slots)], axis=1
    )
    rows = [
        field[pl.ds(pl.multiple_of(cols[k, s] * edge, edge), edge), lanes] for s in range(slots)
    ]
    return jnp.dot(
        jnp.concatenate([top, low], axis=0),
        jnp.concatenate(rows, axis=0),
        preferred_element_type=f32,
    )


def column_stats(stiff_x, mass_x):
    num = jnp.sum(stiff_x * mass_x, axis=0, keepdims=True)
    den = jnp.sum(mass_x * mass_x, axis=0, keepdims=True)
    rest = stiff_x - (num / jnp.maximum(den, tiny)) * mass_x
    return num, den, jnp.sum(rest * rest, axis=0, keepdims=True)


def shift_and_scale(stats, total_rows):
    num, den, about = stats[0:1, :], stats[1:2, :], stats[2:3, :]
    shift = num / (den + epsilon)
    off = shift - num / jnp.maximum(den, tiny)
    scale = lax.rsqrt((about + off * off * den) / total_rows + epsilon)
    return shift, scale


def hbm():
    return pl.BlockSpec(memory_space=pltpu.HBM)


def turn_kernel(cols, current, coeffs, out_ref):
    rows, edge = current.shape[0], out_ref.shape[1]
    turned = jnp.dot(current[...], coeffs[0], preferred_element_type=f32).astype(bf16)
    blocks = turned.shape[1] // edge
    for b in range(blocks):
        out_ref[b * rows : (b + 1) * rows, :] = turned[:, b * edge : (b + 1) * edge]
    lane = lax.broadcasted_iota(jnp.int32, (16, edge), 1)
    tag = jnp.zeros((16, edge), jnp.int32)
    for s in range(cols.shape[1]):
        tag = jnp.where(lane == s, cols[0, s], tag)
    out_ref[blocks * rows : blocks * rows + 16, :] = tag.astype(f32).astype(bf16)


def rows_kernel(nz, slots, edge, modes, cols, *refs):
    t_refs, km_refs = refs[:nz], refs[nz : 2 * nz - 1]
    placed, stiff_ref, mass_ref = refs[2 * nz - 1 :]
    z = lax.axis_index("blk")
    for k in range(nz):
        at = pl.ds(pl.multiple_of((z ^ k) * edge, edge), edge)
        for b in range(placed.shape[1] // edge):
            placed[at, b * edge : (b + 1) * edge] = t_refs[k][b * edge : (b + 1) * edge, :]
    for k in range(nz - 1):
        both = block_dot(km_refs[k], slots, edge, cols, k, placed, slice(0, modes))
        stiff_ref[k] = both[:edge]
        mass_ref[k] = both[edge:]


def block_stats(z, pairs, sums, stats_ref):
    for k, (stiff_x, mass_x) in enumerate(pairs):
        sums[z ^ k, 0:1, :] = jnp.sum(stiff_x * mass_x, axis=0, keepdims=True)
        sums[z ^ k, 1:2, :] = jnp.sum(mass_x * mass_x, axis=0, keepdims=True)
    total = sums[0]
    for r in range(1, len(pairs)):
        total = total + sums[r]
    own_shift = total[0:1, :] / jnp.maximum(total[1:2, :], tiny)
    for k, (stiff_x, mass_x) in enumerate(pairs):
        rest = stiff_x - own_shift * mass_x
        sums[z ^ k, 2:3, :] = jnp.sum(rest * rest, axis=0, keepdims=True)
    about = sums[0, 2:3, :]
    for r in range(1, len(pairs)):
        about = about + sums[r, 2:3, :]
    stats_ref[0:2, :] = total[0:2, :]
    stats_ref[2:3, :] = about


def stats_kernel(nz, slots, edge, modes, cols, km_last, placed, stiff, mass, stiff_ref, mass_ref, stats_ref, sums):
    z = lax.axis_index("blk")
    both = block_dot(km_last, slots, edge, cols, nz - 1, placed, slice(0, modes))
    stiff_ref[...] = both[:edge]
    mass_ref[...] = both[edge:]
    pairs = [(stiff[k], mass[k]) for k in range(nz - 1)] + [(both[:edge], both[edge:])]
    sums[...] = jnp.zeros_like(sums)
    block_stats(z, pairs, sums, stats_ref)


def early_turn_kernel(modes, placed, coeffs, out_ref):
    out_ref[...] = jnp.dot(
        placed[:, :modes], coeffs[1, :modes, :], preferred_element_type=f32
    ) + jnp.dot(placed[:, modes:], coeffs[1, 2 * modes :, :], preferred_element_type=f32)


def sweep_kernel(nz, slots, edge, modes, total_rows, cols, *refs):
    km_refs = refs[:nz]
    early, stiff, mass, stiff_last, mass_last, stats, coeffs = refs[nz : nz + 7]
    turned_ref, stiff_ref, mass_ref, stats_ref, search, sums = refs[nz + 7 :]
    z = lax.axis_index("blk")
    at = [pl.ds(pl.multiple_of((z ^ k) * edge, edge), edge) for k in range(nz)]
    shift, scale = shift_and_scale(stats, total_rows)
    for k in range(nz):
        stiff_x = stiff[k] if k < nz - 1 else stiff_last[...]
        mass_x = mass[k] if k < nz - 1 else mass_last[...]
        search[at[k], :] = ((stiff_x - shift * mass_x) * scale).astype(bf16)
    late = jnp.dot(search[...], coeffs[1, modes : 2 * modes, :], preferred_element_type=f32)
    turned_ref[...] = (early[...] + late).astype(bf16)
    pairs = []
    for k in range(nz):
        both = block_dot(km_refs[k], slots, edge, cols, k, turned_ref, slice(0, modes))
        stiff_ref[at[k], :] = both[:edge]
        mass_ref[at[k], :] = both[edge:]
        pairs.append((both[:edge], both[edge:]))
    sums[...] = jnp.zeros_like(sums)
    block_stats(z, pairs, sums, stats_ref)


def dense_order(width):
    whole = width // 128 * 128
    return [(0, 0, whole), (1, 0, whole), (0, whole, width), (1, whole, width)]


def gram_rows(full_t, applied, chips, core, out_ref):
    chip = lax.div(lax.axis_index("grp"), 2)
    block = full_t.shape[0] // (2 * chips)
    rows = [
        full_t[pl.ds(pl.multiple_of((2 * j + core) * block, 16), block), :] for j in range(chips)
    ]
    gram = jnp.dot(jnp.concatenate(rows, axis=0), applied[...], preferred_element_type=f32)
    whole = gram.shape[1] // 128
    for j in range(chips):
        mine = gram[j * block : (j + 1) * block]
        for b in range(whole):
            part = mine[:, b * 128 : (b + 1) * 128].astype(bf16)
            out_ref[j ^ chip, b * block : (b + 1) * block, :] = part
        left = mine[:, whole * 128 :]
        left = jnp.concatenate([left[: block // 2], left[block // 2 :]], axis=1).astype(bf16)
        out_ref[j ^ chip, whole * block : whole * block + block // 2, :] = left


def finish_kernel(block, width, *refs):
    out_ref = refs[-1]
    total = refs[0][...].astype(f32)
    for ref in refs[1:-1]:
        total = total + ref[...].astype(f32)
    whole = width // 128
    left = total[2 * whole * block :, :]
    left = jnp.concatenate([left[:, :64], left[:, 64:]], axis=0)
    for op in range(2):
        for b in range(whole):
            at = (op * whole + b) * block
            out_ref[:, op, b * 128 : (b + 1) * 128] = total[at : at + block]
        out_ref[:, op, whole * 128 :] = left[:, op * 32 : (op + 1) * 32]


def gram_kernel(nz, chips, slots, edge, modes, total_rows, split, cols, *refs):
    km_refs = refs[:nz]
    turned, stiff, mass, stats = refs[nz : nz + 4]
    gram_ref, full, full_t, applied, chosen = refs[nz + 4 :]
    z = lax.axis_index("blk")
    at = [pl.ds(pl.multiple_of((z ^ k) * edge, edge), edge) for k in range(nz)]
    width = 3 * modes // nz
    shift, scale = shift_and_scale(stats, total_rows)
    full[:, 0:modes] = turned[:, 0:modes]
    full[:, modes : 2 * modes] = ((stiff[...] - shift * mass[...]) * scale).astype(bf16)
    full[:, 2 * modes : 3 * modes] = turned[:, modes : 2 * modes]
    window = chosen.shape[1]
    start = z * width // 128 * 128
    picked = full[:, pl.ds(pl.multiple_of(start, 128), window)].astype(f32)
    chosen[...] = pltpu.roll(picked, window - (z * width - start), 1).astype(bf16)
    for k in range(nz):
        both = block_dot(km_refs[k], slots, edge, cols, k, chosen, slice(0, width)).astype(bf16)
        column = 0
        for op, first, last in dense_order(width) if split else [(0, 0, width), (1, 0, width)]:
            part = both[op * edge : (op + 1) * edge, first:last]
            applied[at[k], column : column + last - first] = part
            column += last - first
    full_t[...] = full[...].T
    if split:
        gram_rows(full_t, applied, chips, 1 - lax.rem(lax.axis_index("grp"), 2), gram_ref)
    else:
        gram_ref[...] = jnp.dot(full_t[...], applied[...], preferred_element_type=f32).astype(bf16)


def results_kernel(edge, total_rows, stats, full, basis_ref, ritz_ref):
    z = lax.axis_index("blk")
    basis_ref[...] = full[pl.ds(pl.multiple_of(z * edge, edge), edge), :]
    ritz_ref[...] = shift_and_scale(stats, total_rows)[0]


def gram_rest_kernel(chips, full_t, applied, gram_ref):
    gram_rows(full_t, applied, chips, lax.rem(lax.axis_index("grp"), 2), gram_ref)


def call(kernel, inputs, n_smem, out_shape, scratch, flops):
    return pl.pallas_call(
        kernel,
        out_shape=out_shape,
        in_specs=[smem()] * n_smem + [vmem()] * (len(inputs) - n_smem),
        out_specs=jax.tree.map(lambda _: vmem(), out_shape),
        scratch_shapes=scratch,
        compiler_params=pltpu.CompilerParams(vmem_limit_bytes=VMEM_BYTES),
        cost_estimate=pl.CostEstimate(flops=flops, bytes_accessed=4_000_000, transcendentals=0),
    )(*inputs)


def by_xor(size, k):
    return [(i, i ^ k) for i in range(size)]


def merge(one, two):
    num, den = one[0] + two[0], one[1] + two[1]
    apart = one[0] / jnp.maximum(one[1], tiny) - two[0] / jnp.maximum(two[1], tiny)
    weight = jnp.sqrt(one[1]) * jnp.sqrt(two[1]) * lax.rsqrt(jnp.maximum(den, tiny))
    gap = apart * weight
    return jnp.stack([num, den, (one[2] + two[2]) + gap * gap])


def merge_over(axis, size, stats):
    step = 1
    if axis == "grp" and size >= 8:
        stats = merge(stats, lax.ppermute(stats, axis, by_xor(size, 1)))
        step = 2
        if size == 8:
            got = [lax.ppermute(stats, axis, by_xor(size, 2 * k)) for k in (1, 2, 3)]
            return merge(merge(stats, got[0]), merge(got[1], got[2]))
    while step < size:
        stats = merge(stats, lax.ppermute(stats, axis, by_xor(size, step)))
        step *= 2
    return stats


def hold_kernel(*refs):
    pass


def hold(arrays, until):
    anywhere = pl.BlockSpec(memory_space=pl.ANY)
    return pl.pallas_call(
        hold_kernel,
        out_shape=tuple(jax.ShapeDtypeStruct(a.shape, a.dtype) for a in arrays),
        in_specs=[anywhere] * (len(arrays) + len(until)),
        out_specs=(anywhere,) * len(arrays),
        input_output_aliases={i: i for i in range(len(arrays))},
        compiler_params=pltpu.CompilerParams(vmem_limit_bytes=1024 * 1024),
        cost_estimate=pl.CostEstimate(flops=0, bytes_accessed=0, transcendentals=0),
    )(*arrays, *until)


def gather(arrays, nz):
    far = nz // 2

    def send(held, step):
        return tuple(lax.ppermute(a, "blk", by_xor(nz, step)) for a in held)

    parts = {0: tuple(arrays)}
    if nz == 4:
        parts[2], parts[1] = send(arrays, 2), send(arrays, 1)
        parts[2] = hold(parts[2], parts[1])
        parts[3] = send(parts[2], 1)
    else:
        while far:
            parts |= {k ^ far: send(held, far) for k, held in parts.items()}
            far //= 2
    return [[parts[k][i] for k in range(nz)] for i in range(len(arrays))]


def body(basis, coeffs, stiff_blocks, mass_blocks, block_cols):
    nz, ng = lax.axis_size("blk"), lax.axis_size("grp")
    current = basis[0]
    edge, columns = current.shape
    slots = block_cols.shape[-1]
    modes = columns // 3
    rows = edge * nz
    total_rows = rows * ng
    width = columns // nz

    payload = jnp.concatenate(
        [
            stiff_blocks[0, 0].reshape(slots * edge, edge),
            mass_blocks[0, 0].reshape(slots * edge, edge),
        ],
        axis=0,
    )
    turned = call(
        turn_kernel,
        [block_cols[0], current, coeffs],
        1,
        jax.ShapeDtypeStruct((2 * modes + 16, edge), bf16),
        [],
        2 * edge * columns * 2 * modes,
    )
    km_parts, t_parts = gather((payload, turned), nz)

    cols = jnp.stack([p[2 * modes, :slots] for p in t_parts]).astype(jnp.int32)
    some = jax.ShapeDtypeStruct((nz - 1, edge, modes), f32)
    last = jax.ShapeDtypeStruct((edge, modes), f32)
    stats_shape = jax.ShapeDtypeStruct((3, modes), f32)
    work = 4 * edge * slots * edge * modes
    placed, stiff_some, mass_some = call(
        functools.partial(rows_kernel, nz, slots, edge, modes),
        [cols, *t_parts, *km_parts[:-1]],
        1,
        (jax.ShapeDtypeStruct((rows, 2 * modes), bf16), some, some),
        [],
        (nz - 1) * work,
    )
    stiff_last, mass_last, stats = call(
        functools.partial(stats_kernel, nz, slots, edge, modes),
        [cols, km_parts[-1], placed, stiff_some, mass_some],
        1,
        (last, last, stats_shape),
        [pltpu.VMEM((nz, 8, modes), f32)],
        work,
    )
    stats = merge_over("grp", ng, stats)
    early = call(
        functools.partial(early_turn_kernel, modes),
        [placed, coeffs],
        0,
        jax.ShapeDtypeStruct((rows, 2 * modes), f32),
        [],
        8 * rows * modes * modes,
    )
    turned, stiff_x, mass_x, stats = call(
        functools.partial(sweep_kernel, nz, slots, edge, modes, total_rows),
        [cols, *km_parts, early, stiff_some, mass_some, stiff_last, mass_last, stats, coeffs],
        1,
        (
            jax.ShapeDtypeStruct((rows, 2 * modes), bf16),
            jax.ShapeDtypeStruct((rows, modes), f32),
            jax.ShapeDtypeStruct((rows, modes), f32),
            stats_shape,
        ),
        [pltpu.VMEM((rows, modes), bf16), pltpu.VMEM((nz, 8, modes), f32)],
        4 * rows * modes * modes + nz * work,
    )
    stats = merge_over("grp", ng, stats)

    chips = ng // 2
    block = columns // ng
    split = block % 16 == 0 and width % 128 == 32
    gram_shape = jax.ShapeDtypeStruct(
        (chips, block * 2 * width // 128, 128) if split else (columns, 2 * width), bf16
    )
    window = -(-(width + max(i * width % 128 for i in range(nz))) // 128) * 128
    gram, full, full_t, applied = call(
        functools.partial(gram_kernel, nz, chips, slots, edge, modes, total_rows, split),
        [cols, *km_parts, turned, stiff_x, mass_x, stats],
        1,
        (
            gram_shape,
            jax.ShapeDtypeStruct((rows, columns), bf16),
            jax.ShapeDtypeStruct((columns, rows), bf16),
            jax.ShapeDtypeStruct((rows, 2 * width), bf16),
        ),
        [pltpu.VMEM((rows, window), bf16)],
        2 * rows * columns * width,
    )
    basis_out, ritz = call(
        functools.partial(results_kernel, edge, total_rows),
        [stats, full],
        0,
        (jax.ShapeDtypeStruct((edge, columns), bf16), jax.ShapeDtypeStruct((1, modes), f32)),
        [],
        0,
    )
    if split:
        got = lax.ppermute(gram, "grp", by_xor(ng, 1))
        keep = call(
            functools.partial(gram_rest_kernel, chips),
            [full_t, applied],
            0,
            gram_shape,
            [],
            2 * rows * columns * width,
        )
        mine = (keep.astype(f32) + got.astype(f32)).astype(bf16)
        pieces = [mine[0]] + [
            lax.ppermute(mine[k], "grp", by_xor(ng, 2 * k)) for k in range(1, chips)
        ]
        total = call(
            functools.partial(finish_kernel, block, width),
            pieces,
            0,
            jax.ShapeDtypeStruct((block, 2, width), f32),
            [],
            0,
        )
    else:
        total = lax.psum_scatter(gram, "grp", scatter_dimension=0, tiled=True)
        total = total.astype(f32).reshape(block, 2, width)
    return (basis_out[None], ritz[0], total)


def solution(mesh):
    in_specs = (
        P("grp", "blk", None),
        P(),
        P("grp", "blk", None, None, None),
        P("grp", "blk", None, None, None),
        P("grp", "blk", None),
    )
    out_specs = (P("grp", "blk", None), P(), P("grp", None, "blk"))
    return jax.shard_map(body, mesh=mesh, in_specs=in_specs, out_specs=out_specs, check_vma=False)
```

```python
import functools

import jax
import jax.numpy as jnp
from jax import lax
from jax.experimental import pallas as pl
from jax.experimental.pallas import tpu as pltpu
from jax.sharding import PartitionSpec as P

epsilon = 1e-06
tiny = 1e-30
f32 = jnp.float32
bf16 = jnp.bfloat16
VMEM_BYTES = 24 * 1024 * 1024
FIRST_VMEM_BYTES = 61 * 1024 * 1024


def vmem():
    return pl.BlockSpec(memory_space=pltpu.VMEM)


def smem():
    return pl.BlockSpec(memory_space=pltpu.SMEM)


def block_dot(pieces_k, slots, edge, cols, k, field, lanes):
    half = slots * edge
    top = jnp.concatenate([pieces_k[s * edge : (s + 1) * edge, :] for s in range(slots)], axis=1)
    low = jnp.concatenate(
        [pieces_k[half + s * edge : half + (s + 1) * edge, :] for s in range(slots)], axis=1
    )
    rows = [
        field[pl.ds(pl.multiple_of(cols[k, s] * edge, edge), edge), lanes] for s in range(slots)
    ]
    return jnp.dot(
        jnp.concatenate([top, low], axis=0),
        jnp.concatenate(rows, axis=0),
        preferred_element_type=f32,
    )


def shift_and_scale(stats, total_rows):
    num, den, about = stats[0:1, :], stats[1:2, :], stats[2:3, :]
    shift = num / (den + epsilon)
    off = shift - num / jnp.maximum(den, tiny)
    scale = lax.rsqrt((about + off * off * den) / total_rows + epsilon)
    return shift, scale


def block_dot(pieces_k, slots, edge, cols, k, field, lanes):
    half = slots * edge
    top = jnp.concatenate([pieces_k[s * edge : (s + 1) * edge, :] for s in range(slots)], axis=1)
    low = jnp.concatenate(
        [pieces_k[half + s * edge : half + (s + 1) * edge, :] for s in range(slots)], axis=1
    )
    rows = [
        field[pl.ds(pl.multiple_of(cols[k, s] * edge, edge), edge), lanes] for s in range(slots)
    ]
    return jnp.dot(
        jnp.concatenate([top, low], axis=0),
        jnp.concatenate(rows, axis=0),
        preferred_element_type=f32,
    )


def column_stats(stiff_x, mass_x):
    num = jnp.sum(stiff_x * mass_x, axis=0, keepdims=True)
    den = jnp.sum(mass_x * mass_x, axis=0, keepdims=True)
    rest = stiff_x - (num / jnp.maximum(den, tiny)) * mass_x
    return num, den, jnp.sum(rest * rest, axis=0, keepdims=True)


def shift_and_scale(stats, total_rows):
    num, den, about = stats[0:1, :], stats[1:2, :], stats[2:3, :]
    shift = num / (den + epsilon)
    off = shift - num / jnp.maximum(den, tiny)
    scale = lax.rsqrt((about + off * off * den) / total_rows + epsilon)
    return shift, scale


def hbm():
    return pl.BlockSpec(memory_space=pltpu.HBM)


def turn_kernel(chunks, cols, current_hbm, coeffs_hbm, out_ref, current, coeffs, sems):
    depth = current.shape[1] // chunks
    copies = [pltpu.make_async_copy(current_hbm, current, sems.at[0])]
    for c in range(chunks):
        part = pl.ds(c * depth, depth)
        copies.append(pltpu.make_async_copy(coeffs_hbm.at[0, part], coeffs.at[part], sems.at[c + 1]))
    for copy in copies:
        copy.start()
    rows, edge = current.shape[0], out_ref.shape[1]
    lane = lax.broadcasted_iota(jnp.int32, (16, edge), 1)
    tag = jnp.zeros((16, edge), jnp.int32)
    for s in range(cols.shape[1]):
        tag = jnp.where(lane == s, cols[0, s], tag)
    copies[0].wait()
    turned = None
    for c in range(chunks):
        copies[c + 1].wait()
        part = slice(c * depth, (c + 1) * depth)
        more = jnp.dot(current[:, part], coeffs[part, :], preferred_element_type=f32)
        turned = more if turned is None else turned + more
    turned = turned.astype(bf16)
    blocks = turned.shape[1] // edge
    for b in range(blocks):
        out_ref[b * rows : (b + 1) * rows, :] = turned[:, b * edge : (b + 1) * edge]
    out_ref[blocks * rows : blocks * rows + 16, :] = tag.astype(f32).astype(bf16)


def turn_first(cols, current, coeffs, modes):
    rows, columns = current.shape
    chunks = 3
    in_hbm = pl.BlockSpec(memory_space=pltpu.HBM)
    return pl.pallas_call(
        functools.partial(turn_kernel, chunks),
        out_shape=jax.ShapeDtypeStruct((2 * modes + 16, rows), bf16),
        in_specs=[smem(), in_hbm, in_hbm],
        out_specs=vmem(),
        scratch_shapes=[
            pltpu.VMEM((rows, columns), bf16),
            pltpu.VMEM((columns, 2 * modes), bf16),
            pltpu.SemaphoreType.DMA((chunks + 1,)),
        ],
        compiler_params=pltpu.CompilerParams(vmem_limit_bytes=FIRST_VMEM_BYTES),
        cost_estimate=pl.CostEstimate(
            flops=4 * rows * columns * modes, bytes_accessed=4 * columns * modes, transcendentals=0
        ),
    )(cols, current, coeffs)


def rows_kernel(nz, slots, edge, modes, cols, *refs):
    t_refs, km_refs = refs[:nz], refs[nz : 2 * nz - 1]
    placed, stiff_ref, mass_ref = refs[2 * nz - 1 :]
    z = lax.axis_index("blk")
    for k in range(nz):
        at = pl.ds(pl.multiple_of((z ^ k) * edge, edge), edge)
        for b in range(placed.shape[1] // edge):
            placed[at, b * edge : (b + 1) * edge] = t_refs[k][b * edge : (b + 1) * edge, :]
    for k in range(nz - 1):
        both = block_dot(km_refs[k], slots, edge, cols, k, placed, slice(0, modes))
        stiff_ref[k] = both[:edge]
        mass_ref[k] = both[edge:]


def block_stats(z, pairs, sums, stats_ref):
    for k, (stiff_x, mass_x) in enumerate(pairs):
        sums[z ^ k, 0:1, :] = jnp.sum(stiff_x * mass_x, axis=0, keepdims=True)
        sums[z ^ k, 1:2, :] = jnp.sum(mass_x * mass_x, axis=0, keepdims=True)
    total = sums[0]
    for r in range(1, len(pairs)):
        total = total + sums[r]
    own_shift = total[0:1, :] / jnp.maximum(total[1:2, :], tiny)
    for k, (stiff_x, mass_x) in enumerate(pairs):
        rest = stiff_x - own_shift * mass_x
        sums[z ^ k, 2:3, :] = jnp.sum(rest * rest, axis=0, keepdims=True)
    about = sums[0, 2:3, :]
    for r in range(1, len(pairs)):
        about = about + sums[r, 2:3, :]
    stats_ref[0:2, :] = total[0:2, :]
    stats_ref[2:3, :] = about


def stats_kernel(nz, slots, edge, modes, cols, km_last, placed, stiff, mass, stiff_ref, mass_ref, stats_ref, sums):
    z = lax.axis_index("blk")
    both = block_dot(km_last, slots, edge, cols, nz - 1, placed, slice(0, modes))
    stiff_ref[...] = both[:edge]
    mass_ref[...] = both[edge:]
    pairs = [(stiff[k], mass[k]) for k in range(nz - 1)] + [(both[:edge], both[edge:])]
    sums[...] = jnp.zeros_like(sums)
    block_stats(z, pairs, sums, stats_ref)


def early_turn_kernel(modes, placed, coeffs, out_ref):
    out_ref[...] = jnp.dot(
        placed[:, :modes], coeffs[1, :modes, :], preferred_element_type=f32
    ) + jnp.dot(placed[:, modes:], coeffs[1, 2 * modes :, :], preferred_element_type=f32)


def sweep_kernel(nz, slots, edge, modes, total_rows, cols, *refs):
    km_refs = refs[:nz]
    early, stiff, mass, stiff_last, mass_last, stats, coeffs = refs[nz : nz + 7]
    turned_ref, stiff_ref, mass_ref, stats_ref, search, sums = refs[nz + 7 :]
    z = lax.axis_index("blk")
    at = [pl.ds(pl.multiple_of((z ^ k) * edge, edge), edge) for k in range(nz)]
    shift, scale = shift_and_scale(stats, total_rows)
    for k in range(nz):
        stiff_x = stiff[k] if k < nz - 1 else stiff_last[...]
        mass_x = mass[k] if k < nz - 1 else mass_last[...]
        search[at[k], :] = ((stiff_x - shift * mass_x) * scale).astype(bf16)
    late = jnp.dot(search[...], coeffs[1, modes : 2 * modes, :], preferred_element_type=f32)
    turned_ref[...] = (early[...] + late).astype(bf16)
    pairs = []
    for k in range(nz):
        both = block_dot(km_refs[k], slots, edge, cols, k, turned_ref, slice(0, modes))
        stiff_ref[at[k], :] = both[:edge]
        mass_ref[at[k], :] = both[edge:]
        pairs.append((both[:edge], both[edge:]))
    sums[...] = jnp.zeros_like(sums)
    block_stats(z, pairs, sums, stats_ref)


def dense_order(width):
    whole = width // 128 * 128
    return [(0, 0, whole), (1, 0, whole), (0, whole, width), (1, whole, width)]


def gram_rows(full_t, applied, chips, core, out_ref):
    chip = lax.div(lax.axis_index("grp"), 2)
    block = full_t.shape[0] // (2 * chips)
    rows = [
        full_t[pl.ds(pl.multiple_of((2 * j + core) * block, 16), block), :] for j in range(chips)
    ]
    gram = jnp.dot(jnp.concatenate(rows, axis=0), applied[...], preferred_element_type=f32)
    whole = gram.shape[1] // 128
    for j in range(chips):
        mine = gram[j * block : (j + 1) * block]
        for b in range(whole):
            part = mine[:, b * 128 : (b + 1) * 128].astype(bf16)
            out_ref[j ^ chip, b * block : (b + 1) * block, :] = part
        left = mine[:, whole * 128 :]
        left = jnp.concatenate([left[: block // 2], left[block // 2 :]], axis=1).astype(bf16)
        out_ref[j ^ chip, whole * block : whole * block + block // 2, :] = left


def finish_kernel(block, width, *refs):
    out_ref = refs[-1]
    total = refs[0][...].astype(f32)
    for ref in refs[1:-1]:
        total = total + ref[...].astype(f32)
    whole = width // 128
    left = total[2 * whole * block :, :]
    left = jnp.concatenate([left[:, :64], left[:, 64:]], axis=0)
    for op in range(2):
        for b in range(whole):
            at = (op * whole + b) * block
            out_ref[:, op, b * 128 : (b + 1) * 128] = total[at : at + block]
        out_ref[:, op, whole * 128 :] = left[:, op * 32 : (op + 1) * 32]


def gram_kernel(nz, chips, slots, edge, modes, total_rows, split, cols, *refs):
    km_refs = refs[:nz]
    turned, stiff, mass, stats = refs[nz : nz + 4]
    gram_ref, full, full_t, applied, chosen = refs[nz + 4 :]
    z = lax.axis_index("blk")
    at = [pl.ds(pl.multiple_of((z ^ k) * edge, edge), edge) for k in range(nz)]
    width = 3 * modes // nz
    shift, scale = shift_and_scale(stats, total_rows)
    full[:, 0:modes] = turned[:, 0:modes]
    full[:, modes : 2 * modes] = ((stiff[...] - shift * mass[...]) * scale).astype(bf16)
    full[:, 2 * modes : 3 * modes] = turned[:, modes : 2 * modes]
    window = chosen.shape[1]
    start = z * width // 128 * 128
    picked = full[:, pl.ds(pl.multiple_of(start, 128), window)].astype(f32)
    chosen[...] = pltpu.roll(picked, window - (z * width - start), 1).astype(bf16)
    for k in range(nz):
        both = block_dot(km_refs[k], slots, edge, cols, k, chosen, slice(0, width)).astype(bf16)
        column = 0
        for op, first, last in dense_order(width) if split else [(0, 0, width), (1, 0, width)]:
            part = both[op * edge : (op + 1) * edge, first:last]
            applied[at[k], column : column + last - first] = part
            column += last - first
    full_t[...] = full[...].T
    if split:
        gram_rows(full_t, applied, chips, 1 - lax.rem(lax.axis_index("grp"), 2), gram_ref)
    else:
        gram_ref[...] = jnp.dot(full_t[...], applied[...], preferred_element_type=f32).astype(bf16)


def results_kernel(edge, total_rows, stats, full, basis_ref, ritz_ref):
    z = lax.axis_index("blk")
    basis_ref[...] = full[pl.ds(pl.multiple_of(z * edge, edge), edge), :]
    ritz_ref[...] = shift_and_scale(stats, total_rows)[0]


def gram_rest_kernel(chips, full_t, applied, gram_ref):
    gram_rows(full_t, applied, chips, lax.rem(lax.axis_index("grp"), 2), gram_ref)


def call(kernel, inputs, n_smem, out_shape, scratch, flops):
    return pl.pallas_call(
        kernel,
        out_shape=out_shape,
        in_specs=[smem()] * n_smem + [vmem()] * (len(inputs) - n_smem),
        out_specs=jax.tree.map(lambda _: vmem(), out_shape),
        scratch_shapes=scratch,
        compiler_params=pltpu.CompilerParams(vmem_limit_bytes=VMEM_BYTES),
        cost_estimate=pl.CostEstimate(flops=flops, bytes_accessed=4_000_000, transcendentals=0),
    )(*inputs)


def by_xor(size, k):
    return [(i, i ^ k) for i in range(size)]


def merge(one, two):
    num, den = one[0] + two[0], one[1] + two[1]
    apart = one[0] / jnp.maximum(one[1], tiny) - two[0] / jnp.maximum(two[1], tiny)
    weight = jnp.sqrt(one[1]) * jnp.sqrt(two[1]) * lax.rsqrt(jnp.maximum(den, tiny))
    gap = apart * weight
    return jnp.stack([num, den, (one[2] + two[2]) + gap * gap])


def merge_over(axis, size, stats):
    step = 1
    if axis == "grp" and size >= 8:
        stats = merge(stats, lax.ppermute(stats, axis, by_xor(size, 1)))
        step = 2
        if size == 8:
            got = [lax.ppermute(stats, axis, by_xor(size, 2 * k)) for k in (1, 2, 3)]
            return merge(merge(stats, got[0]), merge(got[1], got[2]))
    while step < size:
        stats = merge(stats, lax.ppermute(stats, axis, by_xor(size, step)))
        step *= 2
    return stats


def hold_kernel(*refs):
    pass


def hold(arrays, until):
    anywhere = pl.BlockSpec(memory_space=pl.ANY)
    return pl.pallas_call(
        hold_kernel,
        out_shape=tuple(jax.ShapeDtypeStruct(a.shape, a.dtype) for a in arrays),
        in_specs=[anywhere] * (len(arrays) + len(until)),
        out_specs=(anywhere,) * len(arrays),
        input_output_aliases={i: i for i in range(len(arrays))},
        compiler_params=pltpu.CompilerParams(vmem_limit_bytes=1024 * 1024),
        cost_estimate=pl.CostEstimate(flops=0, bytes_accessed=0, transcendentals=0),
    )(*arrays, *until)


def gather(operators, turned, nz):
    def send(x, step):
        return lax.ppermute(x, "blk", by_xor(nz, step))

    if nz == 4:
        km_2, km_1 = send(operators, 2), send(operators, 1)
        t_2, t_1 = send(turned, 2), send(turned, 1)
        (km_2,) = hold((km_2,), (km_1,))
        km_3 = send(km_2, 1)
        (t_2,) = hold((t_2,), (t_1,))
        return [operators, km_1, km_2, km_3], [turned, t_1, t_2, send(t_2, 1)]
    parts, far = {0: (operators, turned)}, nz // 2
    while far:
        parts |= {k ^ far: tuple(send(x, far) for x in held) for k, held in parts.items()}
        far //= 2
    return [[parts[k][i] for k in range(nz)] for i in range(2)]


def body(basis, coeffs, stiff_blocks, mass_blocks, block_cols):
    nz, ng = lax.axis_size("blk"), lax.axis_size("grp")
    current = basis[0]
    edge, columns = current.shape
    slots = block_cols.shape[-1]
    modes = columns // 3
    rows = edge * nz
    total_rows = rows * ng
    width = columns // nz

    payload = jnp.concatenate(
        [
            stiff_blocks[0, 0].reshape(slots * edge, edge),
            mass_blocks[0, 0].reshape(slots * edge, edge),
        ],
        axis=0,
    )
    turned = turn_first(block_cols[0], current, coeffs, modes)
    km_parts, t_parts = gather(payload, turned, nz)

    cols = jnp.stack([p[2 * modes, :slots] for p in t_parts]).astype(jnp.int32)
    some = jax.ShapeDtypeStruct((nz - 1, edge, modes), f32)
    last = jax.ShapeDtypeStruct((edge, modes), f32)
    stats_shape = jax.ShapeDtypeStruct((3, modes), f32)
    work = 4 * edge * slots * edge * modes
    placed, stiff_some, mass_some = call(
        functools.partial(rows_kernel, nz, slots, edge, modes),
        [cols, *t_parts, *km_parts[:-1]],
        1,
        (jax.ShapeDtypeStruct((rows, 2 * modes), bf16), some, some),
        [],
        (nz - 1) * work,
    )
    stiff_last, mass_last, stats = call(
        functools.partial(stats_kernel, nz, slots, edge, modes),
        [cols, km_parts[-1], placed, stiff_some, mass_some],
        1,
        (last, last, stats_shape),
        [pltpu.VMEM((nz, 8, modes), f32)],
        work,
    )
    stats = merge_over("grp", ng, stats)
    early = call(
        functools.partial(early_turn_kernel, modes),
        [placed, coeffs],
        0,
        jax.ShapeDtypeStruct((rows, 2 * modes), f32),
        [],
        8 * rows * modes * modes,
    )
    turned, stiff_x, mass_x, stats = call(
        functools.partial(sweep_kernel, nz, slots, edge, modes, total_rows),
        [cols, *km_parts, early, stiff_some, mass_some, stiff_last, mass_last, stats, coeffs],
        1,
        (
            jax.ShapeDtypeStruct((rows, 2 * modes), bf16),
            jax.ShapeDtypeStruct((rows, modes), f32),
            jax.ShapeDtypeStruct((rows, modes), f32),
            stats_shape,
        ),
        [pltpu.VMEM((rows, modes), bf16), pltpu.VMEM((nz, 8, modes), f32)],
        4 * rows * modes * modes + nz * work,
    )
    stats = merge_over("grp", ng, stats)

    chips = ng // 2
    block = columns // ng
    split = block % 16 == 0 and width % 128 == 32
    gram_shape = jax.ShapeDtypeStruct(
        (chips, block * 2 * width // 128, 128) if split else (columns, 2 * width), bf16
    )
    window = -(-(width + max(i * width % 128 for i in range(nz))) // 128) * 128
    gram, full, full_t, applied = call(
        functools.partial(gram_kernel, nz, chips, slots, edge, modes, total_rows, split),
        [cols, *km_parts, turned, stiff_x, mass_x, stats],
        1,
        (
            gram_shape,
            jax.ShapeDtypeStruct((rows, columns), bf16),
            jax.ShapeDtypeStruct((columns, rows), bf16),
            jax.ShapeDtypeStruct((rows, 2 * width), bf16),
        ),
        [pltpu.VMEM((rows, window), bf16)],
        2 * rows * columns * width,
    )
    basis_out, ritz = call(
        functools.partial(results_kernel, edge, total_rows),
        [stats, full],
        0,
        (jax.ShapeDtypeStruct((edge, columns), bf16), jax.ShapeDtypeStruct((1, modes), f32)),
        [],
        0,
    )
    if split:
        got = lax.ppermute(gram, "grp", by_xor(ng, 1))
        keep = call(
            functools.partial(gram_rest_kernel, chips),
            [full_t, applied],
            0,
            gram_shape,
            [],
            2 * rows * columns * width,
        )
        mine = (keep.astype(f32) + got.astype(f32)).astype(bf16)
        pieces = [mine[0]] + [
            lax.ppermute(mine[k], "grp", by_xor(ng, 2 * k)) for k in range(1, chips)
        ]
        total = call(
            functools.partial(finish_kernel, block, width),
            pieces,
            0,
            jax.ShapeDtypeStruct((block, 2, width), f32),
            [],
            0,
        )
    else:
        total = lax.psum_scatter(gram, "grp", scatter_dimension=0, tiled=True)
        total = total.astype(f32).reshape(block, 2, width)
    return (basis_out[None], ritz[0], total)


def solution(mesh):
    in_specs = (
        P("grp", "blk", None),
        P(),
        P("grp", "blk", None, None, None),
        P("grp", "blk", None, None, None),
        P("grp", "blk", None),
    )
    out_specs = (P("grp", "blk", None), P(), P("grp", None, "blk"))
    return jax.shard_map(body, mesh=mesh, in_specs=in_specs, out_specs=out_specs, check_vma=False)
```

```python
import functools

import jax
import jax.numpy as jnp
from jax import lax
from jax.experimental import pallas as pl
from jax.experimental.pallas import tpu as pltpu
from jax.sharding import PartitionSpec as P

epsilon = 1e-06
tiny = 1e-30
f32 = jnp.float32
bf16 = jnp.bfloat16
VMEM_BYTES = 24 * 1024 * 1024
FIRST_VMEM_BYTES = 61 * 1024 * 1024


def vmem():
    return pl.BlockSpec(memory_space=pltpu.VMEM)


def smem():
    return pl.BlockSpec(memory_space=pltpu.SMEM)


def block_dot(pieces_k, slots, edge, cols, k, field, lanes):
    half = slots * edge
    top = jnp.concatenate([pieces_k[s * edge : (s + 1) * edge, :] for s in range(slots)], axis=1)
    low = jnp.concatenate(
        [pieces_k[half + s * edge : half + (s + 1) * edge, :] for s in range(slots)], axis=1
    )
    rows = [
        field[pl.ds(pl.multiple_of(cols[k, s] * edge, edge), edge), lanes] for s in range(slots)
    ]
    return jnp.dot(
        jnp.concatenate([top, low], axis=0),
        jnp.concatenate(rows, axis=0),
        preferred_element_type=f32,
    )


def shift_and_scale(stats, total_rows):
    num, den, about = stats[0:1, :], stats[1:2, :], stats[2:3, :]
    shift = num / (den + epsilon)
    off = shift - num / jnp.maximum(den, tiny)
    scale = lax.rsqrt((about + off * off * den) / total_rows + epsilon)
    return shift, scale


def block_dot(pieces_k, slots, edge, cols, k, field, lanes):
    half = slots * edge
    top = jnp.concatenate([pieces_k[s * edge : (s + 1) * edge, :] for s in range(slots)], axis=1)
    low = jnp.concatenate(
        [pieces_k[half + s * edge : half + (s + 1) * edge, :] for s in range(slots)], axis=1
    )
    rows = [
        field[pl.ds(pl.multiple_of(cols[k, s] * edge, edge), edge), lanes] for s in range(slots)
    ]
    return jnp.dot(
        jnp.concatenate([top, low], axis=0),
        jnp.concatenate(rows, axis=0),
        preferred_element_type=f32,
    )


def column_stats(stiff_x, mass_x):
    num = jnp.sum(stiff_x * mass_x, axis=0, keepdims=True)
    den = jnp.sum(mass_x * mass_x, axis=0, keepdims=True)
    rest = stiff_x - (num / jnp.maximum(den, tiny)) * mass_x
    return num, den, jnp.sum(rest * rest, axis=0, keepdims=True)


def shift_and_scale(stats, total_rows):
    num, den, about = stats[0:1, :], stats[1:2, :], stats[2:3, :]
    shift = num / (den + epsilon)
    off = shift - num / jnp.maximum(den, tiny)
    scale = lax.rsqrt((about + off * off * den) / total_rows + epsilon)
    return shift, scale


def hbm():
    return pl.BlockSpec(memory_space=pltpu.HBM)


def turn_kernel(chunks, copies_each, cols_hbm, current_hbm, coeffs_hbm, out_ref, current, coeffs, cols, sems):
    depth = current.shape[1] // chunks
    piece = depth // copies_each
    copies = [pltpu.make_async_copy(current_hbm, current, sems.at[0])]
    for c in range(chunks * copies_each):
        part = pl.ds(c * piece, piece)
        copies.append(pltpu.make_async_copy(coeffs_hbm.at[0, part], coeffs.at[part], sems.at[c + 1]))
    copies.append(pltpu.make_async_copy(cols_hbm, cols, sems.at[chunks * copies_each + 1]))
    for copy in copies:
        copy.start()
    rows, edge = current.shape[0], out_ref.shape[1]
    copies[0].wait()
    turned = None
    for c in range(chunks):
        for d in range(copies_each):
            copies[c * copies_each + d + 1].wait()
        part = slice(c * depth, (c + 1) * depth)
        more = jnp.dot(current[:, part], coeffs[part, :], preferred_element_type=f32)
        turned = more if turned is None else turned + more
    copies[-1].wait()
    lane = lax.broadcasted_iota(jnp.int32, (16, edge), 1)
    tag = jnp.zeros((16, edge), jnp.int32)
    for s in range(cols.shape[1]):
        tag = jnp.where(lane == s, cols[0, s], tag)
    turned = turned.astype(bf16)
    blocks = turned.shape[1] // edge
    for b in range(blocks):
        out_ref[b * rows : (b + 1) * rows, :] = turned[:, b * edge : (b + 1) * edge]
    out_ref[blocks * rows : blocks * rows + 16, :] = tag.astype(f32).astype(bf16)


def turn_first(cols, current, coeffs, modes):
    rows, columns = current.shape
    chunks, copies_each = 3, 2
    in_hbm = pl.BlockSpec(memory_space=pltpu.HBM)
    return pl.pallas_call(
        functools.partial(turn_kernel, chunks, copies_each),
        out_shape=jax.ShapeDtypeStruct((2 * modes + 16, rows), bf16),
        in_specs=[in_hbm, in_hbm, in_hbm],
        out_specs=vmem(),
        scratch_shapes=[
            pltpu.VMEM((rows, columns), bf16),
            pltpu.VMEM((columns, 2 * modes), bf16),
            pltpu.SMEM(cols.shape, jnp.int32),
            pltpu.SemaphoreType.DMA((chunks * copies_each + 2,)),
        ],
        compiler_params=pltpu.CompilerParams(vmem_limit_bytes=FIRST_VMEM_BYTES),
        cost_estimate=pl.CostEstimate(
            flops=4 * rows * columns * modes, bytes_accessed=4 * columns * modes, transcendentals=0
        ),
    )(cols, current, coeffs)


def rows_kernel(nz, slots, edge, modes, cols, *refs):
    t_refs, km_refs = refs[:nz], refs[nz : 2 * nz - 1]
    placed, stiff_ref, mass_ref = refs[2 * nz - 1 :]
    z = lax.axis_index("blk")
    for k in range(nz):
        at = pl.ds(pl.multiple_of((z ^ k) * edge, edge), edge)
        for b in range(placed.shape[1] // edge):
            placed[at, b * edge : (b + 1) * edge] = t_refs[k][b * edge : (b + 1) * edge, :]
    for k in range(nz - 1):
        both = block_dot(km_refs[k], slots, edge, cols, k, placed, slice(0, modes))
        stiff_ref[k] = both[:edge]
        mass_ref[k] = both[edge:]


def block_stats(z, pairs, sums, stats_ref):
    for k, (stiff_x, mass_x) in enumerate(pairs):
        sums[z ^ k, 0:1, :] = jnp.sum(stiff_x * mass_x, axis=0, keepdims=True)
        sums[z ^ k, 1:2, :] = jnp.sum(mass_x * mass_x, axis=0, keepdims=True)
    total = sums[0]
    for r in range(1, len(pairs)):
        total = total + sums[r]
    own_shift = total[0:1, :] / jnp.maximum(total[1:2, :], tiny)
    for k, (stiff_x, mass_x) in enumerate(pairs):
        rest = stiff_x - own_shift * mass_x
        sums[z ^ k, 2:3, :] = jnp.sum(rest * rest, axis=0, keepdims=True)
    about = sums[0, 2:3, :]
    for r in range(1, len(pairs)):
        about = about + sums[r, 2:3, :]
    stats_ref[0:2, :] = total[0:2, :]
    stats_ref[2:3, :] = about


def stats_kernel(nz, slots, edge, modes, cols, km_last, placed, stiff, mass, stiff_ref, mass_ref, stats_ref, sums):
    z = lax.axis_index("blk")
    both = block_dot(km_last, slots, edge, cols, nz - 1, placed, slice(0, modes))
    stiff_ref[...] = both[:edge]
    mass_ref[...] = both[edge:]
    pairs = [(stiff[k], mass[k]) for k in range(nz - 1)] + [(both[:edge], both[edge:])]
    sums[...] = jnp.zeros_like(sums)
    block_stats(z, pairs, sums, stats_ref)


def early_turn_kernel(modes, placed, coeffs, out_ref):
    out_ref[...] = jnp.dot(
        placed[:, :modes], coeffs[1, :modes, :], preferred_element_type=f32
    ) + jnp.dot(placed[:, modes:], coeffs[1, 2 * modes :, :], preferred_element_type=f32)


def sweep_kernel(nz, slots, edge, modes, total_rows, cols, *refs):
    km_refs = refs[:nz]
    early, stiff, mass, stiff_last, mass_last, stats, coeffs = refs[nz : nz + 7]
    turned_ref, stiff_ref, mass_ref, stats_ref, search, sums = refs[nz + 7 :]
    z = lax.axis_index("blk")
    at = [pl.ds(pl.multiple_of((z ^ k) * edge, edge), edge) for k in range(nz)]
    shift, scale = shift_and_scale(stats, total_rows)
    for k in range(nz):
        stiff_x = stiff[k] if k < nz - 1 else stiff_last[...]
        mass_x = mass[k] if k < nz - 1 else mass_last[...]
        search[at[k], :] = ((stiff_x - shift * mass_x) * scale).astype(bf16)
    late = jnp.dot(search[...], coeffs[1, modes : 2 * modes, :], preferred_element_type=f32)
    turned_ref[...] = (early[...] + late).astype(bf16)
    pairs = []
    for k in range(nz):
        both = block_dot(km_refs[k], slots, edge, cols, k, turned_ref, slice(0, modes))
        stiff_ref[at[k], :] = both[:edge]
        mass_ref[at[k], :] = both[edge:]
        pairs.append((both[:edge], both[edge:]))
    sums[...] = jnp.zeros_like(sums)
    block_stats(z, pairs, sums, stats_ref)


def dense_order(width):
    whole = width // 128 * 128
    return [(0, 0, whole), (1, 0, whole), (0, whole, width), (1, whole, width)]


def gram_rows(full_t, applied, chips, core, out_ref):
    chip = lax.div(lax.axis_index("grp"), 2)
    block = full_t.shape[0] // (2 * chips)
    rows = [
        full_t[pl.ds(pl.multiple_of((2 * j + core) * block, 16), block), :] for j in range(chips)
    ]
    gram = jnp.dot(jnp.concatenate(rows, axis=0), applied[...], preferred_element_type=f32)
    whole = gram.shape[1] // 128
    for j in range(chips):
        mine = gram[j * block : (j + 1) * block]
        for b in range(whole):
            part = mine[:, b * 128 : (b + 1) * 128].astype(bf16)
            out_ref[j ^ chip, b * block : (b + 1) * block, :] = part
        left = mine[:, whole * 128 :]
        left = jnp.concatenate([left[: block // 2], left[block // 2 :]], axis=1).astype(bf16)
        out_ref[j ^ chip, whole * block : whole * block + block // 2, :] = left


def finish_kernel(block, width, *refs):
    out_ref = refs[-1]
    total = refs[0][...].astype(f32)
    for ref in refs[1:-1]:
        total = total + ref[...].astype(f32)
    whole = width // 128
    left = total[2 * whole * block :, :]
    left = jnp.concatenate([left[:, :64], left[:, 64:]], axis=0)
    for op in range(2):
        for b in range(whole):
            at = (op * whole + b) * block
            out_ref[:, op, b * 128 : (b + 1) * 128] = total[at : at + block]
        out_ref[:, op, whole * 128 :] = left[:, op * 32 : (op + 1) * 32]


def gram_kernel(nz, chips, slots, edge, modes, total_rows, split, cols, *refs):
    km_refs = refs[:nz]
    turned, stiff, mass, stats = refs[nz : nz + 4]
    gram_ref, full, full_t, applied, chosen = refs[nz + 4 :]
    z = lax.axis_index("blk")
    at = [pl.ds(pl.multiple_of((z ^ k) * edge, edge), edge) for k in range(nz)]
    width = 3 * modes // nz
    shift, scale = shift_and_scale(stats, total_rows)
    full[:, 0:modes] = turned[:, 0:modes]
    full[:, modes : 2 * modes] = ((stiff[...] - shift * mass[...]) * scale).astype(bf16)
    full[:, 2 * modes : 3 * modes] = turned[:, modes : 2 * modes]
    window = chosen.shape[1]
    start = z * width // 128 * 128
    picked = full[:, pl.ds(pl.multiple_of(start, 128), window)].astype(f32)
    chosen[...] = pltpu.roll(picked, window - (z * width - start), 1).astype(bf16)
    for k in range(nz):
        both = block_dot(km_refs[k], slots, edge, cols, k, chosen, slice(0, width)).astype(bf16)
        column = 0
        for op, first, last in dense_order(width) if split else [(0, 0, width), (1, 0, width)]:
            part = both[op * edge : (op + 1) * edge, first:last]
            applied[at[k], column : column + last - first] = part
            column += last - first
    full_t[...] = full[...].T
    if split:
        gram_rows(full_t, applied, chips, 1 - lax.rem(lax.axis_index("grp"), 2), gram_ref)
    else:
        gram_ref[...] = jnp.dot(full_t[...], applied[...], preferred_element_type=f32).astype(bf16)


def results_kernel(edge, total_rows, stats, full, basis_ref, ritz_ref):
    z = lax.axis_index("blk")
    basis_ref[...] = full[pl.ds(pl.multiple_of(z * edge, edge), edge), :]
    ritz_ref[...] = shift_and_scale(stats, total_rows)[0]


def gram_rest_kernel(chips, full_t, applied, gram_ref):
    gram_rows(full_t, applied, chips, lax.rem(lax.axis_index("grp"), 2), gram_ref)


def call(kernel, inputs, n_smem, out_shape, scratch, flops):
    return pl.pallas_call(
        kernel,
        out_shape=out_shape,
        in_specs=[smem()] * n_smem + [vmem()] * (len(inputs) - n_smem),
        out_specs=jax.tree.map(lambda _: vmem(), out_shape),
        scratch_shapes=scratch,
        compiler_params=pltpu.CompilerParams(vmem_limit_bytes=VMEM_BYTES),
        cost_estimate=pl.CostEstimate(flops=flops, bytes_accessed=4_000_000, transcendentals=0),
    )(*inputs)


def by_xor(size, k):
    return [(i, i ^ k) for i in range(size)]


def merge(one, two):
    num, den = one[0] + two[0], one[1] + two[1]
    apart = one[0] / jnp.maximum(one[1], tiny) - two[0] / jnp.maximum(two[1], tiny)
    weight = jnp.sqrt(one[1]) * jnp.sqrt(two[1]) * lax.rsqrt(jnp.maximum(den, tiny))
    gap = apart * weight
    return jnp.stack([num, den, (one[2] + two[2]) + gap * gap])


def merge_over(axis, size, stats):
    step = 1
    if axis == "grp" and size >= 8:
        stats = merge(stats, lax.ppermute(stats, axis, by_xor(size, 1)))
        step = 2
        if size == 8:
            got = [lax.ppermute(stats, axis, by_xor(size, 2 * k)) for k in (1, 2, 3)]
            return merge(merge(stats, got[0]), merge(got[1], got[2]))
    while step < size:
        stats = merge(stats, lax.ppermute(stats, axis, by_xor(size, step)))
        step *= 2
    return stats


def hold_kernel(*refs):
    pass


def hold(arrays, until):
    anywhere = pl.BlockSpec(memory_space=pl.ANY)
    return pl.pallas_call(
        hold_kernel,
        out_shape=tuple(jax.ShapeDtypeStruct(a.shape, a.dtype) for a in arrays),
        in_specs=[anywhere] * (len(arrays) + len(until)),
        out_specs=(anywhere,) * len(arrays),
        input_output_aliases={i: i for i in range(len(arrays))},
        compiler_params=pltpu.CompilerParams(vmem_limit_bytes=1024 * 1024),
        cost_estimate=pl.CostEstimate(flops=0, bytes_accessed=0, transcendentals=0),
    )(*arrays, *until)


def gather(operators, turned, nz):
    def send(x, step):
        return lax.ppermute(x, "blk", by_xor(nz, step))

    if nz == 4:
        km_2, km_1 = send(operators, 2), send(operators, 1)
        t_2, t_1 = send(turned, 2), send(turned, 1)
        (km_2,) = hold((km_2,), (km_1,))
        km_3 = send(km_2, 1)
        (t_2,) = hold((t_2,), (t_1,))
        return [operators, km_1, km_2, km_3], [turned, t_1, t_2, send(t_2, 1)]
    parts, far = {0: (operators, turned)}, nz // 2
    while far:
        parts |= {k ^ far: tuple(send(x, far) for x in held) for k, held in parts.items()}
        far //= 2
    return [[parts[k][i] for k in range(nz)] for i in range(2)]


def body(basis, coeffs, stiff_blocks, mass_blocks, block_cols):
    nz, ng = lax.axis_size("blk"), lax.axis_size("grp")
    current = basis[0]
    edge, columns = current.shape
    slots = block_cols.shape[-1]
    modes = columns // 3
    rows = edge * nz
    total_rows = rows * ng
    width = columns // nz

    payload = jnp.concatenate(
        [
            stiff_blocks[0, 0].reshape(slots * edge, edge),
            mass_blocks[0, 0].reshape(slots * edge, edge),
        ],
        axis=0,
    )
    turned = turn_first(block_cols[0], current, coeffs, modes)
    km_parts, t_parts = gather(payload, turned, nz)

    cols = jnp.stack([p[2 * modes, :slots] for p in t_parts]).astype(jnp.int32)
    some = jax.ShapeDtypeStruct((nz - 1, edge, modes), f32)
    last = jax.ShapeDtypeStruct((edge, modes), f32)
    stats_shape = jax.ShapeDtypeStruct((3, modes), f32)
    work = 4 * edge * slots * edge * modes
    placed, stiff_some, mass_some = call(
        functools.partial(rows_kernel, nz, slots, edge, modes),
        [cols, *t_parts, *km_parts[:-1]],
        1,
        (jax.ShapeDtypeStruct((rows, 2 * modes), bf16), some, some),
        [],
        (nz - 1) * work,
    )
    stiff_last, mass_last, stats = call(
        functools.partial(stats_kernel, nz, slots, edge, modes),
        [cols, km_parts[-1], placed, stiff_some, mass_some],
        1,
        (last, last, stats_shape),
        [pltpu.VMEM((nz, 8, modes), f32)],
        work,
    )
    stats = merge_over("grp", ng, stats)
    early = call(
        functools.partial(early_turn_kernel, modes),
        [placed, coeffs],
        0,
        jax.ShapeDtypeStruct((rows, 2 * modes), f32),
        [],
        8 * rows * modes * modes,
    )
    turned, stiff_x, mass_x, stats = call(
        functools.partial(sweep_kernel, nz, slots, edge, modes, total_rows),
        [cols, *km_parts, early, stiff_some, mass_some, stiff_last, mass_last, stats, coeffs],
        1,
        (
            jax.ShapeDtypeStruct((rows, 2 * modes), bf16),
            jax.ShapeDtypeStruct((rows, modes), f32),
            jax.ShapeDtypeStruct((rows, modes), f32),
            stats_shape,
        ),
        [pltpu.VMEM((rows, modes), bf16), pltpu.VMEM((nz, 8, modes), f32)],
        4 * rows * modes * modes + nz * work,
    )
    stats = merge_over("grp", ng, stats)

    chips = ng // 2
    block = columns // ng
    split = block % 16 == 0 and width % 128 == 32
    gram_shape = jax.ShapeDtypeStruct(
        (chips, block * 2 * width // 128, 128) if split else (columns, 2 * width), bf16
    )
    window = -(-(width + max(i * width % 128 for i in range(nz))) // 128) * 128
    gram, full, full_t, applied = call(
        functools.partial(gram_kernel, nz, chips, slots, edge, modes, total_rows, split),
        [cols, *km_parts, turned, stiff_x, mass_x, stats],
        1,
        (
            gram_shape,
            jax.ShapeDtypeStruct((rows, columns), bf16),
            jax.ShapeDtypeStruct((columns, rows), bf16),
            jax.ShapeDtypeStruct((rows, 2 * width), bf16),
        ),
        [pltpu.VMEM((rows, window), bf16)],
        2 * rows * columns * width,
    )
    basis_out, ritz = call(
        functools.partial(results_kernel, edge, total_rows),
        [stats, full],
        0,
        (jax.ShapeDtypeStruct((edge, columns), bf16), jax.ShapeDtypeStruct((1, modes), f32)),
        [],
        0,
    )
    if split:
        got = lax.ppermute(gram, "grp", by_xor(ng, 1))
        keep = call(
            functools.partial(gram_rest_kernel, chips),
            [full_t, applied],
            0,
            gram_shape,
            [],
            2 * rows * columns * width,
        )
        mine = (keep.astype(f32) + got.astype(f32)).astype(bf16)
        pieces = [mine[0]] + [
            lax.ppermute(mine[k], "grp", by_xor(ng, 2 * k)) for k in range(1, chips)
        ]
        total = call(
            functools.partial(finish_kernel, block, width),
            pieces,
            0,
            jax.ShapeDtypeStruct((block, 2, width), f32),
            [],
            0,
        )
    else:
        total = lax.psum_scatter(gram, "grp", scatter_dimension=0, tiled=True)
        total = total.astype(f32).reshape(block, 2, width)
    return (basis_out[None], ritz[0], total)


def solution(mesh):
    in_specs = (
        P("grp", "blk", None),
        P(),
        P("grp", "blk", None, None, None),
        P("grp", "blk", None, None, None),
        P("grp", "blk", None),
    )
    out_specs = (P("grp", "blk", None), P(), P("grp", None, "blk"))
    return jax.shard_map(body, mesh=mesh, in_specs=in_specs, out_specs=out_specs, check_vma=False)
```

```python
import functools

import jax
import jax.numpy as jnp
from jax import lax
from jax.experimental import pallas as pl
from jax.experimental.pallas import tpu as pltpu
from jax.sharding import PartitionSpec as P

epsilon = 1e-06
tiny = 1e-30
f32 = jnp.float32
bf16 = jnp.bfloat16
VMEM_BYTES = 24 * 1024 * 1024
FIRST_VMEM_BYTES = 61 * 1024 * 1024


def vmem():
    return pl.BlockSpec(memory_space=pltpu.VMEM)


def smem():
    return pl.BlockSpec(memory_space=pltpu.SMEM)


def block_dot(pieces_k, slots, edge, cols, k, field, lanes):
    half = slots * edge
    top = jnp.concatenate([pieces_k[s * edge : (s + 1) * edge, :] for s in range(slots)], axis=1)
    low = jnp.concatenate(
        [pieces_k[half + s * edge : half + (s + 1) * edge, :] for s in range(slots)], axis=1
    )
    rows = [
        field[pl.ds(pl.multiple_of(cols[k, s] * edge, edge), edge), lanes] for s in range(slots)
    ]
    return jnp.dot(
        jnp.concatenate([top, low], axis=0),
        jnp.concatenate(rows, axis=0),
        preferred_element_type=f32,
    )


def shift_and_scale(stats, total_rows):
    num, den, about = stats[0:1, :], stats[1:2, :], stats[2:3, :]
    shift = num / (den + epsilon)
    off = shift - num / jnp.maximum(den, tiny)
    scale = lax.rsqrt((about + off * off * den) / total_rows + epsilon)
    return shift, scale


def block_dot(pieces_k, slots, edge, cols, k, field, lanes):
    half = slots * edge
    top = jnp.concatenate([pieces_k[s * edge : (s + 1) * edge, :] for s in range(slots)], axis=1)
    low = jnp.concatenate(
        [pieces_k[half + s * edge : half + (s + 1) * edge, :] for s in range(slots)], axis=1
    )
    rows = [
        field[pl.ds(pl.multiple_of(cols[k, s] * edge, edge), edge), lanes] for s in range(slots)
    ]
    return jnp.dot(
        jnp.concatenate([top, low], axis=0),
        jnp.concatenate(rows, axis=0),
        preferred_element_type=f32,
    )


def column_stats(stiff_x, mass_x):
    num = jnp.sum(stiff_x * mass_x, axis=0, keepdims=True)
    den = jnp.sum(mass_x * mass_x, axis=0, keepdims=True)
    rest = stiff_x - (num / jnp.maximum(den, tiny)) * mass_x
    return num, den, jnp.sum(rest * rest, axis=0, keepdims=True)


def shift_and_scale(stats, total_rows):
    num, den, about = stats[0:1, :], stats[1:2, :], stats[2:3, :]
    shift = num / (den + epsilon)
    off = shift - num / jnp.maximum(den, tiny)
    scale = lax.rsqrt((about + off * off * den) / total_rows + epsilon)
    return shift, scale


def hbm():
    return pl.BlockSpec(memory_space=pltpu.HBM)


def turn_kernel(chunks, copies_each, cols_hbm, current_hbm, coeffs_hbm, out_ref, current, coeffs, cols, sems):
    depth = current.shape[1] // chunks
    piece = depth // copies_each
    copies = [pltpu.make_async_copy(current_hbm, current, sems.at[0])]
    for c in range(chunks * copies_each):
        part = pl.ds(c * piece, piece)
        copies.append(pltpu.make_async_copy(coeffs_hbm.at[0, part], coeffs.at[part], sems.at[c + 1]))
    copies.append(pltpu.make_async_copy(cols_hbm, cols, sems.at[chunks * copies_each + 1]))
    for copy in copies:
        copy.start()
    rows, edge = current.shape[0], out_ref.shape[1]
    copies[0].wait()
    turned = None
    for c in range(chunks):
        for d in range(copies_each):
            copies[c * copies_each + d + 1].wait()
        part = slice(c * depth, (c + 1) * depth)
        more = jnp.dot(current[:, part], coeffs[part, :], preferred_element_type=f32)
        turned = more if turned is None else turned + more
    copies[-1].wait()
    lane = lax.broadcasted_iota(jnp.int32, (16, edge), 1)
    tag = jnp.zeros((16, edge), jnp.int32)
    for s in range(cols.shape[1]):
        tag = jnp.where(lane == s, cols[0, s], tag)
    turned = turned.astype(bf16)
    blocks = turned.shape[1] // edge
    for b in range(blocks):
        out_ref[b * rows : (b + 1) * rows, :] = turned[:, b * edge : (b + 1) * edge]
    out_ref[blocks * rows : blocks * rows + 16, :] = tag.astype(f32).astype(bf16)


def turn_first(cols, current, coeffs, modes):
    rows, columns = current.shape
    chunks, copies_each = 3, 2
    in_hbm = pl.BlockSpec(memory_space=pltpu.HBM)
    return pl.pallas_call(
        functools.partial(turn_kernel, chunks, copies_each),
        out_shape=jax.ShapeDtypeStruct((2 * modes + 16, rows), bf16),
        in_specs=[in_hbm, in_hbm, in_hbm],
        out_specs=vmem(),
        scratch_shapes=[
            pltpu.VMEM((rows, columns), bf16),
            pltpu.VMEM((columns, 2 * modes), bf16),
            pltpu.SMEM(cols.shape, jnp.int32),
            pltpu.SemaphoreType.DMA((chunks * copies_each + 2,)),
        ],
        compiler_params=pltpu.CompilerParams(vmem_limit_bytes=FIRST_VMEM_BYTES),
        cost_estimate=pl.CostEstimate(
            flops=4 * rows * columns * modes, bytes_accessed=4 * columns * modes, transcendentals=0
        ),
    )(cols, current, coeffs)


def rows_kernel(nz, slots, edge, modes, cols, *refs):
    t_refs, km_refs = refs[:nz], refs[nz : 2 * nz - 1]
    placed, stiff_ref, mass_ref = refs[2 * nz - 1 :]
    z = lax.axis_index("blk")
    for k in range(nz):
        at = pl.ds(pl.multiple_of((z ^ k) * edge, edge), edge)
        for b in range(placed.shape[1] // edge):
            placed[at, b * edge : (b + 1) * edge] = t_refs[k][b * edge : (b + 1) * edge, :]
    for k in range(nz - 1):
        both = block_dot(km_refs[k], slots, edge, cols, k, placed, slice(0, modes))
        stiff_ref[k] = both[:edge]
        mass_ref[k] = both[edge:]


def block_products(place, stiff_x, mass_x, sums):
    sums[place, 0:1, :] = jnp.sum(stiff_x * mass_x, axis=0, keepdims=True)
    sums[place, 1:2, :] = jnp.sum(mass_x * mass_x, axis=0, keepdims=True)


def block_stats(z, pairs, sums, stats_ref):
    total = sums[0]
    for r in range(1, len(pairs)):
        total = total + sums[r]
    own_shift = total[0:1, :] / jnp.maximum(total[1:2, :], tiny)
    for k, (stiff_x, mass_x) in enumerate(pairs):
        rest = stiff_x - own_shift * mass_x
        sums[z ^ k, 2:3, :] = jnp.sum(rest * rest, axis=0, keepdims=True)
    about = sums[0, 2:3, :]
    for r in range(1, len(pairs)):
        about = about + sums[r, 2:3, :]
    stats_ref[0:2, :] = total[0:2, :]
    stats_ref[2:3, :] = about


def stats_kernel(
    nz, slots, edge, modes, cols_ref, km_last, placed, stiff, mass, stiff_ref, mass_ref, stats_ref, sums, cols, sem
):
    fetch = pltpu.make_async_copy(cols_ref, cols, sem)
    fetch.start()
    z = lax.axis_index("blk")
    sums[...] = jnp.zeros_like(sums)
    for k in range(nz - 1):
        block_products(z ^ k, stiff[k], mass[k], sums)
    fetch.wait()
    both = block_dot(km_last, slots, edge, cols, nz - 1, placed, slice(0, modes))
    stiff_ref[...] = both[:edge]
    mass_ref[...] = both[edge:]
    block_products(z ^ (nz - 1), both[:edge], both[edge:], sums)
    pairs = [(stiff[k], mass[k]) for k in range(nz - 1)] + [(both[:edge], both[edge:])]
    block_stats(z, pairs, sums, stats_ref)


def early_turn_kernel(modes, placed, coeffs, out_ref):
    out_ref[...] = jnp.dot(
        placed[:, :modes], coeffs[1, :modes, :], preferred_element_type=f32
    ) + jnp.dot(placed[:, modes:], coeffs[1, 2 * modes :, :], preferred_element_type=f32)


def sweep_kernel(nz, slots, edge, modes, total_rows, cols_ref, *refs):
    *refs, cols, sem = refs
    fetch = pltpu.make_async_copy(cols_ref, cols, sem)
    fetch.start()
    km_refs = refs[:nz]
    early, stiff, mass, stiff_last, mass_last, stats, coeffs = refs[nz : nz + 7]
    turned_ref, stiff_ref, mass_ref, stats_ref, search, sums = refs[nz + 7 :]
    z = lax.axis_index("blk")
    at = [pl.ds(pl.multiple_of((z ^ k) * edge, edge), edge) for k in range(nz)]
    shift, scale = shift_and_scale(stats, total_rows)
    for k in range(nz):
        stiff_x = stiff[k] if k < nz - 1 else stiff_last[...]
        mass_x = mass[k] if k < nz - 1 else mass_last[...]
        search[at[k], :] = ((stiff_x - shift * mass_x) * scale).astype(bf16)
    late = jnp.dot(search[...], coeffs[1, modes : 2 * modes, :], preferred_element_type=f32)
    turned_ref[...] = (early[...] + late).astype(bf16)
    sums[...] = jnp.zeros_like(sums)
    fetch.wait()
    pairs = []
    for k in range(nz):
        both = block_dot(km_refs[k], slots, edge, cols, k, turned_ref, slice(0, modes))
        stiff_ref[at[k], :] = both[:edge]
        mass_ref[at[k], :] = both[edge:]
        block_products(z ^ k, both[:edge], both[edge:], sums)
        pairs.append((both[:edge], both[edge:]))
    block_stats(z, pairs, sums, stats_ref)


def dense_order(width):
    whole = width // 128 * 128
    return [(0, 0, whole), (1, 0, whole), (0, whole, width), (1, whole, width)]


def gram_rows(full_t, applied, chips, core, out_ref):
    chip = lax.div(lax.axis_index("grp"), 2)
    block = full_t.shape[0] // (2 * chips)
    rows = [
        full_t[pl.ds(pl.multiple_of((2 * j + core) * block, 16), block), :] for j in range(chips)
    ]
    gram = jnp.dot(jnp.concatenate(rows, axis=0), applied[...], preferred_element_type=f32)
    whole = gram.shape[1] // 128
    for j in range(chips):
        mine = gram[j * block : (j + 1) * block]
        for b in range(whole):
            part = mine[:, b * 128 : (b + 1) * 128].astype(bf16)
            out_ref[j ^ chip, b * block : (b + 1) * block, :] = part
        left = mine[:, whole * 128 :]
        left = jnp.concatenate([left[: block // 2], left[block // 2 :]], axis=1).astype(bf16)
        out_ref[j ^ chip, whole * block : whole * block + block // 2, :] = left


def finish_kernel(block, width, *refs):
    out_ref = refs[-1]
    total = refs[0][...].astype(f32)
    for ref in refs[1:-1]:
        total = total + ref[...].astype(f32)
    whole = width // 128
    left = total[2 * whole * block :, :]
    left = jnp.concatenate([left[:, :64], left[:, 64:]], axis=0)
    for op in range(2):
        for b in range(whole):
            at = (op * whole + b) * block
            out_ref[:, op, b * 128 : (b + 1) * 128] = total[at : at + block]
        out_ref[:, op, whole * 128 :] = left[:, op * 32 : (op + 1) * 32]


def gram_kernel(nz, chips, slots, edge, modes, total_rows, split, cols_ref, *refs):
    *refs, cols, sem = refs
    fetch = pltpu.make_async_copy(cols_ref, cols, sem)
    fetch.start()
    km_refs = refs[:nz]
    turned, stiff, mass, stats = refs[nz : nz + 4]
    gram_ref, full, full_t, applied, chosen = refs[nz + 4 :]
    z = lax.axis_index("blk")
    at = [pl.ds(pl.multiple_of((z ^ k) * edge, edge), edge) for k in range(nz)]
    width = 3 * modes // nz
    shift, scale = shift_and_scale(stats, total_rows)
    full[:, 0:modes] = turned[:, 0:modes]
    full[:, modes : 2 * modes] = ((stiff[...] - shift * mass[...]) * scale).astype(bf16)
    full[:, 2 * modes : 3 * modes] = turned[:, modes : 2 * modes]
    full_t[...] = full[...].T
    window = chosen.shape[1]
    start = z * width // 128 * 128
    picked = full[:, pl.ds(pl.multiple_of(start, 128), window)].astype(f32)
    chosen[...] = pltpu.roll(picked, window - (z * width - start), 1).astype(bf16)
    fetch.wait()
    for k in range(nz):
        both = block_dot(km_refs[k], slots, edge, cols, k, chosen, slice(0, width)).astype(bf16)
        column = 0
        for op, first, last in dense_order(width) if split else [(0, 0, width), (1, 0, width)]:
            part = both[op * edge : (op + 1) * edge, first:last]
            applied[at[k], column : column + last - first] = part
            column += last - first
    if split:
        gram_rows(full_t, applied, chips, 1 - lax.rem(lax.axis_index("grp"), 2), gram_ref)
    else:
        gram_ref[...] = jnp.dot(full_t[...], applied[...], preferred_element_type=f32).astype(bf16)


def results_kernel(edge, total_rows, stats, full, basis_ref, ritz_ref):
    z = lax.axis_index("blk")
    basis_ref[...] = full[pl.ds(pl.multiple_of(z * edge, edge), edge), :]
    ritz_ref[...] = shift_and_scale(stats, total_rows)[0]


def gram_rest_kernel(chips, full_t, applied, gram_ref):
    gram_rows(full_t, applied, chips, lax.rem(lax.axis_index("grp"), 2), gram_ref)


def call(kernel, inputs, n_smem, out_shape, scratch, flops, n_any=0):
    return pl.pallas_call(
        kernel,
        out_shape=out_shape,
        in_specs=[smem()] * n_smem
        + [pl.BlockSpec(memory_space=pl.ANY)] * n_any
        + [vmem()] * (len(inputs) - n_smem - n_any),
        out_specs=jax.tree.map(lambda _: vmem(), out_shape),
        scratch_shapes=scratch,
        compiler_params=pltpu.CompilerParams(vmem_limit_bytes=VMEM_BYTES),
        cost_estimate=pl.CostEstimate(flops=flops, bytes_accessed=4_000_000, transcendentals=0),
    )(*inputs)


def by_xor(size, k):
    return [(i, i ^ k) for i in range(size)]


def merge(one, two):
    num, den = one[0] + two[0], one[1] + two[1]
    apart = one[0] / jnp.maximum(one[1], tiny) - two[0] / jnp.maximum(two[1], tiny)
    weight = jnp.sqrt(one[1]) * jnp.sqrt(two[1]) * lax.rsqrt(jnp.maximum(den, tiny))
    gap = apart * weight
    return jnp.stack([num, den, (one[2] + two[2]) + gap * gap])


def merge_over(axis, size, stats):
    step = 1
    if axis == "grp" and size >= 8:
        stats = merge(stats, lax.ppermute(stats, axis, by_xor(size, 1)))
        step = 2
        if size == 8:
            got = [lax.ppermute(stats, axis, by_xor(size, 2 * k)) for k in (1, 2, 3)]
            return merge(merge(stats, got[0]), merge(got[1], got[2]))
    while step < size:
        stats = merge(stats, lax.ppermute(stats, axis, by_xor(size, step)))
        step *= 2
    return stats


def hold_kernel(*refs):
    pass


def hold(arrays, until):
    anywhere = pl.BlockSpec(memory_space=pl.ANY)
    return pl.pallas_call(
        hold_kernel,
        out_shape=tuple(jax.ShapeDtypeStruct(a.shape, a.dtype) for a in arrays),
        in_specs=[anywhere] * (len(arrays) + len(until)),
        out_specs=(anywhere,) * len(arrays),
        input_output_aliases={i: i for i in range(len(arrays))},
        compiler_params=pltpu.CompilerParams(vmem_limit_bytes=1024 * 1024),
        cost_estimate=pl.CostEstimate(flops=0, bytes_accessed=0, transcendentals=0),
    )(*arrays, *until)


def gather(operators, turned, nz):
    def send(x, step):
        return lax.ppermute(x, "blk", by_xor(nz, step))

    if nz == 4:
        km_2, km_1 = send(operators, 2), send(operators, 1)
        t_2, t_1 = send(turned, 2), send(turned, 1)
        (km_2,) = hold((km_2,), (km_1,))
        km_3 = send(km_2, 1)
        (t_2,) = hold((t_2,), (t_1,))
        return [operators, km_1, km_2, km_3], [turned, t_1, t_2, send(t_2, 1)]
    parts, far = {0: (operators, turned)}, nz // 2
    while far:
        parts |= {k ^ far: tuple(send(x, far) for x in held) for k, held in parts.items()}
        far //= 2
    return [[parts[k][i] for k in range(nz)] for i in range(2)]


def body(basis, coeffs, stiff_blocks, mass_blocks, block_cols):
    nz, ng = lax.axis_size("blk"), lax.axis_size("grp")
    current = basis[0]
    edge, columns = current.shape
    slots = block_cols.shape[-1]
    modes = columns // 3
    rows = edge * nz
    total_rows = rows * ng
    width = columns // nz

    payload = jnp.concatenate(
        [
            stiff_blocks[0, 0].reshape(slots * edge, edge),
            mass_blocks[0, 0].reshape(slots * edge, edge),
        ],
        axis=0,
    )
    turned = turn_first(block_cols[0], current, coeffs, modes)
    km_parts, t_parts = gather(payload, turned, nz)

    cols = jnp.stack([p[2 * modes, :slots] for p in t_parts]).astype(jnp.int32)
    some = jax.ShapeDtypeStruct((nz - 1, edge, modes), f32)
    last = jax.ShapeDtypeStruct((edge, modes), f32)
    stats_shape = jax.ShapeDtypeStruct((3, modes), f32)
    work = 4 * edge * slots * edge * modes
    placed, stiff_some, mass_some = call(
        functools.partial(rows_kernel, nz, slots, edge, modes),
        [cols, *t_parts, *km_parts[:-1]],
        1,
        (jax.ShapeDtypeStruct((rows, 2 * modes), bf16), some, some),
        [],
        (nz - 1) * work,
    )
    fetched = [pltpu.SMEM((nz, slots), jnp.int32), pltpu.SemaphoreType.DMA(())]
    stiff_last, mass_last, stats = call(
        functools.partial(stats_kernel, nz, slots, edge, modes),
        [cols, km_parts[-1], placed, stiff_some, mass_some],
        0,
        (last, last, stats_shape),
        [pltpu.VMEM((nz, 8, modes), f32), *fetched],
        work,
        n_any=1,
    )
    stats = merge_over("grp", ng, stats)
    early = call(
        functools.partial(early_turn_kernel, modes),
        [placed, coeffs],
        0,
        jax.ShapeDtypeStruct((rows, 2 * modes), f32),
        [],
        8 * rows * modes * modes,
    )
    turned, stiff_x, mass_x, stats = call(
        functools.partial(sweep_kernel, nz, slots, edge, modes, total_rows),
        [cols, *km_parts, early, stiff_some, mass_some, stiff_last, mass_last, stats, coeffs],
        0,
        (
            jax.ShapeDtypeStruct((rows, 2 * modes), bf16),
            jax.ShapeDtypeStruct((rows, modes), f32),
            jax.ShapeDtypeStruct((rows, modes), f32),
            stats_shape,
        ),
        [pltpu.VMEM((rows, modes), bf16), pltpu.VMEM((nz, 8, modes), f32), *fetched],
        4 * rows * modes * modes + nz * work,
        n_any=1,
    )
    stats = merge_over("grp", ng, stats)

    chips = ng // 2
    block = columns // ng
    split = block % 16 == 0 and width % 128 == 32
    gram_shape = jax.ShapeDtypeStruct(
        (chips, block * 2 * width // 128, 128) if split else (columns, 2 * width), bf16
    )
    window = -(-(width + max(i * width % 128 for i in range(nz))) // 128) * 128
    gram, full, full_t, applied = call(
        functools.partial(gram_kernel, nz, chips, slots, edge, modes, total_rows, split),
        [cols, *km_parts, turned, stiff_x, mass_x, stats],
        0,
        (
            gram_shape,
            jax.ShapeDtypeStruct((rows, columns), bf16),
            jax.ShapeDtypeStruct((columns, rows), bf16),
            jax.ShapeDtypeStruct((rows, 2 * width), bf16),
        ),
        [pltpu.VMEM((rows, window), bf16), *fetched],
        2 * rows * columns * width,
        n_any=1,
    )
    basis_out, ritz = call(
        functools.partial(results_kernel, edge, total_rows),
        [stats, full],
        0,
        (jax.ShapeDtypeStruct((edge, columns), bf16), jax.ShapeDtypeStruct((1, modes), f32)),
        [],
        0,
    )
    if split:
        got = lax.ppermute(gram, "grp", by_xor(ng, 1))
        keep = call(
            functools.partial(gram_rest_kernel, chips),
            [full_t, applied],
            0,
            gram_shape,
            [],
            2 * rows * columns * width,
        )
        mine = (keep.astype(f32) + got.astype(f32)).astype(bf16)
        pieces = [mine[0]] + [
            lax.ppermute(mine[k], "grp", by_xor(ng, 2 * k)) for k in range(1, chips)
        ]
        total = call(
            functools.partial(finish_kernel, block, width),
            pieces,
            0,
            jax.ShapeDtypeStruct((block, 2, width), f32),
            [],
            0,
        )
    else:
        total = lax.psum_scatter(gram, "grp", scatter_dimension=0, tiled=True)
        total = total.astype(f32).reshape(block, 2, width)
    return (basis_out[None], ritz[0], total)


def solution(mesh):
    in_specs = (
        P("grp", "blk", None),
        P(),
        P("grp", "blk", None, None, None),
        P("grp", "blk", None, None, None),
        P("grp", "blk", None),
    )
    out_specs = (P("grp", "blk", None), P(), P("grp", None, "blk"))
    return jax.shard_map(body, mesh=mesh, in_specs=in_specs, out_specs=out_specs, check_vma=False)
```

```python
import functools

import jax
import jax.numpy as jnp
from jax import lax
from jax.experimental import pallas as pl
from jax.experimental.pallas import tpu as pltpu
from jax.sharding import PartitionSpec as P

epsilon = 1e-06
tiny = 1e-30
f32 = jnp.float32
bf16 = jnp.bfloat16
VMEM_BYTES = 24 * 1024 * 1024
FIRST_VMEM_BYTES = 61 * 1024 * 1024


def vmem():
    return pl.BlockSpec(memory_space=pltpu.VMEM)


def smem():
    return pl.BlockSpec(memory_space=pltpu.SMEM)


def block_dot(pieces_k, slots, edge, cols, k, field, lanes):
    half = slots * edge
    top = jnp.concatenate([pieces_k[s * edge : (s + 1) * edge, :] for s in range(slots)], axis=1)
    low = jnp.concatenate(
        [pieces_k[half + s * edge : half + (s + 1) * edge, :] for s in range(slots)], axis=1
    )
    rows = [
        field[pl.ds(pl.multiple_of(cols[k, s] * edge, edge), edge), lanes] for s in range(slots)
    ]
    return jnp.dot(
        jnp.concatenate([top, low], axis=0),
        jnp.concatenate(rows, axis=0),
        preferred_element_type=f32,
    )


def shift_and_scale(stats, total_rows):
    num, den, about = stats[0:1, :], stats[1:2, :], stats[2:3, :]
    shift = num / (den + epsilon)
    off = shift - num / jnp.maximum(den, tiny)
    scale = lax.rsqrt((about + off * off * den) / total_rows + epsilon)
    return shift, scale


def block_dot(pieces_k, slots, edge, cols, k, field, lanes):
    half = slots * edge
    top = jnp.concatenate([pieces_k[s * edge : (s + 1) * edge, :] for s in range(slots)], axis=1)
    low = jnp.concatenate(
        [pieces_k[half + s * edge : half + (s + 1) * edge, :] for s in range(slots)], axis=1
    )
    rows = [
        field[pl.ds(pl.multiple_of(cols[k, s] * edge, edge), edge), lanes] for s in range(slots)
    ]
    return jnp.dot(
        jnp.concatenate([top, low], axis=0),
        jnp.concatenate(rows, axis=0),
        preferred_element_type=f32,
    )


def column_stats(stiff_x, mass_x):
    num = jnp.sum(stiff_x * mass_x, axis=0, keepdims=True)
    den = jnp.sum(mass_x * mass_x, axis=0, keepdims=True)
    rest = stiff_x - (num / jnp.maximum(den, tiny)) * mass_x
    return num, den, jnp.sum(rest * rest, axis=0, keepdims=True)


def shift_and_scale(stats, total_rows):
    num, den, about = stats[0:1, :], stats[1:2, :], stats[2:3, :]
    shift = num / (den + epsilon)
    off = shift - num / jnp.maximum(den, tiny)
    scale = lax.rsqrt((about + off * off * den) / total_rows + epsilon)
    return shift, scale


def hbm():
    return pl.BlockSpec(memory_space=pltpu.HBM)


def turn_kernel(chunks, copies_each, cols_hbm, current_hbm, coeffs_hbm, out_ref, current, coeffs, cols, sems):
    depth = current.shape[1] // chunks
    piece = depth // copies_each
    copies = [pltpu.make_async_copy(current_hbm, current, sems.at[0])]
    for c in range(chunks * copies_each):
        part = pl.ds(c * piece, piece)
        copies.append(pltpu.make_async_copy(coeffs_hbm.at[0, part], coeffs.at[part], sems.at[c + 1]))
    copies.append(pltpu.make_async_copy(cols_hbm, cols, sems.at[chunks * copies_each + 1]))
    for copy in copies:
        copy.start()
    rows, edge = current.shape[0], out_ref.shape[1]
    copies[0].wait()
    turned = None
    for c in range(chunks):
        for d in range(copies_each):
            copies[c * copies_each + d + 1].wait()
        part = slice(c * depth, (c + 1) * depth)
        more = jnp.dot(current[:, part], coeffs[part, :], preferred_element_type=f32)
        turned = more if turned is None else turned + more
    copies[-1].wait()
    lane = lax.broadcasted_iota(jnp.int32, (16, edge), 1)
    tag = jnp.zeros((16, edge), jnp.int32)
    for s in range(cols.shape[1]):
        tag = jnp.where(lane == s, cols[0, s], tag)
    turned = turned.astype(bf16)
    blocks = turned.shape[1] // edge
    for b in range(blocks):
        out_ref[b * rows : (b + 1) * rows, :] = turned[:, b * edge : (b + 1) * edge]
    out_ref[blocks * rows : blocks * rows + 16, :] = tag.astype(f32).astype(bf16)


def turn_first(cols, current, coeffs, modes):
    rows, columns = current.shape
    chunks, copies_each = 3, 2
    in_hbm = pl.BlockSpec(memory_space=pltpu.HBM)
    return pl.pallas_call(
        functools.partial(turn_kernel, chunks, copies_each),
        out_shape=jax.ShapeDtypeStruct((2 * modes + 16, rows), bf16),
        in_specs=[in_hbm, in_hbm, in_hbm],
        out_specs=vmem(),
        scratch_shapes=[
            pltpu.VMEM((rows, columns), bf16),
            pltpu.VMEM((columns, 2 * modes), bf16),
            pltpu.SMEM(cols.shape, jnp.int32),
            pltpu.SemaphoreType.DMA((chunks * copies_each + 2,)),
        ],
        compiler_params=pltpu.CompilerParams(vmem_limit_bytes=FIRST_VMEM_BYTES),
        cost_estimate=pl.CostEstimate(
            flops=4 * rows * columns * modes, bytes_accessed=4 * columns * modes, transcendentals=0
        ),
    )(cols, current, coeffs)


def rows_kernel(nz, slots, edge, modes, cols, *refs):
    t_refs, km_refs = refs[:nz], refs[nz : 2 * nz - 1]
    placed, stiff_ref, mass_ref = refs[2 * nz - 1 :]
    z = lax.axis_index("blk")
    for k in range(nz):
        at = pl.ds(pl.multiple_of((z ^ k) * edge, edge), edge)
        for b in range(placed.shape[1] // edge):
            placed[at, b * edge : (b + 1) * edge] = t_refs[k][b * edge : (b + 1) * edge, :]
    for k in range(nz - 1):
        both = block_dot(km_refs[k], slots, edge, cols, k, placed, slice(0, modes))
        stiff_ref[k] = both[:edge]
        mass_ref[k] = both[edge:]


def block_products(place, stiff_x, mass_x, sums):
    sums[place, 0:1, :] = jnp.sum(stiff_x * mass_x, axis=0, keepdims=True)
    sums[place, 1:2, :] = jnp.sum(mass_x * mass_x, axis=0, keepdims=True)


def block_stats(z, pairs, sums, stats_ref):
    total = sums[0]
    for r in range(1, len(pairs)):
        total = total + sums[r]
    own_shift = total[0:1, :] / jnp.maximum(total[1:2, :], tiny)
    for k, (stiff_x, mass_x) in enumerate(pairs):
        rest = stiff_x - own_shift * mass_x
        sums[z ^ k, 2:3, :] = jnp.sum(rest * rest, axis=0, keepdims=True)
    about = sums[0, 2:3, :]
    for r in range(1, len(pairs)):
        about = about + sums[r, 2:3, :]
    stats_ref[0:2, :] = total[0:2, :]
    stats_ref[2:3, :] = about


def stats_kernel(
    nz, slots, edge, modes, cols_ref, km_last, placed, stiff, mass, stiff_ref, mass_ref, stats_ref, sums, cols, sem
):
    fetch = pltpu.make_async_copy(cols_ref, cols, sem)
    fetch.start()
    z = lax.axis_index("blk")
    sums[...] = jnp.zeros_like(sums)
    for k in range(nz - 1):
        block_products(z ^ k, stiff[k], mass[k], sums)
    fetch.wait()
    both = block_dot(km_last, slots, edge, cols, nz - 1, placed, slice(0, modes))
    stiff_ref[...] = both[:edge]
    mass_ref[...] = both[edge:]
    block_products(z ^ (nz - 1), both[:edge], both[edge:], sums)
    pairs = [(stiff[k], mass[k]) for k in range(nz - 1)] + [(both[:edge], both[edge:])]
    block_stats(z, pairs, sums, stats_ref)


def early_turn_kernel(modes, placed, coeffs, out_ref):
    out_ref[...] = jnp.dot(
        placed[:, :modes], coeffs[1, :modes, :], preferred_element_type=f32
    ) + jnp.dot(placed[:, modes:], coeffs[1, 2 * modes :, :], preferred_element_type=f32)


def sweep_kernel(nz, slots, edge, modes, total_rows, cols_ref, *refs):
    *refs, cols, sem = refs
    fetch = pltpu.make_async_copy(cols_ref, cols, sem)
    fetch.start()
    km_refs = refs[:nz]
    early, stiff, mass, stiff_last, mass_last, stats, coeffs = refs[nz : nz + 7]
    turned_ref, stiff_ref, mass_ref, stats_ref, search, sums = refs[nz + 7 :]
    z = lax.axis_index("blk")
    at = [pl.ds(pl.multiple_of((z ^ k) * edge, edge), edge) for k in range(nz)]
    shift, scale = shift_and_scale(stats, total_rows)
    for k in range(nz):
        stiff_x = stiff[k] if k < nz - 1 else stiff_last[...]
        mass_x = mass[k] if k < nz - 1 else mass_last[...]
        search[at[k], :] = ((stiff_x - shift * mass_x) * scale).astype(bf16)
    late = jnp.dot(search[...], coeffs[1, modes : 2 * modes, :], preferred_element_type=f32)
    turned_ref[...] = (early[...] + late).astype(bf16)
    sums[...] = jnp.zeros_like(sums)
    fetch.wait()
    pairs = []
    for k in range(nz):
        both = block_dot(km_refs[k], slots, edge, cols, k, turned_ref, slice(0, modes))
        stiff_ref[at[k], :] = both[:edge]
        mass_ref[at[k], :] = both[edge:]
        block_products(z ^ k, both[:edge], both[edge:], sums)
        pairs.append((both[:edge], both[edge:]))
    block_stats(z, pairs, sums, stats_ref)


def dense_order(width):
    whole = width // 128 * 128
    return [(0, 0, whole), (1, 0, whole), (0, whole, width), (1, whole, width)]


def gram_rows(full_t, applied, chips, core, bounds, out_refs):
    chip = lax.div(lax.axis_index("grp"), 2)
    block = full_t.shape[0] // (2 * chips)
    rows = [
        full_t[pl.ds(pl.multiple_of((2 * j + core) * block, 16), block), :] for j in range(chips)
    ]
    gram = jnp.dot(jnp.concatenate(rows, axis=0), applied[...], preferred_element_type=f32)
    whole = gram.shape[1] // 128
    for (low, high), out_ref in zip(bounds, out_refs):
        size = high - low
        for j in range(chips):
            mine = gram[j * block + low : j * block + high]
            for b in range(whole):
                part = mine[:, b * 128 : (b + 1) * 128].astype(bf16)
                out_ref[j ^ chip, b * size : (b + 1) * size, :] = part
            left = mine[:, whole * 128 :]
            left = jnp.concatenate([left[: size // 2], left[size // 2 :]], axis=1).astype(bf16)
            out_ref[j ^ chip, whole * size : whole * size + size // 2, :] = left


def finish_kernel(bounds, width, *refs):
    *refs, out_ref = refs
    each = len(refs) // len(bounds)
    whole = width // 128
    for i, (low, high) in enumerate(bounds):
        size = high - low
        total = refs[i * each][...].astype(f32)
        for ref in refs[i * each + 1 : (i + 1) * each]:
            total = total + ref[...].astype(f32)
        left = total[2 * whole * size :, :]
        left = jnp.concatenate([left[:, :64], left[:, 64:]], axis=0)
        for op in range(2):
            for b in range(whole):
                at = (op * whole + b) * size
                out_ref[low:high, op, b * 128 : (b + 1) * 128] = total[at : at + size]
            out_ref[low:high, op, whole * 128 :] = left[:, op * 32 : (op + 1) * 32]


def gram_kernel(nz, chips, slots, edge, modes, total_rows, bounds, cols_ref, *refs):
    *refs, cols, sem = refs
    fetch = pltpu.make_async_copy(cols_ref, cols, sem)
    fetch.start()
    km_refs = refs[:nz]
    turned, stiff, mass, stats = refs[nz : nz + 4]
    *gram_refs, full, full_t, applied, chosen = refs[nz + 4 :]
    z = lax.axis_index("blk")
    at = [pl.ds(pl.multiple_of((z ^ k) * edge, edge), edge) for k in range(nz)]
    width = 3 * modes // nz
    shift, scale = shift_and_scale(stats, total_rows)
    full[:, 0:modes] = turned[:, 0:modes]
    full[:, modes : 2 * modes] = ((stiff[...] - shift * mass[...]) * scale).astype(bf16)
    full[:, 2 * modes : 3 * modes] = turned[:, modes : 2 * modes]
    full_t[...] = full[...].T
    window = chosen.shape[1]
    start = z * width // 128 * 128
    picked = full[:, pl.ds(pl.multiple_of(start, 128), window)].astype(f32)
    chosen[...] = pltpu.roll(picked, window - (z * width - start), 1).astype(bf16)
    fetch.wait()
    for k in range(nz):
        both = block_dot(km_refs[k], slots, edge, cols, k, chosen, slice(0, width)).astype(bf16)
        column = 0
        for op, first, last in dense_order(width) if bounds else [(0, 0, width), (1, 0, width)]:
            part = both[op * edge : (op + 1) * edge, first:last]
            applied[at[k], column : column + last - first] = part
            column += last - first
    if bounds:
        other = 1 - lax.rem(lax.axis_index("grp"), 2)
        gram_rows(full_t, applied, chips, other, bounds, gram_refs)
    else:
        gram_refs[0][...] = jnp.dot(full_t[...], applied[...], preferred_element_type=f32).astype(bf16)


def results_kernel(edge, total_rows, stats, full, basis_ref, ritz_ref):
    z = lax.axis_index("blk")
    basis_ref[...] = full[pl.ds(pl.multiple_of(z * edge, edge), edge), :]
    ritz_ref[...] = shift_and_scale(stats, total_rows)[0]


def gram_rest_kernel(chips, bounds, full_t, applied, *gram_refs):
    own = lax.rem(lax.axis_index("grp"), 2)
    gram_rows(full_t, applied, chips, own, bounds, gram_refs)


def call(kernel, inputs, n_smem, out_shape, scratch, flops, n_any=0):
    return pl.pallas_call(
        kernel,
        out_shape=out_shape,
        in_specs=[smem()] * n_smem
        + [pl.BlockSpec(memory_space=pl.ANY)] * n_any
        + [vmem()] * (len(inputs) - n_smem - n_any),
        out_specs=jax.tree.map(lambda _: vmem(), out_shape),
        scratch_shapes=scratch,
        compiler_params=pltpu.CompilerParams(vmem_limit_bytes=VMEM_BYTES),
        cost_estimate=pl.CostEstimate(flops=flops, bytes_accessed=4_000_000, transcendentals=0),
    )(*inputs)


def by_xor(size, k):
    return [(i, i ^ k) for i in range(size)]


def merge(one, two):
    num, den = one[0] + two[0], one[1] + two[1]
    apart = one[0] / jnp.maximum(one[1], tiny) - two[0] / jnp.maximum(two[1], tiny)
    weight = jnp.sqrt(one[1]) * jnp.sqrt(two[1]) * lax.rsqrt(jnp.maximum(den, tiny))
    gap = apart * weight
    return jnp.stack([num, den, (one[2] + two[2]) + gap * gap])


def merge_over(axis, size, stats):
    step = 1
    if axis == "grp" and size >= 8:
        stats = merge(stats, lax.ppermute(stats, axis, by_xor(size, 1)))
        step = 2
        if size == 8:
            got = [lax.ppermute(stats, axis, by_xor(size, 2 * k)) for k in (1, 2, 3)]
            return merge(merge(stats, got[0]), merge(got[1], got[2]))
    while step < size:
        stats = merge(stats, lax.ppermute(stats, axis, by_xor(size, step)))
        step *= 2
    return stats


def hold_kernel(*refs):
    pass


def hold(arrays, until):
    anywhere = pl.BlockSpec(memory_space=pl.ANY)
    return pl.pallas_call(
        hold_kernel,
        out_shape=tuple(jax.ShapeDtypeStruct(a.shape, a.dtype) for a in arrays),
        in_specs=[anywhere] * (len(arrays) + len(until)),
        out_specs=(anywhere,) * len(arrays),
        input_output_aliases={i: i for i in range(len(arrays))},
        compiler_params=pltpu.CompilerParams(vmem_limit_bytes=1024 * 1024),
        cost_estimate=pl.CostEstimate(flops=0, bytes_accessed=0, transcendentals=0),
    )(*arrays, *until)


def gather(operators, turned, nz):
    def send(x, step):
        return lax.ppermute(x, "blk", by_xor(nz, step))

    if nz == 4:
        km_2, km_1 = send(operators, 2), send(operators, 1)
        t_2, t_1 = send(turned, 2), send(turned, 1)
        (km_2,) = hold((km_2,), (km_1,))
        km_3 = send(km_2, 1)
        (t_2,) = hold((t_2,), (t_1,))
        return [operators, km_1, km_2, km_3], [turned, t_1, t_2, send(t_2, 1)]
    parts, far = {0: (operators, turned)}, nz // 2
    while far:
        parts |= {k ^ far: tuple(send(x, far) for x in held) for k, held in parts.items()}
        far //= 2
    return [[parts[k][i] for k in range(nz)] for i in range(2)]


def body(basis, coeffs, stiff_blocks, mass_blocks, block_cols):
    nz, ng = lax.axis_size("blk"), lax.axis_size("grp")
    current = basis[0]
    edge, columns = current.shape
    slots = block_cols.shape[-1]
    modes = columns // 3
    rows = edge * nz
    total_rows = rows * ng
    width = columns // nz

    payload = jnp.concatenate(
        [
            stiff_blocks[0, 0].reshape(slots * edge, edge),
            mass_blocks[0, 0].reshape(slots * edge, edge),
        ],
        axis=0,
    )
    turned = turn_first(block_cols[0], current, coeffs, modes)
    km_parts, t_parts = gather(payload, turned, nz)

    cols = jnp.stack([p[2 * modes, :slots] for p in t_parts]).astype(jnp.int32)
    some = jax.ShapeDtypeStruct((nz - 1, edge, modes), f32)
    last = jax.ShapeDtypeStruct((edge, modes), f32)
    stats_shape = jax.ShapeDtypeStruct((3, modes), f32)
    work = 4 * edge * slots * edge * modes
    placed, stiff_some, mass_some = call(
        functools.partial(rows_kernel, nz, slots, edge, modes),
        [cols, *t_parts, *km_parts[:-1]],
        1,
        (jax.ShapeDtypeStruct((rows, 2 * modes), bf16), some, some),
        [],
        (nz - 1) * work,
    )
    fetched = [pltpu.SMEM((nz, slots), jnp.int32), pltpu.SemaphoreType.DMA(())]
    stiff_last, mass_last, stats = call(
        functools.partial(stats_kernel, nz, slots, edge, modes),
        [cols, km_parts[-1], placed, stiff_some, mass_some],
        0,
        (last, last, stats_shape),
        [pltpu.VMEM((nz, 8, modes), f32), *fetched],
        work,
        n_any=1,
    )
    stats = merge_over("grp", ng, stats)
    early = call(
        functools.partial(early_turn_kernel, modes),
        [placed, coeffs],
        0,
        jax.ShapeDtypeStruct((rows, 2 * modes), f32),
        [],
        8 * rows * modes * modes,
    )
    turned, stiff_x, mass_x, stats = call(
        functools.partial(sweep_kernel, nz, slots, edge, modes, total_rows),
        [cols, *km_parts, early, stiff_some, mass_some, stiff_last, mass_last, stats, coeffs],
        0,
        (
            jax.ShapeDtypeStruct((rows, 2 * modes), bf16),
            jax.ShapeDtypeStruct((rows, modes), f32),
            jax.ShapeDtypeStruct((rows, modes), f32),
            stats_shape,
        ),
        [pltpu.VMEM((rows, modes), bf16), pltpu.VMEM((nz, 8, modes), f32), *fetched],
        4 * rows * modes * modes + nz * work,
        n_any=1,
    )
    stats = merge_over("grp", ng, stats)

    chips = ng // 2
    block = columns // ng
    bounds = []
    if block % 32 == 16 and width % 128 == 32:
        first_rows = (block + 16) // 32 * 16
        bounds = [(0, first_rows), (first_rows, block)]
    gram_shapes = tuple(
        jax.ShapeDtypeStruct((chips, (high - low) * 2 * width // 128, 128), bf16)
        for low, high in bounds
    ) or (jax.ShapeDtypeStruct((columns, 2 * width), bf16),)
    window = -(-(width + max(i * width % 128 for i in range(nz))) // 128) * 128
    *grams, full, full_t, applied = call(
        functools.partial(gram_kernel, nz, chips, slots, edge, modes, total_rows, bounds),
        [cols, *km_parts, turned, stiff_x, mass_x, stats],
        0,
        (
            *gram_shapes,
            jax.ShapeDtypeStruct((rows, columns), bf16),
            jax.ShapeDtypeStruct((columns, rows), bf16),
            jax.ShapeDtypeStruct((rows, 2 * width), bf16),
        ),
        [pltpu.VMEM((rows, window), bf16), *fetched],
        2 * rows * columns * width,
        n_any=1,
    )
    basis_out, ritz = call(
        functools.partial(results_kernel, edge, total_rows),
        [stats, full],
        0,
        (jax.ShapeDtypeStruct((edge, columns), bf16), jax.ShapeDtypeStruct((1, modes), f32)),
        [],
        0,
    )
    if bounds:
        got = [lax.ppermute(x, "grp", by_xor(ng, 1)) for x in grams]
        keep = call(
            functools.partial(gram_rest_kernel, chips, bounds),
            [full_t, applied],
            0,
            gram_shapes,
            [],
            2 * rows * columns * width,
        )
        pieces = []
        for one, two in zip(keep, got):
            mine = (one.astype(f32) + two.astype(f32)).astype(bf16)
            pieces += [mine[0]] + [
                lax.ppermute(mine[k], "grp", by_xor(ng, 2 * k)) for k in range(1, chips)
            ]
        total = call(
            functools.partial(finish_kernel, bounds, width),
            pieces,
            0,
            jax.ShapeDtypeStruct((block, 2, width), f32),
            [],
            0,
        )
    else:
        total = lax.psum_scatter(grams[0], "grp", scatter_dimension=0, tiled=True)
        total = total.astype(f32).reshape(block, 2, width)
    return (basis_out[None], ritz[0], total)


def solution(mesh):
    in_specs = (
        P("grp", "blk", None),
        P(),
        P("grp", "blk", None, None, None),
        P("grp", "blk", None, None, None),
        P("grp", "blk", None),
    )
    out_specs = (P("grp", "blk", None), P(), P("grp", None, "blk"))
    return jax.shard_map(body, mesh=mesh, in_specs=in_specs, out_specs=out_specs, check_vma=False)
```

```python
import functools

import jax
import jax.numpy as jnp
from jax import lax
from jax.experimental import pallas as pl
from jax.experimental.pallas import tpu as pltpu
from jax.sharding import PartitionSpec as P

epsilon = 1e-06
tiny = 1e-30
f32 = jnp.float32
bf16 = jnp.bfloat16
VMEM_BYTES = 24 * 1024 * 1024
FIRST_VMEM_BYTES = 58 * 1024 * 1024


def vmem():
    return pl.BlockSpec(memory_space=pltpu.VMEM)


def smem():
    return pl.BlockSpec(memory_space=pltpu.SMEM)


def block_dot(pieces_k, slots, edge, cols, k, field, lanes):
    half = slots * edge
    top = jnp.concatenate([pieces_k[s * edge : (s + 1) * edge, :] for s in range(slots)], axis=1)
    low = jnp.concatenate(
        [pieces_k[half + s * edge : half + (s + 1) * edge, :] for s in range(slots)], axis=1
    )
    rows = [
        field[pl.ds(pl.multiple_of(cols[k, s] * edge, edge), edge), lanes] for s in range(slots)
    ]
    return jnp.dot(
        jnp.concatenate([top, low], axis=0),
        jnp.concatenate(rows, axis=0),
        preferred_element_type=f32,
    )


def shift_and_scale(stats, total_rows):
    num, den, about = stats[0:1, :], stats[1:2, :], stats[2:3, :]
    shift = num / (den + epsilon)
    off = shift - num / jnp.maximum(den, tiny)
    scale = lax.rsqrt((about + off * off * den) / total_rows + epsilon)
    return shift, scale


def block_dot(pieces_k, slots, edge, cols, k, field, lanes):
    half = slots * edge
    top = jnp.concatenate([pieces_k[s * edge : (s + 1) * edge, :] for s in range(slots)], axis=1)
    low = jnp.concatenate(
        [pieces_k[half + s * edge : half + (s + 1) * edge, :] for s in range(slots)], axis=1
    )
    rows = [
        field[pl.ds(pl.multiple_of(cols[k, s] * edge, edge), edge), lanes] for s in range(slots)
    ]
    return jnp.dot(
        jnp.concatenate([top, low], axis=0),
        jnp.concatenate(rows, axis=0),
        preferred_element_type=f32,
    )


def column_stats(stiff_x, mass_x):
    num = jnp.sum(stiff_x * mass_x, axis=0, keepdims=True)
    den = jnp.sum(mass_x * mass_x, axis=0, keepdims=True)
    rest = stiff_x - (num / jnp.maximum(den, tiny)) * mass_x
    return num, den, jnp.sum(rest * rest, axis=0, keepdims=True)


def shift_and_scale(stats, total_rows):
    num, den, about = stats[0:1, :], stats[1:2, :], stats[2:3, :]
    shift = num / (den + epsilon)
    off = shift - num / jnp.maximum(den, tiny)
    scale = lax.rsqrt((about + off * off * den) / total_rows + epsilon)
    return shift, scale


def hbm():
    return pl.BlockSpec(memory_space=pltpu.HBM)


def turn_kernel(chunks, copies_each, cols_hbm, current_hbm, coeffs_hbm, out_ref, current, coeffs, cols, sems):
    depth = current.shape[1] // chunks
    piece = depth // copies_each
    copies = [pltpu.make_async_copy(current_hbm, current, sems.at[0])]
    for c in range(chunks * copies_each):
        part = pl.ds(c * piece, piece)
        copies.append(pltpu.make_async_copy(coeffs_hbm.at[0, part], coeffs.at[part], sems.at[c + 1]))
    copies.append(pltpu.make_async_copy(cols_hbm, cols, sems.at[chunks * copies_each + 1]))
    for copy in copies:
        copy.start()
    rows, edge = current.shape[0], out_ref.shape[1]
    copies[0].wait()
    turned = None
    for c in range(chunks):
        for d in range(copies_each):
            copies[c * copies_each + d + 1].wait()
        part = slice(c * depth, (c + 1) * depth)
        more = jnp.dot(current[:, part], coeffs[part, :], preferred_element_type=f32)
        turned = more if turned is None else turned + more
    copies[-1].wait()
    lane = lax.broadcasted_iota(jnp.int32, (16, edge), 1)
    tag = jnp.zeros((16, edge), jnp.int32)
    for s in range(cols.shape[1]):
        tag = jnp.where(lane == s, cols[0, s], tag)
    turned = turned.astype(bf16)
    blocks = turned.shape[1] // edge
    for b in range(blocks):
        out_ref[b * rows : (b + 1) * rows, :] = turned[:, b * edge : (b + 1) * edge]
    out_ref[blocks * rows : blocks * rows + 16, :] = tag.astype(f32).astype(bf16)


def turn_first(cols, current, coeffs, modes):
    rows, columns = current.shape
    chunks, copies_each = 3, 2
    in_hbm = pl.BlockSpec(memory_space=pltpu.HBM)
    return pl.pallas_call(
        functools.partial(turn_kernel, chunks, copies_each),
        out_shape=pltpu.VMEM((2 * modes + 16, rows), bf16),
        in_specs=[in_hbm, in_hbm, in_hbm],
        out_specs=vmem(),
        scratch_shapes=[
            pltpu.VMEM((rows, columns), bf16),
            pltpu.VMEM((columns, 2 * modes), bf16),
            pltpu.SMEM(cols.shape, jnp.int32),
            pltpu.SemaphoreType.DMA((chunks * copies_each + 2,)),
        ],
        compiler_params=pltpu.CompilerParams(vmem_limit_bytes=FIRST_VMEM_BYTES),
        cost_estimate=pl.CostEstimate(
            flops=4 * rows * columns * modes, bytes_accessed=4 * columns * modes, transcendentals=0
        ),
    )(cols, current, coeffs)


def rows_kernel(nz, slots, edge, modes, cols, *refs):
    t_refs, km_refs = refs[:nz], refs[nz : 2 * nz - 1]
    placed, stiff_ref, mass_ref = refs[2 * nz - 1 :]
    z = lax.axis_index("blk")
    for k in range(nz):
        at = pl.ds(pl.multiple_of((z ^ k) * edge, edge), edge)
        for b in range(placed.shape[1] // edge):
            placed[at, b * edge : (b + 1) * edge] = t_refs[k][b * edge : (b + 1) * edge, :]
    for k in range(nz - 1):
        both = block_dot(km_refs[k], slots, edge, cols, k, placed, slice(0, modes))
        stiff_ref[k] = both[:edge]
        mass_ref[k] = both[edge:]


def block_products(place, stiff_x, mass_x, sums):
    sums[place, 0:1, :] = jnp.sum(stiff_x * mass_x, axis=0, keepdims=True)
    sums[place, 1:2, :] = jnp.sum(mass_x * mass_x, axis=0, keepdims=True)


def block_stats(z, pairs, sums, stats_ref):
    total = sums[0]
    for r in range(1, len(pairs)):
        total = total + sums[r]
    own_shift = total[0:1, :] / jnp.maximum(total[1:2, :], tiny)
    for k, (stiff_x, mass_x) in enumerate(pairs):
        rest = stiff_x - own_shift * mass_x
        sums[z ^ k, 2:3, :] = jnp.sum(rest * rest, axis=0, keepdims=True)
    about = sums[0, 2:3, :]
    for r in range(1, len(pairs)):
        about = about + sums[r, 2:3, :]
    stats_ref[0:2, :] = total[0:2, :]
    stats_ref[2:3, :] = about


def stats_kernel(
    nz, slots, edge, modes, cols_ref, km_last, placed, stiff, mass, stiff_ref, mass_ref, stats_ref, sums, cols, sem
):
    fetch = pltpu.make_async_copy(cols_ref, cols, sem)
    fetch.start()
    z = lax.axis_index("blk")
    sums[...] = jnp.zeros_like(sums)
    for k in range(nz - 1):
        block_products(z ^ k, stiff[k], mass[k], sums)
    fetch.wait()
    both = block_dot(km_last, slots, edge, cols, nz - 1, placed, slice(0, modes))
    stiff_ref[...] = both[:edge]
    mass_ref[...] = both[edge:]
    block_products(z ^ (nz - 1), both[:edge], both[edge:], sums)
    pairs = [(stiff[k], mass[k]) for k in range(nz - 1)] + [(both[:edge], both[edge:])]
    block_stats(z, pairs, sums, stats_ref)


def early_turn_kernel(modes, placed, coeffs, out_ref):
    out_ref[...] = jnp.dot(
        placed[:, :modes], coeffs[1, :modes, :], preferred_element_type=f32
    ) + jnp.dot(placed[:, modes:], coeffs[1, 2 * modes :, :], preferred_element_type=f32)


def sweep_kernel(nz, slots, edge, modes, total_rows, cols_ref, *refs):
    *refs, cols, sem = refs
    fetch = pltpu.make_async_copy(cols_ref, cols, sem)
    fetch.start()
    km_refs = refs[:nz]
    early, stiff, mass, stiff_last, mass_last, stats, coeffs = refs[nz : nz + 7]
    turned_ref, stiff_ref, mass_ref, stats_ref, search, sums = refs[nz + 7 :]
    z = lax.axis_index("blk")
    at = [pl.ds(pl.multiple_of((z ^ k) * edge, edge), edge) for k in range(nz)]
    shift, scale = shift_and_scale(stats, total_rows)
    for k in range(nz):
        stiff_x = stiff[k] if k < nz - 1 else stiff_last[...]
        mass_x = mass[k] if k < nz - 1 else mass_last[...]
        search[at[k], :] = ((stiff_x - shift * mass_x) * scale).astype(bf16)
    late = jnp.dot(search[...], coeffs[1, modes : 2 * modes, :], preferred_element_type=f32)
    turned_ref[...] = (early[...] + late).astype(bf16)
    sums[...] = jnp.zeros_like(sums)
    fetch.wait()
    pairs = []
    for k in range(nz):
        both = block_dot(km_refs[k], slots, edge, cols, k, turned_ref, slice(0, modes))
        stiff_ref[at[k], :] = both[:edge]
        mass_ref[at[k], :] = both[edge:]
        block_products(z ^ k, both[:edge], both[edge:], sums)
        pairs.append((both[:edge], both[edge:]))
    block_stats(z, pairs, sums, stats_ref)


def dense_order(width):
    whole = width // 128 * 128
    return [(0, 0, whole), (1, 0, whole), (0, whole, width), (1, whole, width)]


def gram_rows(full_t, applied, chips, core, bounds, out_refs):
    chip = lax.div(lax.axis_index("grp"), 2)
    block = full_t.shape[0] // (2 * chips)
    rows = [
        full_t[pl.ds(pl.multiple_of((2 * j + core) * block, 16), block), :] for j in range(chips)
    ]
    gram = jnp.dot(jnp.concatenate(rows, axis=0), applied[...], preferred_element_type=f32)
    whole = gram.shape[1] // 128
    for (low, high), out_ref in zip(bounds, out_refs):
        size = high - low
        for j in range(chips):
            mine = gram[j * block + low : j * block + high]
            for b in range(whole):
                part = mine[:, b * 128 : (b + 1) * 128].astype(bf16)
                out_ref[j ^ chip, b * size : (b + 1) * size, :] = part
            left = mine[:, whole * 128 :]
            left = jnp.concatenate([left[: size // 2], left[size // 2 :]], axis=1).astype(bf16)
            out_ref[j ^ chip, whole * size : whole * size + size // 2, :] = left


def finish_kernel(bounds, width, *refs):
    *refs, out_hbm, out_ref, sems = refs
    each = len(refs) // len(bounds)
    whole = width // 128
    writes = []
    for i, (low, high) in enumerate(bounds):
        size = high - low
        total = refs[i * each][...].astype(f32)
        for ref in refs[i * each + 1 : (i + 1) * each]:
            total = total + ref[...].astype(f32)
        left = total[2 * whole * size :, :]
        left = jnp.concatenate([left[:, :64], left[:, 64:]], axis=0)
        for op in range(2):
            for b in range(whole):
                at = (op * whole + b) * size
                out_ref[low:high, op, b * 128 : (b + 1) * 128] = total[at : at + size]
            out_ref[low:high, op, whole * 128 :] = left[:, op * 32 : (op + 1) * 32]
        part = pl.ds(low, size)
        writes.append(pltpu.make_async_copy(out_ref.at[part], out_hbm.at[part], sems.at[i]))
        writes[-1].start()
    for write in writes:
        write.wait()


def gram_kernel(nz, chips, slots, edge, modes, total_rows, bounds, cols_ref, *refs):
    *refs, cols, sem = refs
    fetch = pltpu.make_async_copy(cols_ref, cols, sem)
    fetch.start()
    km_refs = refs[:nz]
    turned, stiff, mass, stats = refs[nz : nz + 4]
    *gram_refs, full, full_t, applied, chosen = refs[nz + 4 :]
    z = lax.axis_index("blk")
    at = [pl.ds(pl.multiple_of((z ^ k) * edge, edge), edge) for k in range(nz)]
    width = 3 * modes // nz
    shift, scale = shift_and_scale(stats, total_rows)
    full[:, 0:modes] = turned[:, 0:modes]
    full[:, modes : 2 * modes] = ((stiff[...] - shift * mass[...]) * scale).astype(bf16)
    full[:, 2 * modes : 3 * modes] = turned[:, modes : 2 * modes]
    full_t[...] = full[...].T
    window = chosen.shape[1]
    start = z * width // 128 * 128
    picked = full[:, pl.ds(pl.multiple_of(start, 128), window)].astype(f32)
    chosen[...] = pltpu.roll(picked, window - (z * width - start), 1).astype(bf16)
    fetch.wait()
    for k in range(nz):
        both = block_dot(km_refs[k], slots, edge, cols, k, chosen, slice(0, width)).astype(bf16)
        column = 0
        for op, first, last in dense_order(width) if bounds else [(0, 0, width), (1, 0, width)]:
            part = both[op * edge : (op + 1) * edge, first:last]
            applied[at[k], column : column + last - first] = part
            column += last - first
    if bounds:
        other = 1 - lax.rem(lax.axis_index("grp"), 2)
        gram_rows(full_t, applied, chips, other, bounds, gram_refs)
    else:
        gram_refs[0][...] = jnp.dot(full_t[...], applied[...], preferred_element_type=f32).astype(bf16)


def results_kernel(edge, total_rows, stats, full, basis_ref, ritz_ref):
    z = lax.axis_index("blk")
    basis_ref[...] = full[pl.ds(pl.multiple_of(z * edge, edge), edge), :]
    ritz_ref[...] = shift_and_scale(stats, total_rows)[0]


def gram_rest_kernel(chips, bounds, full_t, applied, *gram_refs):
    own = lax.rem(lax.axis_index("grp"), 2)
    gram_rows(full_t, applied, chips, own, bounds, gram_refs)


def call(kernel, inputs, n_smem, out_shape, scratch, flops, n_any=0):
    return pl.pallas_call(
        kernel,
        out_shape=out_shape,
        in_specs=[smem()] * n_smem
        + [pl.BlockSpec(memory_space=pl.ANY)] * n_any
        + [vmem()] * (len(inputs) - n_smem - n_any),
        out_specs=jax.tree.map(lambda _: vmem(), out_shape),
        scratch_shapes=scratch,
        compiler_params=pltpu.CompilerParams(vmem_limit_bytes=VMEM_BYTES),
        cost_estimate=pl.CostEstimate(flops=flops, bytes_accessed=4_000_000, transcendentals=0),
    )(*inputs)


def by_xor(size, k):
    return [(i, i ^ k) for i in range(size)]


def merge(one, two):
    num, den = one[0] + two[0], one[1] + two[1]
    apart = one[0] / jnp.maximum(one[1], tiny) - two[0] / jnp.maximum(two[1], tiny)
    weight = jnp.sqrt(one[1]) * jnp.sqrt(two[1]) * lax.rsqrt(jnp.maximum(den, tiny))
    gap = apart * weight
    return jnp.stack([num, den, (one[2] + two[2]) + gap * gap])


def merge_over(axis, size, stats):
    step = 1
    if axis == "grp" and size >= 8:
        stats = merge(stats, lax.ppermute(stats, axis, by_xor(size, 1)))
        step = 2
        if size == 8:
            got = [lax.ppermute(stats, axis, by_xor(size, 2 * k)) for k in (1, 2, 3)]
            return merge(merge(stats, got[0]), merge(got[1], got[2]))
    while step < size:
        stats = merge(stats, lax.ppermute(stats, axis, by_xor(size, step)))
        step *= 2
    return stats


def hold_kernel(*refs):
    pass


def hold(arrays, until):
    anywhere = pl.BlockSpec(memory_space=pl.ANY)
    return pl.pallas_call(
        hold_kernel,
        out_shape=tuple(jax.ShapeDtypeStruct(a.shape, a.dtype) for a in arrays),
        in_specs=[anywhere] * (len(arrays) + len(until)),
        out_specs=(anywhere,) * len(arrays),
        input_output_aliases={i: i for i in range(len(arrays))},
        compiler_params=pltpu.CompilerParams(vmem_limit_bytes=1024 * 1024),
        cost_estimate=pl.CostEstimate(flops=0, bytes_accessed=0, transcendentals=0),
    )(*arrays, *until)


def gather(operators, turned, nz):
    def send(x, step):
        return lax.ppermute(x, "blk", by_xor(nz, step))

    if nz == 4:
        km_2, km_1 = send(operators, 2), send(operators, 1)
        t_2, t_1 = send(turned, 2), send(turned, 1)
        (km_2,) = hold((km_2,), (km_1,))
        km_3 = send(km_2, 1)
        (t_2,) = hold((t_2,), (t_1,))
        return [operators, km_1, km_2, km_3], [turned, t_1, t_2, send(t_2, 1)]
    parts, far = {0: (operators, turned)}, nz // 2
    while far:
        parts |= {k ^ far: tuple(send(x, far) for x in held) for k, held in parts.items()}
        far //= 2
    return [[parts[k][i] for k in range(nz)] for i in range(2)]


def body(basis, coeffs, stiff_blocks, mass_blocks, block_cols):
    nz, ng = lax.axis_size("blk"), lax.axis_size("grp")
    current = basis[0]
    edge, columns = current.shape
    slots = block_cols.shape[-1]
    modes = columns // 3
    rows = edge * nz
    total_rows = rows * ng
    width = columns // nz

    payload = jnp.concatenate(
        [
            stiff_blocks[0, 0].reshape(slots * edge, edge),
            mass_blocks[0, 0].reshape(slots * edge, edge),
        ],
        axis=0,
    )
    turned = turn_first(block_cols[0], current, coeffs, modes)
    km_parts, t_parts = gather(payload, turned, nz)

    cols = jnp.stack([p[2 * modes, :slots] for p in t_parts]).astype(jnp.int32)
    some = jax.ShapeDtypeStruct((nz - 1, edge, modes), f32)
    last = jax.ShapeDtypeStruct((edge, modes), f32)
    stats_shape = jax.ShapeDtypeStruct((3, modes), f32)
    work = 4 * edge * slots * edge * modes
    placed, stiff_some, mass_some = call(
        functools.partial(rows_kernel, nz, slots, edge, modes),
        [cols, *t_parts, *km_parts[:-1]],
        1,
        (jax.ShapeDtypeStruct((rows, 2 * modes), bf16), some, some),
        [],
        (nz - 1) * work,
    )
    fetched = [pltpu.SMEM((nz, slots), jnp.int32), pltpu.SemaphoreType.DMA(())]
    stiff_last, mass_last, stats = call(
        functools.partial(stats_kernel, nz, slots, edge, modes),
        [cols, km_parts[-1], placed, stiff_some, mass_some],
        0,
        (last, last, stats_shape),
        [pltpu.VMEM((nz, 8, modes), f32), *fetched],
        work,
        n_any=1,
    )
    stats = merge_over("grp", ng, stats)
    early = call(
        functools.partial(early_turn_kernel, modes),
        [placed, coeffs],
        0,
        jax.ShapeDtypeStruct((rows, 2 * modes), f32),
        [],
        8 * rows * modes * modes,
    )
    turned, stiff_x, mass_x, stats = call(
        functools.partial(sweep_kernel, nz, slots, edge, modes, total_rows),
        [cols, *km_parts, early, stiff_some, mass_some, stiff_last, mass_last, stats, coeffs],
        0,
        (
            jax.ShapeDtypeStruct((rows, 2 * modes), bf16),
            jax.ShapeDtypeStruct((rows, modes), f32),
            jax.ShapeDtypeStruct((rows, modes), f32),
            stats_shape,
        ),
        [pltpu.VMEM((rows, modes), bf16), pltpu.VMEM((nz, 8, modes), f32), *fetched],
        4 * rows * modes * modes + nz * work,
        n_any=1,
    )
    stats = merge_over("grp", ng, stats)

    chips = ng // 2
    block = columns // ng
    bounds = []
    if block % 32 == 16 and width % 128 == 32:
        first_rows = (block + 16) // 32 * 16
        bounds = [(0, first_rows), (first_rows, block)]
    gram_shapes = tuple(
        jax.ShapeDtypeStruct((chips, (high - low) * 2 * width // 128, 128), bf16)
        for low, high in bounds
    ) or (jax.ShapeDtypeStruct((columns, 2 * width), bf16),)
    window = -(-(width + max(i * width % 128 for i in range(nz))) // 128) * 128
    *grams, full, full_t, applied = call(
        functools.partial(gram_kernel, nz, chips, slots, edge, modes, total_rows, bounds),
        [cols, *km_parts, turned, stiff_x, mass_x, stats],
        0,
        (
            *gram_shapes,
            jax.ShapeDtypeStruct((rows, columns), bf16),
            jax.ShapeDtypeStruct((columns, rows), bf16),
            jax.ShapeDtypeStruct((rows, 2 * width), bf16),
        ),
        [pltpu.VMEM((rows, window), bf16), *fetched],
        2 * rows * columns * width,
        n_any=1,
    )
    basis_out, ritz = call(
        functools.partial(results_kernel, edge, total_rows),
        [stats, full],
        0,
        (jax.ShapeDtypeStruct((edge, columns), bf16), jax.ShapeDtypeStruct((1, modes), f32)),
        [],
        0,
    )
    if bounds:
        got = [lax.ppermute(x, "grp", by_xor(ng, 1)) for x in grams]
        keep = call(
            functools.partial(gram_rest_kernel, chips, bounds),
            [full_t, applied],
            0,
            gram_shapes,
            [],
            2 * rows * columns * width,
        )
        pieces = []
        for one, two in zip(keep, got):
            mine = (one.astype(f32) + two.astype(f32)).astype(bf16)
            pieces += [mine[0]] + [
                lax.ppermute(mine[k], "grp", by_xor(ng, 2 * k)) for k in range(1, chips)
            ]
        total = pl.pallas_call(
            functools.partial(finish_kernel, bounds, width),
            out_shape=jax.ShapeDtypeStruct((block, 2, width), f32),
            in_specs=[vmem()] * len(pieces),
            out_specs=pl.BlockSpec(memory_space=pl.ANY),
            scratch_shapes=[
                pltpu.VMEM((block, 2, width), f32),
                pltpu.SemaphoreType.DMA((len(bounds),)),
            ],
            compiler_params=pltpu.CompilerParams(vmem_limit_bytes=VMEM_BYTES),
        )(*pieces)
    else:
        total = lax.psum_scatter(grams[0], "grp", scatter_dimension=0, tiled=True)
        total = total.astype(f32).reshape(block, 2, width)
    return (basis_out[None], ritz[0], total)


def solution(mesh):
    in_specs = (
        P("grp", "blk", None),
        P(),
        P("grp", "blk", None, None, None),
        P("grp", "blk", None, None, None),
        P("grp", "blk", None),
    )
    out_specs = (P("grp", "blk", None), P(), P("grp", None, "blk"))
    return jax.shard_map(body, mesh=mesh, in_specs=in_specs, out_specs=out_specs, check_vma=False)
```

```python
import functools

import jax
import jax.numpy as jnp
from jax import lax
from jax.experimental import pallas as pl
from jax.experimental.pallas import tpu as pltpu
from jax.sharding import PartitionSpec as P

epsilon = 1e-06
tiny = 1e-30
f32 = jnp.float32
bf16 = jnp.bfloat16
VMEM_BYTES = 24 * 1024 * 1024
FIRST_VMEM_BYTES = 58 * 1024 * 1024


def vmem():
    return pl.BlockSpec(memory_space=pltpu.VMEM)


def smem():
    return pl.BlockSpec(memory_space=pltpu.SMEM)


def block_dot(pieces_k, slots, edge, cols, k, field, lanes):
    half = slots * edge
    top = jnp.concatenate([pieces_k[s * edge : (s + 1) * edge, :] for s in range(slots)], axis=1)
    low = jnp.concatenate(
        [pieces_k[half + s * edge : half + (s + 1) * edge, :] for s in range(slots)], axis=1
    )
    rows = [
        field[pl.ds(pl.multiple_of(cols[k, s] * edge, edge), edge), lanes] for s in range(slots)
    ]
    return jnp.dot(
        jnp.concatenate([top, low], axis=0),
        jnp.concatenate(rows, axis=0),
        preferred_element_type=f32,
    )


def merge_parts(one, two):
    num, den = one[0] + two[0], one[1] + two[1]
    apart = one[0] / jnp.maximum(one[1], tiny) - two[0] / jnp.maximum(two[1], tiny)
    weight = jnp.sqrt(one[1]) * jnp.sqrt(two[1]) * lax.rsqrt(jnp.maximum(den, tiny))
    gap = apart * weight
    return num, den, (one[2] + two[2]) + gap * gap


def own_stats(stiff_x, mass_x):
    num = jnp.sum(stiff_x * mass_x, axis=0, keepdims=True)
    den = jnp.sum(mass_x * mass_x, axis=0, keepdims=True)
    rest = stiff_x - (num / jnp.maximum(den, tiny)) * mass_x
    return num, den, jnp.sum(rest * rest, axis=0, keepdims=True)


def shift_and_scale(stats, total_rows):
    num, den, about = stats[0:1, :], stats[1:2, :], stats[2:3, :]
    shift = num / (den + epsilon)
    off = shift - num / jnp.maximum(den, tiny)
    scale = lax.rsqrt((about + off * off * den) / total_rows + epsilon)
    return shift, scale


def block_dot(pieces_k, slots, edge, cols, k, field, lanes):
    half = slots * edge
    top = jnp.concatenate([pieces_k[s * edge : (s + 1) * edge, :] for s in range(slots)], axis=1)
    low = jnp.concatenate(
        [pieces_k[half + s * edge : half + (s + 1) * edge, :] for s in range(slots)], axis=1
    )
    rows = [
        field[pl.ds(pl.multiple_of(cols[k, s] * edge, edge), edge), lanes] for s in range(slots)
    ]
    return jnp.dot(
        jnp.concatenate([top, low], axis=0),
        jnp.concatenate(rows, axis=0),
        preferred_element_type=f32,
    )


def column_stats(stiff_x, mass_x):
    num = jnp.sum(stiff_x * mass_x, axis=0, keepdims=True)
    den = jnp.sum(mass_x * mass_x, axis=0, keepdims=True)
    rest = stiff_x - (num / jnp.maximum(den, tiny)) * mass_x
    return num, den, jnp.sum(rest * rest, axis=0, keepdims=True)


def shift_and_scale(stats, total_rows):
    num, den, about = stats[0:1, :], stats[1:2, :], stats[2:3, :]
    shift = num / (den + epsilon)
    off = shift - num / jnp.maximum(den, tiny)
    scale = lax.rsqrt((about + off * off * den) / total_rows + epsilon)
    return shift, scale


def hbm():
    return pl.BlockSpec(memory_space=pltpu.HBM)


def turn_kernel(chunks, copies_each, cols_hbm, current_hbm, coeffs_hbm, out_ref, current, coeffs, cols, sems):
    depth = current.shape[1] // chunks
    piece = depth // copies_each
    copies = [pltpu.make_async_copy(current_hbm, current, sems.at[0])]
    for c in range(chunks * copies_each):
        part = pl.ds(c * piece, piece)
        copies.append(pltpu.make_async_copy(coeffs_hbm.at[0, part], coeffs.at[part], sems.at[c + 1]))
    copies.append(pltpu.make_async_copy(cols_hbm, cols, sems.at[chunks * copies_each + 1]))
    for copy in copies:
        copy.start()
    rows, edge = current.shape[0], out_ref.shape[1]
    copies[0].wait()
    turned = None
    for c in range(chunks):
        for d in range(copies_each):
            copies[c * copies_each + d + 1].wait()
        part = slice(c * depth, (c + 1) * depth)
        more = jnp.dot(current[:, part], coeffs[part, :], preferred_element_type=f32)
        turned = more if turned is None else turned + more
    copies[-1].wait()
    lane = lax.broadcasted_iota(jnp.int32, (16, edge), 1)
    tag = jnp.zeros((16, edge), jnp.int32)
    for s in range(cols.shape[1]):
        tag = jnp.where(lane == s, cols[0, s], tag)
    turned = turned.astype(bf16)
    blocks = turned.shape[1] // edge
    for b in range(blocks):
        out_ref[b * rows : (b + 1) * rows, :] = turned[:, b * edge : (b + 1) * edge]
    out_ref[blocks * rows : blocks * rows + 16, :] = tag.astype(f32).astype(bf16)


def turn_first(cols, current, coeffs, modes):
    rows, columns = current.shape
    chunks, copies_each = 3, 2
    in_hbm = pl.BlockSpec(memory_space=pltpu.HBM)
    return pl.pallas_call(
        functools.partial(turn_kernel, chunks, copies_each),
        out_shape=pltpu.VMEM((2 * modes + 16, rows), bf16),
        in_specs=[in_hbm, in_hbm, in_hbm],
        out_specs=vmem(),
        scratch_shapes=[
            pltpu.VMEM((rows, columns), bf16),
            pltpu.VMEM((columns, 2 * modes), bf16),
            pltpu.SMEM(cols.shape, jnp.int32),
            pltpu.SemaphoreType.DMA((chunks * copies_each + 2,)),
        ],
        compiler_params=pltpu.CompilerParams(vmem_limit_bytes=FIRST_VMEM_BYTES),
        cost_estimate=pl.CostEstimate(
            flops=4 * rows * columns * modes, bytes_accessed=4 * columns * modes, transcendentals=0
        ),
    )(cols, current, coeffs)


def rows_kernel(nz, slots, edge, modes, cols, *refs):
    t_refs, km_refs = refs[:nz], refs[nz : 2 * nz - 1]
    placed, stiff_ref, mass_ref, some_ref = refs[2 * nz - 1 :]
    z = lax.axis_index("blk")
    for k in range(nz):
        at = pl.ds(pl.multiple_of((z ^ k) * edge, edge), edge)
        for b in range(placed.shape[1] // edge):
            placed[at, b * edge : (b + 1) * edge] = t_refs[k][b * edge : (b + 1) * edge, :]
    for k in range(nz - 1):
        both = block_dot(km_refs[k], slots, edge, cols, k, placed, slice(0, modes))
        stiff_ref[k] = both[:edge]
        mass_ref[k] = both[edge:]
        for row, value in enumerate(own_stats(both[:edge], both[edge:])):
            some_ref[k, row : row + 1, :] = value


def block_products(place, stiff_x, mass_x, sums):
    sums[place, 0:1, :] = jnp.sum(stiff_x * mass_x, axis=0, keepdims=True)
    sums[place, 1:2, :] = jnp.sum(mass_x * mass_x, axis=0, keepdims=True)


def block_stats(z, pairs, sums, stats_ref):
    total = sums[0]
    for r in range(1, len(pairs)):
        total = total + sums[r]
    own_shift = total[0:1, :] / jnp.maximum(total[1:2, :], tiny)
    for k, (stiff_x, mass_x) in enumerate(pairs):
        rest = stiff_x - own_shift * mass_x
        sums[z ^ k, 2:3, :] = jnp.sum(rest * rest, axis=0, keepdims=True)
    about = sums[0, 2:3, :]
    for r in range(1, len(pairs)):
        about = about + sums[r, 2:3, :]
    stats_ref[0:2, :] = total[0:2, :]
    stats_ref[2:3, :] = about


def stats_kernel(
    nz, slots, edge, modes, cols_ref, km_last, placed, some, stiff_ref, mass_ref, stats_ref, cols, sem
):
    fetch = pltpu.make_async_copy(cols_ref, cols, sem)
    fetch.start()
    parts = [tuple(some[k, r : r + 1, :] for r in range(3)) for k in range(nz - 1)]
    fetch.wait()
    both = block_dot(km_last, slots, edge, cols, nz - 1, placed, slice(0, modes))
    stiff_ref[...] = both[:edge]
    mass_ref[...] = both[edge:]
    parts.append(own_stats(both[:edge], both[edge:]))
    while len(parts) > 1:
        parts = [merge_parts(*parts[k : k + 2]) for k in range(0, len(parts), 2)]
    for row, value in enumerate(parts[0]):
        stats_ref[row : row + 1, :] = value


def early_turn_kernel(modes, placed, coeffs, out_ref):
    out_ref[...] = jnp.dot(
        placed[:, :modes], coeffs[1, :modes, :], preferred_element_type=f32
    ) + jnp.dot(placed[:, modes:], coeffs[1, 2 * modes :, :], preferred_element_type=f32)


def sweep_kernel(nz, slots, edge, modes, total_rows, cols_ref, *refs):
    *refs, cols, sem = refs
    fetch = pltpu.make_async_copy(cols_ref, cols, sem)
    fetch.start()
    km_refs = refs[:nz]
    early, stiff, mass, stiff_last, mass_last, stats, coeffs = refs[nz : nz + 7]
    turned_ref, stiff_ref, mass_ref, stats_ref, search, sums = refs[nz + 7 :]
    z = lax.axis_index("blk")
    at = [pl.ds(pl.multiple_of((z ^ k) * edge, edge), edge) for k in range(nz)]
    shift, scale = shift_and_scale(stats, total_rows)
    for k in range(nz):
        stiff_x = stiff[k] if k < nz - 1 else stiff_last[...]
        mass_x = mass[k] if k < nz - 1 else mass_last[...]
        search[at[k], :] = ((stiff_x - shift * mass_x) * scale).astype(bf16)
    late = jnp.dot(search[...], coeffs[1, modes : 2 * modes, :], preferred_element_type=f32)
    turned_ref[...] = (early[...] + late).astype(bf16)
    sums[...] = jnp.zeros_like(sums)
    fetch.wait()
    pairs = []
    for k in range(nz):
        both = block_dot(km_refs[k], slots, edge, cols, k, turned_ref, slice(0, modes))
        stiff_ref[at[k], :] = both[:edge]
        mass_ref[at[k], :] = both[edge:]
        block_products(z ^ k, both[:edge], both[edge:], sums)
        pairs.append((both[:edge], both[edge:]))
    block_stats(z, pairs, sums, stats_ref)


def dense_order(width):
    whole = width // 128 * 128
    return [(0, 0, whole), (1, 0, whole), (0, whole, width), (1, whole, width)]


def gram_rows(full_t, applied, chips, core, bounds, out_refs):
    chip = lax.div(lax.axis_index("grp"), 2)
    block = full_t.shape[0] // (2 * chips)
    rows = [
        full_t[pl.ds(pl.multiple_of((2 * j + core) * block, 16), block), :] for j in range(chips)
    ]
    gram = jnp.dot(jnp.concatenate(rows, axis=0), applied[...], preferred_element_type=f32)
    whole = gram.shape[1] // 128
    for (low, high), out_ref in zip(bounds, out_refs):
        size = high - low
        for j in range(chips):
            mine = gram[j * block + low : j * block + high]
            for b in range(whole):
                part = mine[:, b * 128 : (b + 1) * 128].astype(bf16)
                out_ref[j ^ chip, b * size : (b + 1) * size, :] = part
            left = mine[:, whole * 128 :]
            left = jnp.concatenate([left[: size // 2], left[size // 2 :]], axis=1).astype(bf16)
            out_ref[j ^ chip, whole * size : whole * size + size // 2, :] = left


def finish_kernel(bounds, width, *refs):
    *refs, out_hbm, out_ref, sems = refs
    each = len(refs) // len(bounds)
    whole = width // 128
    writes = []
    for i, (low, high) in enumerate(bounds):
        size = high - low
        total = refs[i * each][...].astype(f32)
        for ref in refs[i * each + 1 : (i + 1) * each]:
            total = total + ref[...].astype(f32)
        left = total[2 * whole * size :, :]
        left = jnp.concatenate([left[:, :64], left[:, 64:]], axis=0)
        for op in range(2):
            for b in range(whole):
                at = (op * whole + b) * size
                out_ref[low:high, op, b * 128 : (b + 1) * 128] = total[at : at + size]
            out_ref[low:high, op, whole * 128 :] = left[:, op * 32 : (op + 1) * 32]
        part = pl.ds(low, size)
        writes.append(pltpu.make_async_copy(out_ref.at[part], out_hbm.at[part], sems.at[i]))
        writes[-1].start()
    for write in writes:
        write.wait()


def gram_kernel(nz, chips, slots, edge, modes, total_rows, bounds, cols_ref, *refs):
    *refs, cols, sem = refs
    fetch = pltpu.make_async_copy(cols_ref, cols, sem)
    fetch.start()
    km_refs = refs[:nz]
    turned, stiff, mass, stats = refs[nz : nz + 4]
    *gram_refs, full, full_t, applied, chosen = refs[nz + 4 :]
    z = lax.axis_index("blk")
    at = [pl.ds(pl.multiple_of((z ^ k) * edge, edge), edge) for k in range(nz)]
    width = 3 * modes // nz
    shift, scale = shift_and_scale(stats, total_rows)
    full[:, 0:modes] = turned[:, 0:modes]
    full[:, modes : 2 * modes] = ((stiff[...] - shift * mass[...]) * scale).astype(bf16)
    full[:, 2 * modes : 3 * modes] = turned[:, modes : 2 * modes]
    full_t[...] = full[...].T
    window = chosen.shape[1]
    start = z * width // 128 * 128
    picked = full[:, pl.ds(pl.multiple_of(start, 128), window)].astype(f32)
    chosen[...] = pltpu.roll(picked, window - (z * width - start), 1).astype(bf16)
    fetch.wait()
    for k in range(nz):
        both = block_dot(km_refs[k], slots, edge, cols, k, chosen, slice(0, width)).astype(bf16)
        column = 0
        for op, first, last in dense_order(width) if bounds else [(0, 0, width), (1, 0, width)]:
            part = both[op * edge : (op + 1) * edge, first:last]
            applied[at[k], column : column + last - first] = part
            column += last - first
    if bounds:
        other = 1 - lax.rem(lax.axis_index("grp"), 2)
        gram_rows(full_t, applied, chips, other, bounds, gram_refs)
    else:
        gram_refs[0][...] = jnp.dot(full_t[...], applied[...], preferred_element_type=f32).astype(bf16)


def results_kernel(edge, total_rows, stats, full, basis_ref, ritz_ref):
    z = lax.axis_index("blk")
    basis_ref[...] = full[pl.ds(pl.multiple_of(z * edge, edge), edge), :]
    ritz_ref[...] = shift_and_scale(stats, total_rows)[0]


def gram_rest_kernel(chips, bounds, full_t, applied, *gram_refs):
    own = lax.rem(lax.axis_index("grp"), 2)
    gram_rows(full_t, applied, chips, own, bounds, gram_refs)


def call(kernel, inputs, n_smem, out_shape, scratch, flops, n_any=0):
    return pl.pallas_call(
        kernel,
        out_shape=out_shape,
        in_specs=[smem()] * n_smem
        + [pl.BlockSpec(memory_space=pl.ANY)] * n_any
        + [vmem()] * (len(inputs) - n_smem - n_any),
        out_specs=jax.tree.map(lambda _: vmem(), out_shape),
        scratch_shapes=scratch,
        compiler_params=pltpu.CompilerParams(vmem_limit_bytes=VMEM_BYTES),
        cost_estimate=pl.CostEstimate(flops=flops, bytes_accessed=4_000_000, transcendentals=0),
    )(*inputs)


def by_xor(size, k):
    return [(i, i ^ k) for i in range(size)]


def merge(one, two):
    return jnp.stack(merge_parts(one, two))


def merge_over(axis, size, stats):
    step = 1
    if axis == "grp" and size >= 8:
        stats = merge(stats, lax.ppermute(stats, axis, by_xor(size, 1)))
        step = 2
        if size == 8:
            got = [lax.ppermute(stats, axis, by_xor(size, 2 * k)) for k in (1, 2, 3)]
            return merge(merge(stats, got[0]), merge(got[1], got[2]))
    while step < size:
        stats = merge(stats, lax.ppermute(stats, axis, by_xor(size, step)))
        step *= 2
    return stats


def hold_kernel(*refs):
    pass


def hold(arrays, until):
    anywhere = pl.BlockSpec(memory_space=pl.ANY)
    return pl.pallas_call(
        hold_kernel,
        out_shape=tuple(jax.ShapeDtypeStruct(a.shape, a.dtype) for a in arrays),
        in_specs=[anywhere] * (len(arrays) + len(until)),
        out_specs=(anywhere,) * len(arrays),
        input_output_aliases={i: i for i in range(len(arrays))},
        compiler_params=pltpu.CompilerParams(vmem_limit_bytes=1024 * 1024),
        cost_estimate=pl.CostEstimate(flops=0, bytes_accessed=0, transcendentals=0),
    )(*arrays, *until)


def gather(operators, turned, nz):
    def send(x, step):
        return lax.ppermute(x, "blk", by_xor(nz, step))

    if nz == 4:
        km_2, km_1 = send(operators, 2), send(operators, 1)
        t_2, t_1 = send(turned, 2), send(turned, 1)
        (km_2,) = hold((km_2,), (km_1,))
        km_3 = send(km_2, 1)
        (t_2,) = hold((t_2,), (t_1,))
        return [operators, km_1, km_2, km_3], [turned, t_1, t_2, send(t_2, 1)]
    parts, far = {0: (operators, turned)}, nz // 2
    while far:
        parts |= {k ^ far: tuple(send(x, far) for x in held) for k, held in parts.items()}
        far //= 2
    return [[parts[k][i] for k in range(nz)] for i in range(2)]


def body(basis, coeffs, stiff_blocks, mass_blocks, block_cols):
    nz, ng = lax.axis_size("blk"), lax.axis_size("grp")
    current = basis[0]
    edge, columns = current.shape
    slots = block_cols.shape[-1]
    modes = columns // 3
    rows = edge * nz
    total_rows = rows * ng
    width = columns // nz

    payload = jnp.concatenate(
        [
            stiff_blocks[0, 0].reshape(slots * edge, edge),
            mass_blocks[0, 0].reshape(slots * edge, edge),
        ],
        axis=0,
    )
    turned = turn_first(block_cols[0], current, coeffs, modes)
    km_parts, t_parts = gather(payload, turned, nz)

    cols = jnp.stack([p[2 * modes, :slots] for p in t_parts]).astype(jnp.int32)
    some = jax.ShapeDtypeStruct((nz - 1, edge, modes), f32)
    last = jax.ShapeDtypeStruct((edge, modes), f32)
    stats_shape = jax.ShapeDtypeStruct((3, modes), f32)
    work = 4 * edge * slots * edge * modes
    placed, stiff_some, mass_some, stats_some = call(
        functools.partial(rows_kernel, nz, slots, edge, modes),
        [cols, *t_parts, *km_parts[:-1]],
        1,
        (
            jax.ShapeDtypeStruct((rows, 2 * modes), bf16),
            some,
            some,
            jax.ShapeDtypeStruct((nz - 1, 8, modes), f32),
        ),
        [],
        (nz - 1) * work,
    )
    fetched = [pltpu.SMEM((nz, slots), jnp.int32), pltpu.SemaphoreType.DMA(())]
    stiff_last, mass_last, stats = call(
        functools.partial(stats_kernel, nz, slots, edge, modes),
        [cols, km_parts[-1], placed, stats_some],
        0,
        (last, last, stats_shape),
        fetched,
        work,
        n_any=1,
    )
    stats = merge_over("grp", ng, stats)
    early = call(
        functools.partial(early_turn_kernel, modes),
        [placed, coeffs],
        0,
        jax.ShapeDtypeStruct((rows, 2 * modes), f32),
        [],
        8 * rows * modes * modes,
    )
    turned, stiff_x, mass_x, stats = call(
        functools.partial(sweep_kernel, nz, slots, edge, modes, total_rows),
        [cols, *km_parts, early, stiff_some, mass_some, stiff_last, mass_last, stats, coeffs],
        0,
        (
            jax.ShapeDtypeStruct((rows, 2 * modes), bf16),
            jax.ShapeDtypeStruct((rows, modes), f32),
            jax.ShapeDtypeStruct((rows, modes), f32),
            stats_shape,
        ),
        [pltpu.VMEM((rows, modes), bf16), pltpu.VMEM((nz, 8, modes), f32), *fetched],
        4 * rows * modes * modes + nz * work,
        n_any=1,
    )
    stats = merge_over("grp", ng, stats)

    chips = ng // 2
    block = columns // ng
    bounds = []
    if block % 32 == 16 and width % 128 == 32:
        first_rows = (block + 16) // 32 * 16
        bounds = [(0, first_rows), (first_rows, block)]
    gram_shapes = tuple(
        jax.ShapeDtypeStruct((chips, (high - low) * 2 * width // 128, 128), bf16)
        for low, high in bounds
    ) or (jax.ShapeDtypeStruct((columns, 2 * width), bf16),)
    window = -(-(width + max(i * width % 128 for i in range(nz))) // 128) * 128
    *grams, full, full_t, applied = call(
        functools.partial(gram_kernel, nz, chips, slots, edge, modes, total_rows, bounds),
        [cols, *km_parts, turned, stiff_x, mass_x, stats],
        0,
        (
            *gram_shapes,
            jax.ShapeDtypeStruct((rows, columns), bf16),
            jax.ShapeDtypeStruct((columns, rows), bf16),
            jax.ShapeDtypeStruct((rows, 2 * width), bf16),
        ),
        [pltpu.VMEM((rows, window), bf16), *fetched],
        2 * rows * columns * width,
        n_any=1,
    )
    basis_out, ritz = call(
        functools.partial(results_kernel, edge, total_rows),
        [stats, full],
        0,
        (jax.ShapeDtypeStruct((edge, columns), bf16), jax.ShapeDtypeStruct((1, modes), f32)),
        [],
        0,
    )
    if bounds:
        got = [lax.ppermute(x, "grp", by_xor(ng, 1)) for x in grams]
        keep = call(
            functools.partial(gram_rest_kernel, chips, bounds),
            [full_t, applied],
            0,
            gram_shapes,
            [],
            2 * rows * columns * width,
        )
        pieces = []
        for one, two in zip(keep, got):
            mine = (one.astype(f32) + two.astype(f32)).astype(bf16)
            pieces += [mine[0]] + [
                lax.ppermute(mine[k], "grp", by_xor(ng, 2 * k)) for k in range(1, chips)
            ]
        total = pl.pallas_call(
            functools.partial(finish_kernel, bounds, width),
            out_shape=jax.ShapeDtypeStruct((block, 2, width), f32),
            in_specs=[vmem()] * len(pieces),
            out_specs=pl.BlockSpec(memory_space=pl.ANY),
            scratch_shapes=[
                pltpu.VMEM((block, 2, width), f32),
                pltpu.SemaphoreType.DMA((len(bounds),)),
            ],
            compiler_params=pltpu.CompilerParams(vmem_limit_bytes=VMEM_BYTES),
        )(*pieces)
    else:
        total = lax.psum_scatter(grams[0], "grp", scatter_dimension=0, tiled=True)
        total = total.astype(f32).reshape(block, 2, width)
    return (basis_out[None], ritz[0], total)


def solution(mesh):
    in_specs = (
        P("grp", "blk", None),
        P(),
        P("grp", "blk", None, None, None),
        P("grp", "blk", None, None, None),
        P("grp", "blk", None),
    )
    out_specs = (P("grp", "blk", None), P(), P("grp", None, "blk"))
    return jax.shard_map(body, mesh=mesh, in_specs=in_specs, out_specs=out_specs, check_vma=False)
```

```python
import functools

import jax
import jax.numpy as jnp
from jax import lax
from jax.experimental import pallas as pl
from jax.experimental.pallas import tpu as pltpu
from jax.sharding import PartitionSpec as P

epsilon = 1e-06
tiny = 1e-30
f32 = jnp.float32
bf16 = jnp.bfloat16
VMEM_BYTES = 24 * 1024 * 1024
FIRST_VMEM_BYTES = 58 * 1024 * 1024


def vmem():
    return pl.BlockSpec(memory_space=pltpu.VMEM)


def smem():
    return pl.BlockSpec(memory_space=pltpu.SMEM)


def block_dot(pieces_k, slots, edge, cols, k, field, lanes):
    half = slots * edge
    top = jnp.concatenate([pieces_k[s * edge : (s + 1) * edge, :] for s in range(slots)], axis=1)
    low = jnp.concatenate(
        [pieces_k[half + s * edge : half + (s + 1) * edge, :] for s in range(slots)], axis=1
    )
    rows = [
        field[pl.ds(pl.multiple_of(cols[k, s] * edge, edge), edge), lanes] for s in range(slots)
    ]
    return jnp.dot(
        jnp.concatenate([top, low], axis=0),
        jnp.concatenate(rows, axis=0),
        preferred_element_type=f32,
    )


def merge_parts(one, two):
    num, den = one[0] + two[0], one[1] + two[1]
    apart = one[0] / jnp.maximum(one[1], tiny) - two[0] / jnp.maximum(two[1], tiny)
    weight = jnp.sqrt(one[1]) * jnp.sqrt(two[1]) * lax.rsqrt(jnp.maximum(den, tiny))
    gap = apart * weight
    return num, den, (one[2] + two[2]) + gap * gap


def own_stats(stiff_x, mass_x):
    num = jnp.sum(stiff_x * mass_x, axis=0, keepdims=True)
    den = jnp.sum(mass_x * mass_x, axis=0, keepdims=True)
    rest = stiff_x - (num / jnp.maximum(den, tiny)) * mass_x
    return num, den, jnp.sum(rest * rest, axis=0, keepdims=True)


def shift_and_scale(stats, total_rows):
    num, den, about = stats[0:1, :], stats[1:2, :], stats[2:3, :]
    shift = num / (den + epsilon)
    off = shift - num / jnp.maximum(den, tiny)
    scale = lax.rsqrt((about + off * off * den) / total_rows + epsilon)
    return shift, scale


def block_dot(pieces_k, slots, edge, cols, k, field, lanes):
    half = slots * edge
    top = jnp.concatenate([pieces_k[s * edge : (s + 1) * edge, :] for s in range(slots)], axis=1)
    low = jnp.concatenate(
        [pieces_k[half + s * edge : half + (s + 1) * edge, :] for s in range(slots)], axis=1
    )
    rows = [
        field[pl.ds(pl.multiple_of(cols[k, s] * edge, edge), edge), lanes] for s in range(slots)
    ]
    return jnp.dot(
        jnp.concatenate([top, low], axis=0),
        jnp.concatenate(rows, axis=0),
        preferred_element_type=f32,
    )


def column_stats(stiff_x, mass_x):
    num = jnp.sum(stiff_x * mass_x, axis=0, keepdims=True)
    den = jnp.sum(mass_x * mass_x, axis=0, keepdims=True)
    rest = stiff_x - (num / jnp.maximum(den, tiny)) * mass_x
    return num, den, jnp.sum(rest * rest, axis=0, keepdims=True)


def shift_and_scale(stats, total_rows):
    num, den, about = stats[0:1, :], stats[1:2, :], stats[2:3, :]
    shift = num / (den + epsilon)
    off = shift - num / jnp.maximum(den, tiny)
    scale = lax.rsqrt((about + off * off * den) / total_rows + epsilon)
    return shift, scale


def hbm():
    return pl.BlockSpec(memory_space=pltpu.HBM)


def turn_kernel(chunks, copies_each, cols_hbm, current_hbm, coeffs_hbm, out_ref, current, coeffs, cols, sems):
    depth = current.shape[1] // chunks
    piece = depth // copies_each
    copies = [pltpu.make_async_copy(current_hbm, current, sems.at[0])]
    for c in range(chunks * copies_each):
        part = pl.ds(c * piece, piece)
        copies.append(pltpu.make_async_copy(coeffs_hbm.at[0, part], coeffs.at[part], sems.at[c + 1]))
    copies.append(pltpu.make_async_copy(cols_hbm, cols, sems.at[chunks * copies_each + 1]))
    for copy in copies:
        copy.start()
    rows, edge = current.shape[0], out_ref.shape[1]
    copies[0].wait()
    turned = None
    for c in range(chunks):
        for d in range(copies_each):
            copies[c * copies_each + d + 1].wait()
        part = slice(c * depth, (c + 1) * depth)
        more = jnp.dot(current[:, part], coeffs[part, :], preferred_element_type=f32)
        turned = more if turned is None else turned + more
    copies[-1].wait()
    lane = lax.broadcasted_iota(jnp.int32, (16, edge), 1)
    tag = jnp.zeros((16, edge), jnp.int32)
    for s in range(cols.shape[1]):
        tag = jnp.where(lane == s, cols[0, s], tag)
    turned = turned.astype(bf16)
    blocks = turned.shape[1] // edge
    for b in range(blocks):
        out_ref[b * rows : (b + 1) * rows, :] = turned[:, b * edge : (b + 1) * edge]
    out_ref[blocks * rows : blocks * rows + 16, :] = tag.astype(f32).astype(bf16)


def turn_first(cols, current, coeffs, modes):
    rows, columns = current.shape
    chunks, copies_each = 3, 2
    in_hbm = pl.BlockSpec(memory_space=pltpu.HBM)
    return pl.pallas_call(
        functools.partial(turn_kernel, chunks, copies_each),
        out_shape=pltpu.VMEM((2 * modes + 16, rows), bf16),
        in_specs=[in_hbm, in_hbm, in_hbm],
        out_specs=vmem(),
        scratch_shapes=[
            pltpu.VMEM((rows, columns), bf16),
            pltpu.VMEM((columns, 2 * modes), bf16),
            pltpu.SMEM(cols.shape, jnp.int32),
            pltpu.SemaphoreType.DMA((chunks * copies_each + 2,)),
        ],
        compiler_params=pltpu.CompilerParams(vmem_limit_bytes=FIRST_VMEM_BYTES),
        cost_estimate=pl.CostEstimate(
            flops=4 * rows * columns * modes, bytes_accessed=4 * columns * modes, transcendentals=0
        ),
    )(cols, current, coeffs)


def rows_kernel(nz, slots, edge, modes, cols, *refs):
    t_refs, km_refs = refs[:nz], refs[nz : 2 * nz - 1]
    placed, stiff_ref, mass_ref, some_ref = refs[2 * nz - 1 :]
    z = lax.axis_index("blk")
    for k in range(nz):
        at = pl.ds(pl.multiple_of((z ^ k) * edge, edge), edge)
        for b in range(placed.shape[1] // edge):
            placed[at, b * edge : (b + 1) * edge] = t_refs[k][b * edge : (b + 1) * edge, :]
    for k in range(nz - 1):
        both = block_dot(km_refs[k], slots, edge, cols, k, placed, slice(0, modes))
        stiff_ref[k] = both[:edge]
        mass_ref[k] = both[edge:]
        for row, value in enumerate(own_stats(both[:edge], both[edge:])):
            some_ref[k, row : row + 1, :] = value


def stats_kernel(
    nz, slots, edge, modes, cols_ref, km_last, placed, some, stiff_ref, mass_ref, stats_ref, cols, sem
):
    fetch = pltpu.make_async_copy(cols_ref, cols, sem)
    fetch.start()
    parts = [tuple(some[k, r : r + 1, :] for r in range(3)) for k in range(nz - 1)]
    fetch.wait()
    both = block_dot(km_last, slots, edge, cols, nz - 1, placed, slice(0, modes))
    stiff_ref[...] = both[:edge]
    mass_ref[...] = both[edge:]
    parts.append(own_stats(both[:edge], both[edge:]))
    while len(parts) > 1:
        parts = [merge_parts(*parts[k : k + 2]) for k in range(0, len(parts), 2)]
    for row, value in enumerate(parts[0]):
        stats_ref[row : row + 1, :] = value


def early_turn_kernel(modes, placed, coeffs, out_ref):
    out_ref[...] = jnp.dot(
        placed[:, :modes], coeffs[1, :modes, :], preferred_element_type=f32
    ) + jnp.dot(placed[:, modes:], coeffs[1, 2 * modes :, :], preferred_element_type=f32)


def sweep_kernel(nz, slots, edge, modes, total_rows, cols_ref, *refs):
    *refs, cols, sem = refs
    fetch = pltpu.make_async_copy(cols_ref, cols, sem)
    fetch.start()
    km_refs = refs[:nz]
    early, stiff, mass, stiff_last, mass_last, stats, coeffs = refs[nz : nz + 7]
    turned_ref, stiff_ref, mass_ref, stats_ref, search = refs[nz + 7 :]
    z = lax.axis_index("blk")
    at = [pl.ds(pl.multiple_of((z ^ k) * edge, edge), edge) for k in range(nz)]
    shift, scale = shift_and_scale(stats, total_rows)
    for k in range(nz):
        stiff_x = stiff[k] if k < nz - 1 else stiff_last[...]
        mass_x = mass[k] if k < nz - 1 else mass_last[...]
        search[at[k], :] = ((stiff_x - shift * mass_x) * scale).astype(bf16)
    late = jnp.dot(search[...], coeffs[1, modes : 2 * modes, :], preferred_element_type=f32)
    turned_ref[...] = (early[...] + late).astype(bf16)
    fetch.wait()
    parts = []
    for k in range(nz):
        both = block_dot(km_refs[k], slots, edge, cols, k, turned_ref, slice(0, modes))
        stiff_ref[at[k], :] = both[:edge]
        mass_ref[at[k], :] = both[edge:]
        parts.append(own_stats(both[:edge], both[edge:]))
    while len(parts) > 1:
        parts = [merge_parts(*parts[k : k + 2]) for k in range(0, len(parts), 2)]
    for row, value in enumerate(parts[0]):
        stats_ref[row : row + 1, :] = value


def dense_order(width):
    whole = width // 128 * 128
    return [(0, 0, whole), (1, 0, whole), (0, whole, width), (1, whole, width)]


def gram_rows(full_t, applied, chips, core, bounds, out_refs):
    chip = lax.div(lax.axis_index("grp"), 2)
    block = full_t.shape[0] // (2 * chips)
    rows = [
        full_t[pl.ds(pl.multiple_of((2 * j + core) * block, 16), block), :] for j in range(chips)
    ]
    gram = jnp.dot(jnp.concatenate(rows, axis=0), applied[...], preferred_element_type=f32)
    whole = gram.shape[1] // 128
    for (low, high), out_ref in zip(bounds, out_refs):
        size = high - low
        for j in range(chips):
            mine = gram[j * block + low : j * block + high]
            for b in range(whole):
                part = mine[:, b * 128 : (b + 1) * 128].astype(bf16)
                out_ref[j ^ chip, b * size : (b + 1) * size, :] = part
            left = mine[:, whole * 128 :]
            left = jnp.concatenate([left[: size // 2], left[size // 2 :]], axis=1).astype(bf16)
            out_ref[j ^ chip, whole * size : whole * size + size // 2, :] = left


def finish_kernel(bounds, width, *refs):
    *refs, out_hbm, out_ref, sems = refs
    each = len(refs) // len(bounds)
    whole = width // 128
    writes = []
    for i, (low, high) in enumerate(bounds):
        size = high - low
        total = refs[i * each][...].astype(f32)
        for ref in refs[i * each + 1 : (i + 1) * each]:
            total = total + ref[...].astype(f32)
        left = total[2 * whole * size :, :]
        left = jnp.concatenate([left[:, :64], left[:, 64:]], axis=0)
        for op in range(2):
            for b in range(whole):
                at = (op * whole + b) * size
                out_ref[low:high, op, b * 128 : (b + 1) * 128] = total[at : at + size]
            out_ref[low:high, op, whole * 128 :] = left[:, op * 32 : (op + 1) * 32]
        part = pl.ds(low, size)
        writes.append(pltpu.make_async_copy(out_ref.at[part], out_hbm.at[part], sems.at[i]))
        writes[-1].start()
    for write in writes:
        write.wait()


def gram_kernel(nz, chips, slots, edge, modes, total_rows, bounds, cols_ref, *refs):
    *refs, cols, sem = refs
    fetch = pltpu.make_async_copy(cols_ref, cols, sem)
    fetch.start()
    km_refs = refs[:nz]
    turned, stiff, mass, stats = refs[nz : nz + 4]
    *gram_refs, full, full_t, applied, chosen = refs[nz + 4 :]
    z = lax.axis_index("blk")
    at = [pl.ds(pl.multiple_of((z ^ k) * edge, edge), edge) for k in range(nz)]
    width = 3 * modes // nz
    shift, scale = shift_and_scale(stats, total_rows)
    full[:, 0:modes] = turned[:, 0:modes]
    full[:, modes : 2 * modes] = ((stiff[...] - shift * mass[...]) * scale).astype(bf16)
    full[:, 2 * modes : 3 * modes] = turned[:, modes : 2 * modes]
    full_t[...] = full[...].T
    window = chosen.shape[1]
    start = z * width // 128 * 128
    picked = full[:, pl.ds(pl.multiple_of(start, 128), window)].astype(f32)
    chosen[...] = pltpu.roll(picked, window - (z * width - start), 1).astype(bf16)
    fetch.wait()
    for k in range(nz):
        both = block_dot(km_refs[k], slots, edge, cols, k, chosen, slice(0, width)).astype(bf16)
        column = 0
        for op, first, last in dense_order(width) if bounds else [(0, 0, width), (1, 0, width)]:
            part = both[op * edge : (op + 1) * edge, first:last]
            applied[at[k], column : column + last - first] = part
            column += last - first
    if bounds:
        other = 1 - lax.rem(lax.axis_index("grp"), 2)
        gram_rows(full_t, applied, chips, other, bounds, gram_refs)
    else:
        gram_refs[0][...] = jnp.dot(full_t[...], applied[...], preferred_element_type=f32).astype(bf16)


def results_kernel(edge, total_rows, stats, full, basis_ref, ritz_ref):
    z = lax.axis_index("blk")
    basis_ref[...] = full[pl.ds(pl.multiple_of(z * edge, edge), edge), :]
    ritz_ref[...] = shift_and_scale(stats, total_rows)[0]


def gram_rest_kernel(chips, bounds, full_t, applied, *gram_refs):
    own = lax.rem(lax.axis_index("grp"), 2)
    gram_rows(full_t, applied, chips, own, bounds, gram_refs)


def call(kernel, inputs, n_smem, out_shape, scratch, flops, n_any=0):
    return pl.pallas_call(
        kernel,
        out_shape=out_shape,
        in_specs=[smem()] * n_smem
        + [pl.BlockSpec(memory_space=pl.ANY)] * n_any
        + [vmem()] * (len(inputs) - n_smem - n_any),
        out_specs=jax.tree.map(lambda _: vmem(), out_shape),
        scratch_shapes=scratch,
        compiler_params=pltpu.CompilerParams(vmem_limit_bytes=VMEM_BYTES),
        cost_estimate=pl.CostEstimate(flops=flops, bytes_accessed=4_000_000, transcendentals=0),
    )(*inputs)


def by_xor(size, k):
    return [(i, i ^ k) for i in range(size)]


def merge(one, two):
    return jnp.stack(merge_parts(one, two))


def merge_over(axis, size, stats):
    step = 1
    if axis == "grp" and size >= 8:
        stats = merge(stats, lax.ppermute(stats, axis, by_xor(size, 1)))
        step = 2
        if size == 8:
            got = [lax.ppermute(stats, axis, by_xor(size, 2 * k)) for k in (1, 2, 3)]
            return merge(merge(stats, got[0]), merge(got[1], got[2]))
    while step < size:
        stats = merge(stats, lax.ppermute(stats, axis, by_xor(size, step)))
        step *= 2
    return stats


def hold_kernel(*refs):
    pass


def hold(arrays, until):
    anywhere = pl.BlockSpec(memory_space=pl.ANY)
    return pl.pallas_call(
        hold_kernel,
        out_shape=tuple(jax.ShapeDtypeStruct(a.shape, a.dtype) for a in arrays),
        in_specs=[anywhere] * (len(arrays) + len(until)),
        out_specs=(anywhere,) * len(arrays),
        input_output_aliases={i: i for i in range(len(arrays))},
        compiler_params=pltpu.CompilerParams(vmem_limit_bytes=1024 * 1024),
        cost_estimate=pl.CostEstimate(flops=0, bytes_accessed=0, transcendentals=0),
    )(*arrays, *until)


def gather(operators, turned, nz):
    def send(x, step):
        return lax.ppermute(x, "blk", by_xor(nz, step))

    if nz == 4:
        km_2, km_1 = send(operators, 2), send(operators, 1)
        t_2, t_1 = send(turned, 2), send(turned, 1)
        (km_2,) = hold((km_2,), (km_1,))
        km_3 = send(km_2, 1)
        (t_2,) = hold((t_2,), (t_1,))
        return [operators, km_1, km_2, km_3], [turned, t_1, t_2, send(t_2, 1)]
    parts, far = {0: (operators, turned)}, nz // 2
    while far:
        parts |= {k ^ far: tuple(send(x, far) for x in held) for k, held in parts.items()}
        far //= 2
    return [[parts[k][i] for k in range(nz)] for i in range(2)]


def body(basis, coeffs, stiff_blocks, mass_blocks, block_cols):
    nz, ng = lax.axis_size("blk"), lax.axis_size("grp")
    current = basis[0]
    edge, columns = current.shape
    slots = block_cols.shape[-1]
    modes = columns // 3
    rows = edge * nz
    total_rows = rows * ng
    width = columns // nz

    payload = jnp.concatenate(
        [
            stiff_blocks[0, 0].reshape(slots * edge, edge),
            mass_blocks[0, 0].reshape(slots * edge, edge),
        ],
        axis=0,
    )
    turned = turn_first(block_cols[0], current, coeffs, modes)
    km_parts, t_parts = gather(payload, turned, nz)

    cols = jnp.stack([p[2 * modes, :slots] for p in t_parts]).astype(jnp.int32)
    some = jax.ShapeDtypeStruct((nz - 1, edge, modes), f32)
    last = jax.ShapeDtypeStruct((edge, modes), f32)
    stats_shape = jax.ShapeDtypeStruct((3, modes), f32)
    work = 4 * edge * slots * edge * modes
    placed, stiff_some, mass_some, stats_some = call(
        functools.partial(rows_kernel, nz, slots, edge, modes),
        [cols, *t_parts, *km_parts[:-1]],
        1,
        (
            jax.ShapeDtypeStruct((rows, 2 * modes), bf16),
            some,
            some,
            jax.ShapeDtypeStruct((nz - 1, 8, modes), f32),
        ),
        [],
        (nz - 1) * work,
    )
    fetched = [pltpu.SMEM((nz, slots), jnp.int32), pltpu.SemaphoreType.DMA(())]
    stiff_last, mass_last, stats = call(
        functools.partial(stats_kernel, nz, slots, edge, modes),
        [cols, km_parts[-1], placed, stats_some],
        0,
        (last, last, stats_shape),
        fetched,
        work,
        n_any=1,
    )
    stats = merge_over("grp", ng, stats)
    early = call(
        functools.partial(early_turn_kernel, modes),
        [placed, coeffs],
        0,
        jax.ShapeDtypeStruct((rows, 2 * modes), f32),
        [],
        8 * rows * modes * modes,
    )
    turned, stiff_x, mass_x, stats = call(
        functools.partial(sweep_kernel, nz, slots, edge, modes, total_rows),
        [cols, *km_parts, early, stiff_some, mass_some, stiff_last, mass_last, stats, coeffs],
        0,
        (
            jax.ShapeDtypeStruct((rows, 2 * modes), bf16),
            jax.ShapeDtypeStruct((rows, modes), f32),
            jax.ShapeDtypeStruct((rows, modes), f32),
            stats_shape,
        ),
        [pltpu.VMEM((rows, modes), bf16), *fetched],
        4 * rows * modes * modes + nz * work,
        n_any=1,
    )
    stats = merge_over("grp", ng, stats)

    chips = ng // 2
    block = columns // ng
    bounds = []
    if block % 32 == 16 and width % 128 == 32:
        first_rows = (block + 16) // 32 * 16
        bounds = [(0, first_rows), (first_rows, block)]
    gram_shapes = tuple(
        jax.ShapeDtypeStruct((chips, (high - low) * 2 * width // 128, 128), bf16)
        for low, high in bounds
    ) or (jax.ShapeDtypeStruct((columns, 2 * width), bf16),)
    window = -(-(width + max(i * width % 128 for i in range(nz))) // 128) * 128
    *grams, full, full_t, applied = call(
        functools.partial(gram_kernel, nz, chips, slots, edge, modes, total_rows, bounds),
        [cols, *km_parts, turned, stiff_x, mass_x, stats],
        0,
        (
            *gram_shapes,
            jax.ShapeDtypeStruct((rows, columns), bf16),
            jax.ShapeDtypeStruct((columns, rows), bf16),
            jax.ShapeDtypeStruct((rows, 2 * width), bf16),
        ),
        [pltpu.VMEM((rows, window), bf16), *fetched],
        2 * rows * columns * width,
        n_any=1,
    )
    basis_out, ritz = call(
        functools.partial(results_kernel, edge, total_rows),
        [stats, full],
        0,
        (jax.ShapeDtypeStruct((edge, columns), bf16), jax.ShapeDtypeStruct((1, modes), f32)),
        [],
        0,
    )
    if bounds:
        got = [lax.ppermute(x, "grp", by_xor(ng, 1)) for x in grams]
        keep = call(
            functools.partial(gram_rest_kernel, chips, bounds),
            [full_t, applied],
            0,
            gram_shapes,
            [],
            2 * rows * columns * width,
        )
        pieces = []
        for one, two in zip(keep, got):
            mine = (one.astype(f32) + two.astype(f32)).astype(bf16)
            pieces += [mine[0]] + [
                lax.ppermute(mine[k], "grp", by_xor(ng, 2 * k)) for k in range(1, chips)
            ]
        total = pl.pallas_call(
            functools.partial(finish_kernel, bounds, width),
            out_shape=jax.ShapeDtypeStruct((block, 2, width), f32),
            in_specs=[vmem()] * len(pieces),
            out_specs=pl.BlockSpec(memory_space=pl.ANY),
            scratch_shapes=[
                pltpu.VMEM((block, 2, width), f32),
                pltpu.SemaphoreType.DMA((len(bounds),)),
            ],
            compiler_params=pltpu.CompilerParams(vmem_limit_bytes=VMEM_BYTES),
        )(*pieces)
    else:
        total = lax.psum_scatter(grams[0], "grp", scatter_dimension=0, tiled=True)
        total = total.astype(f32).reshape(block, 2, width)
    return (basis_out[None], ritz[0], total)


def solution(mesh):
    in_specs = (
        P("grp", "blk", None),
        P(),
        P("grp", "blk", None, None, None),
        P("grp", "blk", None, None, None),
        P("grp", "blk", None),
    )
    out_specs = (P("grp", "blk", None), P(), P("grp", None, "blk"))
    return jax.shard_map(body, mesh=mesh, in_specs=in_specs, out_specs=out_specs, check_vma=False)
```
